256 devices in a mesh: py: 8 (over z_lo, core), px: 32 (over y, z_hi, x).
Axes of the slice: x: 4, y: 4, z: 8 (z_hi: 2, z_lo: 4; z = z_hi * 4 + z_lo), core: 2. Of those that a mesh axis runs over, the one named last changes fastest.
Arguments:
- measured: float32 [2, 2, 8, 32, 12544], P(None, None, 'py', 'px'), may hold values from -250 to 250
- psf_taps: bfloat16 [8, 32, 32, 32, 32], P('py', 'px'), may hold values from 0 to 0.011047363
- offsets: int32 [8, 32, 2], P('py', 'px'), may hold values from 0 to 7
- window_mask: int32 [1024, 4096], P('py', 'px'), may hold values 0 or 1
Outputs:
- object_basis: float32 [2, 2, 8, 32, 12544], P(None, None, 'py', 'px')
- image_basis: float32 [2, 2, 8, 32, 12544], P(None, None, 'py', 'px')
- factors: float32 [3, 2, 2], replicated
The draws below stay inside these ranges and needn't reach their ends.
All inputs are finite; a program needn't handle non-finite values. No bound on the sum of `window_mask` on one device may be relied on, other than what follows from the above.
Results may differ from the reference program's by a relative error of at most 0.014.
Values may be sent and summed in bfloat16 or wider, within the bound.
A program may use at most 128 MiB of HBM per device.

```python
import math
import jax
import jax.numpy as jnp
from jax import lax

PLANES = 2
PATCH = 128
KERNEL = 32
DEPTH_LEN = 64
HALF = 8
CORE = 112
HEIGHT = 896
WIDTH = 3584
N_PY = 8
N_PX = 32


def draw_measured(key, part):
    first_key = jax.random.fold_in(key, 11)
    rows_pos = jnp.arange(HEIGHT, dtype=jnp.float32)[:, None] / HEIGHT
    cols_pos = jnp.arange(WIDTH, dtype=jnp.float32)[None, :] / WIDTH
    column_scale = jnp.array([1.0, 3.0], jnp.float32)[:, None, None, None]
    spread = 10.0 ** (0.5 * (rows_pos + cols_pos))
    stacked = jax.random.truncated_normal(first_key, -4.0, 4.0, (2, PLANES, HEIGHT, WIDTH), jnp.float32)
    field = (stacked * spread * column_scale).astype(jnp.float32)
    blocks = field.reshape(2, PLANES, N_PY, CORE, N_PX, CORE)
    return blocks.transpose(0, 1, 2, 4, 3, 5).reshape(2, PLANES, N_PY, N_PX, CORE * CORE)


def plant(drawn, key, least, top_value):
    longest = drawn.shape.index(max(drawn.shape))
    spots = []
    for shift in (0, 1):
        where = [jax.random.randint(jax.random.fold_in(key, axis), (), 0, length) for axis, length in enumerate(drawn.shape)]
        where[longest] = (where[longest] + shift) % drawn.shape[longest]
        spots.append(tuple(where))
    return drawn.at[spots[0]].set(least).at[spots[1]].set(top_value)


def block_levels(key, extent, shards, least, high):
    def one(position, shards_of):
        draws = jax.random.uniform(jax.random.fold_in(jax.random.fold_in(key, 6), position), (shards_of,), jnp.float32, least / len(shards), high / len(shards))
        return jnp.repeat(jnp.exp(draws), extent[position] // shards_of).reshape((-1,) + (1,) * (len(extent) - position - 1))

    level = one(*shards[0])
    for cut in shards[1:]:
        level = level * one(*cut)
    return level


def setup_inputs(seed: int = 0) -> dict:
    key_of = jax.random.split(jax.random.key(seed), 5)
    return {
        "measured": draw_measured(jax.random.fold_in(key_of[4], 71), 0),
        "psf_taps": jnp.clip(0.011047363 * jax.random.uniform(key_of[1], (N_PY, N_PX, KERNEL, KERNEL, KERNEL), jnp.float32) ** block_levels(key_of[1], (N_PY, N_PX, KERNEL, KERNEL, KERNEL), ((0, 8), (1, 32)), -0.2, 0.2), 0.0, 0.011047363).astype(jnp.bfloat16),
        "offsets": plant(jax.random.randint(key_of[2], (N_PY, N_PX, 2), 0, 8), jax.random.fold_in(key_of[2], 1), 0, 7).astype(jnp.int32),
        "window_mask": plant((jax.random.randint(key_of[3], (N_PY * PATCH, N_PX * PATCH), 0, 8) < 7).astype(jnp.int32), jax.random.fold_in(key_of[3], 1), 0, 1),
    }


epsilon = 1e-06

def to_grid(stored):
    blocks = stored.reshape(2, PLANES, N_PY, N_PX, CORE, CORE)
    return blocks.transpose(0, 1, 2, 4, 3, 5).reshape(2, PLANES, HEIGHT, WIDTH)

def to_tiles(field):
    blocks = field.reshape(2, PLANES, N_PY, CORE, N_PX, CORE)
    return blocks.transpose(0, 1, 2, 4, 3, 5).reshape(2, PLANES, N_PY, N_PX, CORE * CORE)

def twiddle(rows, cols, length, shift):
    row_ids = jnp.arange(rows, dtype=jnp.int32)[:, None]
    col_ids = jnp.arange(cols, dtype=jnp.int32)[None, :] + jnp.asarray(shift).astype(jnp.int32)
    phase = row_ids * col_ids % length
    angle = phase.astype(jnp.float32) * jnp.float32(2.0 * math.pi / length)
    return (jnp.cos(angle).astype(jnp.bfloat16), (-jnp.sin(angle)).astype(jnp.bfloat16))

def product(form, table, values):
    return jnp.einsum(form, table.astype(jnp.float32), values.astype(jnp.float32))

def complex_axis(form, cos_table, sin_table, real_in, imag_in):
    real_out = product(form, cos_table, real_in) - product(form, sin_table, imag_in)
    imag_out = product(form, cos_table, imag_in) + product(form, sin_table, real_in)
    return (real_out.astype(jnp.bfloat16), imag_out.astype(jnp.bfloat16))

def spectrum(patch_taps, shift_rows, shift_cols):
    half_kernel = KERNEL // 2
    cos_x, sin_x = twiddle(PATCH, KERNEL, PATCH, shift_cols - half_kernel)
    real_x = product('fi,tji->tjf', cos_x, patch_taps).astype(jnp.bfloat16)
    imag_x = product('fi,tji->tjf', sin_x, patch_taps).astype(jnp.bfloat16)
    cos_y, sin_y = twiddle(PATCH, KERNEL, PATCH, shift_rows - half_kernel)
    real_y, imag_y = complex_axis('gj,tjf->tgf', cos_y, sin_y, real_x, imag_x)
    cos_z, sin_z = twiddle(DEPTH_LEN, KERNEL, DEPTH_LEN, -half_kernel)
    return complex_axis('qt,tgf->qgf', cos_z, sin_z, real_y, imag_y)

def blur(patch_cells, spec_real, spec_imag, adjoint):
    values = patch_cells.astype(jnp.bfloat16)
    cos_p, sin_p = twiddle(PATCH, PATCH, PATCH, 0)
    real_x = product('fx,bzyx->bzyf', cos_p, values).astype(jnp.bfloat16)
    imag_x = product('fx,bzyx->bzyf', sin_p, values).astype(jnp.bfloat16)
    real_y, imag_y = complex_axis('gy,bzyf->bzgf', cos_p, sin_p, real_x, imag_x)
    cos_z, sin_z = twiddle(DEPTH_LEN, PLANES, DEPTH_LEN, 0)
    depth_re, depth_im = complex_axis('qz,bzgf->bqgf', cos_z, sin_z, real_y, imag_y)
    kernel_re = spec_real.astype(jnp.float32)
    kernel_im = spec_imag.astype(jnp.float32)
    if adjoint:
        kernel_im = -kernel_im
    depth_re = depth_re.astype(jnp.float32)
    depth_im = depth_im.astype(jnp.float32)
    prod_re = (depth_re * kernel_re - depth_im * kernel_im).astype(jnp.bfloat16)
    prod_im = (depth_re * kernel_im + depth_im * kernel_re).astype(jnp.bfloat16)
    back_cos, back_sin = twiddle(PLANES, DEPTH_LEN, DEPTH_LEN, 0)
    plane_re, plane_im = complex_axis('zq,bqgf->bzgf', back_cos, -back_sin, prod_re, prod_im)
    row_re, row_im = complex_axis('yg,bzgf->bzyf', cos_p, -sin_p, plane_re, plane_im)
    spatial = product('xf,bzyf->bzyx', cos_p, row_re) + product('xf,bzyf->bzyx', sin_p, row_im)
    return spatial * jnp.float32(1.0 / (DEPTH_LEN * PATCH * PATCH))

def window(mask_block):
    return mask_block.astype(jnp.float32)

def apply_all(field, psf_taps, offsets, window_mask, adjoint):
    padded = jnp.pad(field, ((0, 0), (0, 0), (HALF, HALF), (HALF, HALF)))

    def add_patch(patch_id, summed):
        patch_row = (patch_id // N_PX).astype(jnp.int32)
        patch_col = (patch_id % N_PX).astype(jnp.int32)
        nought = jnp.zeros((), jnp.int32)
        corner = (nought, nought, patch_row * CORE, patch_col * CORE)
        patch_cells = lax.dynamic_slice(padded, corner, (2, PLANES, PATCH, PATCH))
        mask_block = lax.dynamic_slice(window_mask, (patch_row * PATCH, patch_col * PATCH), (PATCH, PATCH))
        weight = window(mask_block)
        patch_taps = psf_taps[patch_row, patch_col]
        shifts = offsets[patch_row, patch_col]
        spec_real, spec_imag = spectrum(patch_taps, shifts[0], shifts[1])
        if adjoint:
            result = blur(patch_cells, spec_real, spec_imag, True) * weight
        else:
            result = blur(patch_cells * weight, spec_real, spec_imag, False)
        previous = lax.dynamic_slice(summed, corner, (2, PLANES, PATCH, PATCH))
        return lax.dynamic_update_slice(summed, previous + result, corner)
    summed = lax.fori_loop(0, N_PY * N_PX, add_patch, jnp.zeros_like(padded))
    return summed[:, :, HALF:HALF + HEIGHT, HALF:HALF + WIDTH]

def factor(pair, count):
    g_first = jnp.sum(pair[0] * pair[0]) / count
    g_cross = jnp.sum(pair[0] * pair[1]) / count
    g_second = jnp.sum(pair[1] * pair[1]) / count
    r_first = jnp.sqrt(g_first + epsilon)
    r_cross = g_cross / r_first
    r_second = jnp.sqrt(g_second - r_cross * r_cross + epsilon)
    return (r_first, r_cross, r_second)

def solve_right(pair, triple):
    leading = pair[0] / triple[0]
    trailing = (pair[1] - triple[1] * leading) / triple[2]
    return jnp.stack([leading, trailing])

def packed(triple):
    return jnp.stack([jnp.stack([triple[0], triple[1]]), jnp.stack([jnp.zeros_like(triple[0]), triple[2]])])

def reference(measured, psf_taps, offsets, window_mask):
    count = jnp.float32(PLANES * HEIGHT * WIDTH)
    measured_grid = to_grid(measured)
    start_factor = factor(measured_grid, count)
    left_basis = solve_right(measured_grid, start_factor)
    adjoint_field = apply_all(left_basis, psf_taps, offsets, window_mask, True)
    alpha_factor = factor(adjoint_field, count)
    object_basis = solve_right(adjoint_field, alpha_factor)
    forward_field = apply_all(object_basis, psf_taps, offsets, window_mask, False)
    residue = jnp.stack([forward_field[0] - alpha_factor[0] * left_basis[0] - alpha_factor[1] * left_basis[1], forward_field[1] - alpha_factor[2] * left_basis[1]])
    beta_factor = factor(residue, count)
    image_basis = solve_right(residue, beta_factor)
    factors = jnp.stack([packed(start_factor), packed(alpha_factor), packed(beta_factor)])
    return (to_tiles(object_basis), to_tiles(image_basis), factors)
```

```python
import functools
import math

import jax
import jax.numpy as jnp
import numpy as np
from jax import lax
from jax.experimental import pallas as pl
from jax.experimental.pallas import tpu as pltpu
from jax.sharding import PartitionSpec as P

PLANES = 2
PATCH = 128
KERNEL = 32
HALF = 8
CORE = 112
FLAT = 2 * PLANES * CORE * CORE // 128
TAP = KERNEL // 2 - 1
EPSILON = 1e-06
F32 = jnp.float32
BF16 = jnp.bfloat16


def tables():
    ids = np.arange(PATCH)
    angle = 2 * np.pi * (np.outer(ids, ids) % PATCH) / PATCH
    cos, sin = np.cos(angle), -np.sin(angle)
    forward = np.block([[cos, sin], [-sin, cos]])
    places = np.arange(64) - KERNEL // 2
    angle = 2 * np.pi * (np.outer(places, ids) % PATCH) / PATCH
    cos, sin = np.cos(angle), -np.sin(angle)
    taps_x = np.concatenate([cos, sin], axis=1)
    taps_y = np.block([[cos.T, -sin.T], [sin.T, cos.T]])
    return [jnp.asarray(t, BF16) for t in (forward, forward.T, taps_x, taps_y)]


def mm(left, right):
    return jnp.dot(left, right, preferred_element_type=F32)


def roll(values, shift):
    shift = shift % 128
    return values if shift == 0 else pltpu.roll(values, shift, 1)


def total(values):
    return jnp.sum(jnp.sum(values, axis=0, keepdims=True), axis=1, keepdims=True)


class Exchange:
    def __init__(self, index, ny, nx, height, rows, cols, planes, packed, turned, row_in, col_in, corner_in, send, recv):
        self.index, self.height = index, height
        self.planes, self.packed, self.turned = planes, packed, turned
        self.row_in, self.col_in, self.corner_in = row_in, col_in, corner_in
        py, px = lax.axis_index("py"), lax.axis_index("px")
        up, down = lax.rem(py + ny - 1, ny), lax.rem(py + 1, ny)
        left, right = lax.rem(px + nx - 1, nx), lax.rem(px + 1, nx)
        top, bottom = pl.ds(rows[0], height), pl.ds(rows[1], height)
        (left_from, left_to), (right_from, right_to) = cols
        plan = [
            (planes.at[:, top, :], row_in.at[1], up, px),
            (planes.at[:, bottom, :], row_in.at[0], down, px),
            (turned.at[:, pl.ds(left_from, height), :], col_in.at[:, pl.ds(left_to, height), :], py, left),
            (turned.at[:, pl.ds(right_from, height), :], col_in.at[:, pl.ds(right_to, height), :], py, right),
            (packed.at[top, :], corner_in.at[3], up, left),
            (packed.at[top, :], corner_in.at[2], up, right),
            (packed.at[bottom, :], corner_in.at[1], down, left),
            (packed.at[bottom, :], corner_in.at[0], down, right),
        ]
        self.copies = [
            pltpu.make_async_remote_copy(
                src_ref=source,
                dst_ref=target,
                send_sem=send.at[index, i],
                recv_sem=recv.at[index, i],
                device_id={"py": to_y, "px": to_x},
                device_id_type=pl.DeviceIdType.MESH,
            )
            for i, (source, target, to_y, to_x) in enumerate(plan)
        ]

    def start(self):
        lane = lax.broadcasted_iota(jnp.int32, (PATCH, 128), 1)
        for copy in self.copies[:2]:
            copy.start()
        packed = roll(self.planes[0], 16)
        for m in range(1, 2 * PLANES):
            packed = jnp.where(lane >= 32 * m, roll(self.planes[m], 16 + 32 * m), packed)
        self.packed[...] = packed
        self.turned[...] = packed.T.reshape(2 * PLANES, 32, PATCH)
        for copy in self.copies[2:]:
            copy.start()

    def wait_recv(self):
        for copy in self.copies:
            copy.wait_recv()

    def wait_send(self):
        for copy in self.copies:
            copy.wait_send()

    def sides(self):
        columns = self.col_in[...].reshape(4 * 32, PATCH).T
        lane = lax.broadcasted_iota(jnp.int32, (self.height, 128), 1)
        is_left = lax.rem(lane, 32) >= 16
        upper = jnp.where(is_left, roll(self.corner_in[0], 16), roll(self.corner_in[1], -16))
        lower = jnp.where(is_left, roll(self.corner_in[2], 16), roll(self.corner_in[3], -16))
        return columns, upper, lower


def normalised(cells):
    s00 = sum(total(cells[0][z] * cells[0][z]) for z in range(PLANES))
    s01 = sum(total(cells[0][z] * cells[1][z]) for z in range(PLANES))
    s11 = sum(total(cells[1][z] * cells[1][z]) for z in range(PLANES))
    tiny = F32(1e-30)
    q0 = lax.rsqrt(jnp.maximum(s00, tiny))
    cross = s01 * q0
    q1 = lax.rsqrt(jnp.maximum(s11 - cross * cross, s11 * F32(1e-6) + tiny))
    first = [cells[0][z] * q0 for z in range(PLANES)]
    second = [(cells[1][z] - cross * first[z]) * q1 for z in range(PLANES)]
    return (first, second), (1.0 / q0, cross, 1.0 / q1)


def blur(cells, spectrum, forward_ref, backward_ref, adjoint):
    half = PATCH
    table, turned = forward_ref[...], backward_ref[...]
    values = jnp.concatenate(
        [jnp.concatenate([cells[k][z].astype(BF16) for k in range(2)], axis=1) for z in range(PLANES)], axis=0
    )
    along_x = mm(values, table).astype(BF16)
    swapped = jnp.concatenate(
        [
            jnp.concatenate([along_x[z * half : (z + 1) * half, c * half : (c + 1) * half] for z in range(PLANES)], axis=1)
            for c in range(2)
        ],
        axis=0,
    )
    along_y = mm(turned, swapped)
    re = [along_y[:half, z * half : (z + 1) * half] for z in range(PLANES)]
    im = [along_y[half:, z * half : (z + 1) * half] for z in range(PLANES)]
    tap_re = [spectrum[:half, t * half : (t + 1) * half] for t in range(3)]
    tap_im = [spectrum[half:, t * half : (t + 1) * half] for t in range(3)]
    sign = -1.0 if adjoint else 1.0
    out_re, out_im = [], []
    for z_out in range(PLANES):
        sum_re = sum_im = None
        for z_in in range(PLANES):
            depth = 1 + (z_in - z_out) if adjoint else 1 - (z_in - z_out)
            a, b = tap_re[depth], sign * tap_im[depth]
            part_re = re[z_in] * a - im[z_in] * b
            part_im = re[z_in] * b + im[z_in] * a
            sum_re = part_re if sum_re is None else sum_re + part_re
            sum_im = part_im if sum_im is None else sum_im + part_im
        out_re.append(sum_re.astype(BF16))
        out_im.append(sum_im.astype(BF16))
    product = jnp.concatenate([jnp.concatenate(out_re, axis=1), jnp.concatenate(out_im, axis=1)], axis=0)
    back_y = mm(table, product).astype(BF16)
    swapped = jnp.concatenate(
        [
            jnp.concatenate([back_y[c * half : (c + 1) * half, z * half : (z + 1) * half] for c in range(2)], axis=1)
            for z in range(PLANES)
        ],
        axis=0,
    )
    back_x = mm(swapped, turned)
    return [[back_x[z * half : (z + 1) * half, k * half : (k + 1) * half] for z in range(PLANES)] for k in range(2)]


def restored(cells, factor):
    first = [factor[0] * cells[0][z] for z in range(PLANES)]
    second = [factor[2] * cells[1][z] + factor[1] * cells[0][z] for z in range(PLANES)]
    return first, second


def factor_of(g00, g01, g11):
    r00 = jnp.sqrt(jnp.maximum(g00, 0.0) + EPSILON)
    r01 = g01 / r00
    r11 = jnp.sqrt(jnp.maximum(g11 - r01 * r01, 0.0) + EPSILON)
    return r00, r01, r11


def kernel(
    ny, nx,
    measured_hbm, taps_hbm, offsets, mask_hbm, forward_hbm, backward_hbm, taps_x_hbm, taps_y_hbm,
    object_hbm, image_hbm, factors_ref,
    measured, taps, mask, forward_ref, backward_ref, taps_x, taps_y,
    spectrum_ref, planes, packed, turned, row8, col_in, corner8, row16, corner16,
    object_flat, forward_flat, image_flat, grid_ref,
    one_out, one_in, two_out, two_in,
    load_sem, store_sem, send_sem, recv_sem, sum_send, sum_recv,
):
    py, px = lax.axis_index("py"), lax.axis_index("px")
    loads = [
        pltpu.make_async_copy(source, target, load_sem.at[i])
        for i, (source, target) in enumerate(
            [
                (measured_hbm, measured),
                (taps_hbm.at[0, 0, pl.ds(TAP, 3)], taps),
                (taps_x_hbm, taps_x),
                (taps_y_hbm, taps_y),
                (mask_hbm, mask),
                (forward_hbm, forward_ref),
                (backward_hbm, backward_ref),
            ]
        )
    ]
    for load in loads:
        load.start()

    row, high, column = px // 8, lax.rem(px // 4, 2), lax.rem(px, 4)
    place_one, place_two = high * ny + py, row * 4 + column

    def partner_one(step):
        at = lax.rem(place_one + step, 16)
        return {"py": lax.rem(at, ny), "px": row * 8 + (at // ny) * 4 + column}

    def partner_two(step):
        at = lax.rem(place_two + step, 16)
        return {"py": py, "px": (at // 4) * 8 + high * 4 + lax.rem(at, 4)}

    exchange = functools.partial(Exchange, ny=ny, nx=nx, send=send_sem, recv=recv_sem)
    first = exchange(
        index=0, height=8, rows=(8, 112), cols=((24, 8), (0, 16)), planes=planes.at[0], packed=packed.at[0],
        turned=turned.at[0], row_in=row8.at[0], col_in=col_in.at[0], corner_in=corner8.at[0],
    )
    second = exchange(
        index=1, height=16, rows=(0, 112), cols=((16, 0), (0, 16)), planes=planes.at[1], packed=packed.at[1],
        turned=turned.at[1], row_in=row16, col_in=col_in.at[1], corner_in=corner16,
    )
    third = exchange(
        index=2, height=8, rows=(0, 120), cols=((16, 0), (8, 24)), planes=planes.at[2], packed=packed.at[2],
        turned=turned.at[2], row_in=row8.at[1], col_in=col_in.at[2], corner_in=corner8.at[1],
    )
    barrier = pltpu.get_barrier_semaphore()
    greeted = 0
    for dy in (ny - 1, 0, 1):
        for dx in (nx - 1, 0, 1):
            if dy or dx:
                to = {"py": lax.rem(py + dy, ny), "px": lax.rem(px + dx, nx)}
                pl.semaphore_signal(barrier, inc=1, device_id=to, device_id_type=pl.DeviceIdType.MESH)
                greeted += 1
    for step in range(1, 16):
        for to in (partner_one(step), partner_two(step)):
            pl.semaphore_signal(barrier, inc=1, device_id=to, device_id_type=pl.DeviceIdType.MESH)
            greeted += 1

    lane = lax.broadcasted_iota(jnp.int32, (PATCH, 128), 1)
    line = lax.broadcasted_iota(jnp.int32, (PATCH, 128), 0)
    owned_lane = (lane >= HALF) & (lane < PATCH - HALF)
    has_up, has_down, has_left, has_right = py > 0, py < ny - 1, px > 0, px < nx - 1
    low_y, high_y = jnp.where(has_up, 0, HALF), jnp.where(has_down, PATCH, PATCH - HALF)
    low_x, high_x = jnp.where(has_left, 0, HALF), jnp.where(has_right, PATCH, PATCH - HALF)
    inside = (line >= low_y) & (line < high_y) & (lane >= low_x) & (lane < high_x)

    loads[0].wait()
    lane14 = lax.broadcasted_iota(jnp.int32, (14, 128), 1)
    for m in range(4):
        planes[0, m, 0:HALF, :] = jnp.zeros((HALF, 128), F32)
        planes[0, m, PATCH - HALF : PATCH, :] = jnp.zeros((HALF, 128), F32)
        for k in range(8):
            if k < 7:
                high_part = measured[pl.ds(98 * m + k, 14, stride=7), :]
            if k == 0:
                both = high_part
            elif k == 7:
                both = measured[pl.ds(98 * m + 6, 14, stride=7), :]
            else:
                low_part = measured[pl.ds(98 * m + k - 1, 14, stride=7), :]
                both = jnp.where(lane14 >= 128 - 16 * k, low_part, high_part)
            planes[0, m, pl.ds(HALF + k, 14, stride=8), :] = roll(both, 16 * k + HALF)

    pl.semaphore_wait(barrier, greeted)
    first.start()

    for load in loads[1:4]:
        load.wait()
    shift_y, shift_x = offsets[0, 0, 0], offsets[0, 0, 1]
    pick_x = (
        lax.broadcasted_iota(jnp.int32, (KERNEL, 64), 1) == lax.broadcasted_iota(jnp.int32, (KERNEL, 64), 0) + shift_x
    )
    pick_y = (
        lax.broadcasted_iota(jnp.int32, (64, KERNEL), 0) == lax.broadcasted_iota(jnp.int32, (64, KERNEL), 1) + shift_y
    )
    pick_x = jnp.where(pick_x, 1.0, 0.0).astype(BF16)
    pick_y = jnp.where(pick_y, 1.0, 0.0).astype(BF16)
    placed = mm(taps[...].reshape(3 * KERNEL, KERNEL), pick_x).astype(BF16)
    kx = mm(placed, taps_x[...]).astype(BF16)
    side_by_side = jnp.concatenate([kx[t * KERNEL : (t + 1) * KERNEL] for t in range(3)], axis=1)
    kx = mm(pick_y, side_by_side).astype(BF16)
    kx = jnp.concatenate(
        [
            jnp.concatenate([kx[:, t * 256 + c * 128 : t * 256 + (c + 1) * 128] for t in range(3)], axis=1)
            for c in range(2)
        ],
        axis=0,
    )
    spectrum_ref[...] = mm(taps_y[...], kx) * F32(1.0 / (PATCH * PATCH))

    for load in loads[4:]:
        load.wait()
    weight = mask[...].astype(F32)

    def tile(left, right):
        return jnp.sum((left * right).reshape(-1, 8, 128), axis=0)

    owned = slice(HALF, PATCH - HALF)
    owned_core = owned_lane[owned]
    own_m = [[jnp.where(owned_core, planes[0, 2 * k + z, owned, :], 0.0) for z in range(PLANES)] for k in range(2)]

    def grams(left, right, pairs):
        return [sum(tile(left[i][z], right[j][z]) for z in range(PLANES)) for i, j in pairs]

    sums = grams(own_m, own_m, ((0, 0), (0, 1), (1, 1)))

    first.wait_recv()
    columns, upper, lower = first.sides()
    columns = jnp.concatenate([upper, columns[owned], lower], axis=0)
    window = [[None, None], [None, None]]
    for m in range(4):
        centre = jnp.concatenate([row8[0, 0, m], planes[0, m, owned, :], row8[0, 1, m]], axis=0)
        cells = jnp.where(owned_lane, centre, roll(columns, -16 - 32 * m))
        window[m // 2][m % 2] = jnp.where(inside, cells, 0.0)
    unit, factor = normalised(window)
    result = restored(blur(unit, spectrum_ref[...], forward_ref, backward_ref, True), factor)
    for m in range(4):
        planes[1, m] = result[m // 2][m % 2] * weight
    second.start()
    first.wait_send()

    second.wait_recv()
    columns, upper, lower = second.sides()
    upper, lower = jnp.where(has_up, upper, 0.0), jnp.where(has_down, lower, 0.0)
    columns = jnp.concatenate([columns[:16] + upper, columns[16:112], columns[112:] + lower], axis=0)
    edge_lane = ((lane < 16) & has_left) | ((lane >= 112) & has_right)
    second.wait_send()
    window = [[None, None], [None, None]]
    own_v = [[None, None], [None, None]]
    keep = jnp.where(inside, weight, 0.0)
    for m in range(4):
        cells = planes[1, m]
        up_rows = jnp.where(has_up, row16[0, m], 0.0)
        down_rows = jnp.where(has_down, row16[1, m], 0.0)
        cells = jnp.concatenate([cells[:16] + up_rows, cells[16:112], cells[112:] + down_rows], axis=0)
        cells = cells + jnp.where(edge_lane, roll(columns, -16 - 32 * m), 0.0)
        planes[1, m] = cells
        own_v[m // 2][m % 2] = jnp.where(owned_core, cells[owned], 0.0)
        window[m // 2][m % 2] = cells * keep
    sums += grams(own_v, own_v, ((0, 0), (0, 1), (1, 1)))
    unit, factor = normalised(window)
    result = restored(blur(unit, spectrum_ref[...], forward_ref, backward_ref, False), factor)
    for m in range(4):
        planes[2, m] = result[m // 2][m % 2]
    third.start()

    def to_flat(source, target):
        for m in range(4):
            for j in range(7):
                head = roll(source(m, pl.ds(HALF + j, 14, stride=8)), -16 * j - HALF)
                tail = roll(source(m, pl.ds(HALF + j + 1, 14, stride=8)), 104 - 16 * j)
                target[pl.ds(98 * m + j, 14, stride=7), :] = jnp.where(lane14 < 112 - 16 * j, head, tail)

    to_flat(lambda m, rows: planes[1, m, rows, :], object_flat)

    third.wait_recv()
    columns, upper, lower = third.sides()
    upper, lower = jnp.where(has_up, upper, 0.0), jnp.where(has_down, lower, 0.0)
    columns = jnp.concatenate([columns[:8], columns[8:16] + upper, columns[16:112], columns[112:120] + lower, columns[120:]], axis=0)
    third.wait_send()
    edge_lane = ((lane >= 8) & (lane < 16) & has_left) | ((lane >= 112) & (lane < 120) & has_right)
    own_f = [[None, None], [None, None]]
    for m in range(4):
        cells = planes[2, m]
        up_rows = jnp.where(has_up, row8[1, 0, m], 0.0)
        down_rows = jnp.where(has_down, row8[1, 1, m], 0.0)
        cells = jnp.concatenate([cells[8:16] + up_rows, cells[16:112], cells[112:120] + down_rows], axis=0)
        cells = cells + jnp.where(edge_lane[owned], roll(columns[owned], -16 - 32 * m), 0.0)
        cells = jnp.where(owned_core, cells, 0.0)
        planes[2, m, owned, :] = cells
        own_f[m // 2][m % 2] = cells
    sums += grams(own_f, own_f, ((0, 0), (0, 1), (1, 1)))
    sums += grams(own_f, own_m, ((0, 0), (0, 1), (1, 0), (1, 1)))

    line16 = lax.broadcasted_iota(jnp.int32, (16, 128), 0)
    lane16 = lax.broadcasted_iota(jnp.int32, (16, 128), 1)
    stacked = jnp.zeros((16, 128), F32)
    for q, values in enumerate(sums):
        stacked = jnp.where(line16 == q, jnp.sum(values, axis=0, keepdims=True), stacked)
    stacked = jnp.sum(stacked, axis=1, keepdims=True)
    mine = jnp.sum(jnp.where(line16 == lane16, stacked, 0.0), axis=0, keepdims=True)

    def all_sum(mine, out_ref, in_ref, place, partner, stage):
        out_ref[...] = mine
        in_ref[place] = mine
        copies = [
            pltpu.make_async_remote_copy(
                src_ref=out_ref,
                dst_ref=in_ref.at[place],
                send_sem=sum_send.at[stage, step],
                recv_sem=sum_recv.at[stage, step],
                device_id=partner(step),
                device_id_type=pl.DeviceIdType.MESH,
            )
            for step in range(1, 16)
        ]
        for copy in copies:
            copy.start()
        return copies

    copies = all_sum(mine, one_out, one_in, place_one, partner_one, 0)
    to_flat(lambda m, rows: planes[2, m, rows, :], forward_flat)
    for copy in copies:
        copy.wait()
    mine = jnp.sum(one_in[...], axis=0)
    copies = all_sum(mine, two_out, two_in, place_two, partner_two, 1)
    for copy in copies:
        copy.wait()
    cells_total = PLANES * CORE * CORE * ny * nx
    gathered = jnp.sum(two_in[...], axis=0) * F32(1.0 / cells_total)
    lane1 = lax.broadcasted_iota(jnp.int32, (1, 128), 1)
    m00, m01, m11, v00, v01, v11, f00, f01, f11, p00, p01, p10, p11 = [
        jnp.sum(jnp.where(lane1 == q, gathered, 0.0), axis=1, keepdims=True) for q in range(13)
    ]
    a, b, c = factor_of(m00, m01, m11)
    u00, u11 = 1.0 / a, 1.0 / c
    u01 = -b * u00 * u11
    w00 = u00 * u00 * v00
    w01 = u00 * (u01 * v00 + u11 * v01)
    w11 = u01 * u01 * v00 + 2.0 * u01 * u11 * v01 + u11 * u11 * v11
    alpha, beta, gamma = factor_of(w00, w01, w11)
    t00 = u00 / alpha
    t11 = u11 / gamma
    t01 = (u01 - beta * t00) / gamma
    x0, x1 = alpha * u00 + beta * u01, beta * u11
    y0, y1 = gamma * u01, gamma * u11

    def form(l, r):
        return (
            l[0] * (r[0] * f00 + r[1] * f01 - r[2] * p00 - r[3] * p01)
            + l[1] * (r[0] * f01 + r[1] * f11 - r[2] * p10 - r[3] * p11)
            - l[2] * (r[0] * p00 + r[1] * p10 - r[2] * m00 - r[3] * m01)
            - l[3] * (r[0] * p01 + r[1] * p11 - r[2] * m01 - r[3] * m11)
        )

    zero = jnp.zeros_like(a)
    z_first, z_second = (t00, zero, x0, x1), (t01, t11, y0, y1)
    rho, sigma, tau = factor_of(form(z_first, z_first), form(z_first, z_second), form(z_second, z_second))
    i0 = [value / rho for value in z_first]
    i1 = [(value - sigma * lead) / tau for value, lead in zip(z_second, i0)]

    half = FLAT // 2
    one, two = slice(0, half), slice(half, FLAT)
    v_one, v_two = object_flat[one, :], object_flat[two, :]
    f_one, f_two = forward_flat[one, :], forward_flat[two, :]
    m_one, m_two = measured[one, :], measured[two, :]
    object_flat[one, :] = t00 * v_one
    object_flat[two, :] = t01 * v_one + t11 * v_two
    image_flat[one, :] = i0[0] * f_one - i0[2] * m_one - i0[3] * m_two
    image_flat[two, :] = i1[0] * f_one + i1[1] * f_two - i1[2] * m_one - i1[3] * m_two
    stores = [
        pltpu.make_async_copy(object_flat, object_hbm, store_sem.at[0]),
        pltpu.make_async_copy(image_flat, image_hbm, store_sem.at[1]),
    ]
    for store in stores:
        store.start()
    which = lax.broadcasted_iota(jnp.int32, (3, 2, 2), 0)
    down = lax.broadcasted_iota(jnp.int32, (3, 2, 2), 1)
    across = lax.broadcasted_iota(jnp.int32, (3, 2, 2), 2)
    factors = jnp.zeros((3, 2, 2), F32)
    for i, triple in enumerate(((a, b, c), (alpha, beta, gamma), (rho, sigma, tau))):
        for (r, k), value in zip(((0, 0), (0, 1), (1, 1)), triple):
            here = (which == i) & (down == r) & (across == k)
            factors = jnp.where(here, value.reshape(1, 1, 1), factors)
    factors_ref[...] = factors
    for store in stores:
        store.wait()


def body(measured, psf_taps, offsets, window_mask):
    ny, nx = lax.axis_size("py"), lax.axis_size("px")
    any_space = pl.BlockSpec(memory_space=pl.ANY)
    vmem = pl.BlockSpec(memory_space=pltpu.VMEM)
    smem = pl.BlockSpec(memory_space=pltpu.SMEM)
    flat = jax.ShapeDtypeStruct((FLAT, 128), F32)
    forward, backward, taps_x, taps_y = tables()
    objects, images, factors = pl.pallas_call(
        functools.partial(kernel, ny, nx),
        out_shape=(flat, flat, jax.ShapeDtypeStruct((3, 2, 2), F32)),
        in_specs=[any_space, any_space, smem, any_space, any_space, any_space, any_space, any_space],
        out_specs=(any_space, any_space, vmem),
        scratch_shapes=[
            pltpu.VMEM((FLAT, 128), F32),
            pltpu.VMEM((3, KERNEL, KERNEL), BF16),
            pltpu.VMEM((PATCH, PATCH), jnp.int32),
            pltpu.VMEM((256, 256), BF16),
            pltpu.VMEM((256, 256), BF16),
            pltpu.VMEM((64, 256), BF16),
            pltpu.VMEM((256, 128), BF16),
            pltpu.VMEM((256, 384), F32),
            pltpu.VMEM((3, 4, PATCH, 128), F32),
            pltpu.VMEM((3, PATCH, 128), F32),
            pltpu.VMEM((3, 4, 32, PATCH), F32),
            pltpu.VMEM((2, 2, 4, 8, 128), F32),
            pltpu.VMEM((3, 4, 32, PATCH), F32),
            pltpu.VMEM((2, 4, 8, 128), F32),
            pltpu.VMEM((2, 4, 16, 128), F32),
            pltpu.VMEM((4, 16, 128), F32),
            pltpu.VMEM((FLAT, 128), F32),
            pltpu.VMEM((FLAT, 128), F32),
            pltpu.VMEM((FLAT, 128), F32),
            pltpu.VMEM((8, 128), F32),
            pltpu.VMEM((1, 128), F32),
            pltpu.VMEM((16, 1, 128), F32),
            pltpu.VMEM((1, 128), F32),
            pltpu.VMEM((16, 1, 128), F32),
            pltpu.SemaphoreType.DMA((7,)),
            pltpu.SemaphoreType.DMA((2,)),
            pltpu.SemaphoreType.DMA((3, 8)),
            pltpu.SemaphoreType.DMA((3, 8)),
            pltpu.SemaphoreType.DMA((2, 16)),
            pltpu.SemaphoreType.DMA((2, 16)),
        ],
        compiler_params=pltpu.CompilerParams(
            collective_id=0, has_side_effects=True, vmem_limit_bytes=48 * 1024 * 1024
        ),
        name="step",
    )(measured.reshape(FLAT, 128), psf_taps, offsets, window_mask, forward, backward, taps_x, taps_y)
    shape = (2, PLANES, 1, 1, CORE * CORE)
    return objects.reshape(shape), images.reshape(shape), factors


def solution(mesh):
    placed = (
        P(None, None, "py", "px", None),
        P("py", "px", None, None, None),
        P("py", "px", None),
        P("py", "px"),
    )
    return jax.shard_map(
        body,
        mesh=mesh,
        in_specs=placed,
        out_specs=(P(None, None, "py", "px", None), P(None, None, "py", "px", None), P()),
        check_vma=False,
    )
```

```python
import functools
import math

import jax
import jax.numpy as jnp
import numpy as np
from jax import lax
from jax.experimental import pallas as pl
from jax.experimental.pallas import tpu as pltpu
from jax.sharding import PartitionSpec as P

PLANES = 2
PATCH = 128
KERNEL = 32
HALF = 8
CORE = 112
FLAT = 2 * PLANES * CORE * CORE // 128
TAP = KERNEL // 2 - 1
EPSILON = 1e-06
F32 = jnp.float32
BF16 = jnp.bfloat16


def tables():
    ids = np.arange(PATCH)
    angle = 2 * np.pi * (np.outer(ids, ids) % PATCH) / PATCH
    cos, sin = np.cos(angle), -np.sin(angle)
    forward = np.block([[cos, sin], [-sin, cos]])
    places = np.arange(64) - KERNEL // 2
    angle = 2 * np.pi * (np.outer(places, ids) % PATCH) / PATCH
    cos, sin = np.cos(angle), -np.sin(angle)
    taps_x = np.concatenate([cos, sin], axis=1)
    taps_y = np.block([[cos.T, -sin.T], [sin.T, cos.T]])
    return [jnp.asarray(t, BF16) for t in (forward, forward.T, taps_x, taps_y)]


def mm(left, right):
    return jnp.dot(left, right, preferred_element_type=F32)


def roll(values, shift):
    shift = shift % 128
    return values if shift == 0 else pltpu.roll(values, shift, 1)


def total(values):
    return jnp.sum(jnp.sum(values, axis=0, keepdims=True), axis=1, keepdims=True)


class Exchange:
    def __init__(self, index, ny, nx, height, rows, cols, planes, packed, turned, row_in, col_in, corner_in, send, recv):
        self.index, self.height = index, height
        self.planes, self.packed, self.turned = planes, packed, turned
        self.row_in, self.col_in, self.corner_in = row_in, col_in, corner_in
        py, px = lax.axis_index("py"), lax.axis_index("px")
        up, down = lax.rem(py + ny - 1, ny), lax.rem(py + 1, ny)
        left, right = lax.rem(px + nx - 1, nx), lax.rem(px + 1, nx)
        top, bottom = pl.ds(rows[0], height), pl.ds(rows[1], height)
        (left_from, left_to), (right_from, right_to) = cols
        plan = [
            (planes.at[:, top, :], row_in.at[1], up, px),
            (planes.at[:, bottom, :], row_in.at[0], down, px),
            (turned.at[:, pl.ds(left_from, height), :], col_in.at[:, pl.ds(left_to, height), :], py, left),
            (turned.at[:, pl.ds(right_from, height), :], col_in.at[:, pl.ds(right_to, height), :], py, right),
            (packed.at[top, :], corner_in.at[3], up, left),
            (packed.at[top, :], corner_in.at[2], up, right),
            (packed.at[bottom, :], corner_in.at[1], down, left),
            (packed.at[bottom, :], corner_in.at[0], down, right),
        ]
        self.copies = [
            pltpu.make_async_remote_copy(
                src_ref=source,
                dst_ref=target,
                send_sem=send.at[index, i],
                recv_sem=recv.at[index, i],
                device_id={"py": to_y, "px": to_x},
                device_id_type=pl.DeviceIdType.MESH,
            )
            for i, (source, target, to_y, to_x) in enumerate(plan)
        ]

    def start(self):
        lane = lax.broadcasted_iota(jnp.int32, (PATCH, 128), 1)
        for copy in self.copies[:2]:
            copy.start()
        packed = roll(self.planes[0], 16)
        for m in range(1, 2 * PLANES):
            packed = jnp.where(lane >= 32 * m, roll(self.planes[m], 16 + 32 * m), packed)
        self.packed[...] = packed
        self.turned[...] = packed.T.reshape(2 * PLANES, 32, PATCH)
        for copy in self.copies[2:]:
            copy.start()

    def wait_recv(self):
        for copy in self.copies:
            copy.wait_recv()

    def wait_send(self):
        for copy in self.copies:
            copy.wait_send()

    def sides(self):
        columns = self.col_in[...].reshape(4 * 32, PATCH).T
        lane = lax.broadcasted_iota(jnp.int32, (self.height, 128), 1)
        is_left = lax.rem(lane, 32) >= 16
        upper = jnp.where(is_left, roll(self.corner_in[0], 16), roll(self.corner_in[1], -16))
        lower = jnp.where(is_left, roll(self.corner_in[2], 16), roll(self.corner_in[3], -16))
        return columns, upper, lower


def normalised(cells):
    s00 = sum(total(cells[0][z] * cells[0][z]) for z in range(PLANES))
    s01 = sum(total(cells[0][z] * cells[1][z]) for z in range(PLANES))
    s11 = sum(total(cells[1][z] * cells[1][z]) for z in range(PLANES))
    tiny = F32(1e-30)
    q0 = lax.rsqrt(jnp.maximum(s00, tiny))
    cross = s01 * q0
    q1 = lax.rsqrt(jnp.maximum(s11 - cross * cross, s11 * F32(1e-6) + tiny))
    first = [cells[0][z] * q0 for z in range(PLANES)]
    second = [(cells[1][z] - cross * first[z]) * q1 for z in range(PLANES)]
    return (first, second), (1.0 / q0, cross, 1.0 / q1)


def blur(cells, spectrum, forward_ref, backward_ref, adjoint):
    half = PATCH
    table, turned = forward_ref[...], backward_ref[...]
    values = jnp.concatenate(
        [jnp.concatenate([cells[k][z].astype(BF16) for k in range(2)], axis=1) for z in range(PLANES)], axis=0
    )
    along_x = mm(values, table).astype(BF16)
    swapped = jnp.concatenate(
        [
            jnp.concatenate([along_x[z * half : (z + 1) * half, c * half : (c + 1) * half] for z in range(PLANES)], axis=1)
            for c in range(2)
        ],
        axis=0,
    )
    along_y = mm(turned, swapped)
    re = [along_y[:half, z * half : (z + 1) * half] for z in range(PLANES)]
    im = [along_y[half:, z * half : (z + 1) * half] for z in range(PLANES)]
    tap_re = [spectrum[:half, t * half : (t + 1) * half] for t in range(3)]
    tap_im = [spectrum[half:, t * half : (t + 1) * half] for t in range(3)]
    sign = -1.0 if adjoint else 1.0
    out_re, out_im = [], []
    for z_out in range(PLANES):
        sum_re = sum_im = None
        for z_in in range(PLANES):
            depth = 1 + (z_in - z_out) if adjoint else 1 - (z_in - z_out)
            a, b = tap_re[depth], sign * tap_im[depth]
            part_re = re[z_in] * a - im[z_in] * b
            part_im = re[z_in] * b + im[z_in] * a
            sum_re = part_re if sum_re is None else sum_re + part_re
            sum_im = part_im if sum_im is None else sum_im + part_im
        out_re.append(sum_re.astype(BF16))
        out_im.append(sum_im.astype(BF16))
    product = jnp.concatenate([jnp.concatenate(out_re, axis=1), jnp.concatenate(out_im, axis=1)], axis=0)
    back_y = mm(table, product).astype(BF16)
    swapped = jnp.concatenate(
        [
            jnp.concatenate([back_y[c * half : (c + 1) * half, z * half : (z + 1) * half] for c in range(2)], axis=1)
            for z in range(PLANES)
        ],
        axis=0,
    )
    back_x = mm(swapped, turned)
    return [[back_x[z * half : (z + 1) * half, k * half : (k + 1) * half] for z in range(PLANES)] for k in range(2)]


def restored(cells, factor):
    first = [factor[0] * cells[0][z] for z in range(PLANES)]
    second = [factor[2] * cells[1][z] + factor[1] * cells[0][z] for z in range(PLANES)]
    return first, second


def factor_of(g00, g01, g11):
    r00 = jnp.sqrt(jnp.maximum(g00, 0.0) + EPSILON)
    r01 = g01 / r00
    r11 = jnp.sqrt(jnp.maximum(g11 - r01 * r01, 0.0) + EPSILON)
    return r00, r01, r11


def kernel(
    ny, nx,
    measured_hbm, taps_hbm, offsets_hbm, mask_hbm, forward_hbm, backward_hbm, taps_x_hbm, taps_y_hbm,
    object_ref, image_ref, factors_ref,
    measured, offsets, taps, mask, forward_ref, backward_ref, taps_x, taps_y,
    spectrum_ref, planes, packed, turned, row8, col_in, corner8, row16, corner16,
    object_flat, forward_flat,
    one_out, one_in, two_out, two_in,
    load_sem, send_sem, recv_sem, sum_send, sum_recv,
):
    py, px = lax.axis_index("py"), lax.axis_index("px")
    row, high, column = px // 8, lax.rem(px // 4, 2), lax.rem(px, 4)
    place_one, place_two = high * ny + py, row * 4 + column

    def partner_one(step):
        at = lax.rem(place_one + step, 16)
        return {"py": lax.rem(at, ny), "px": row * 8 + (at // ny) * 4 + column}

    def partner_two(step):
        at = lax.rem(place_two + step, 16)
        return {"py": py, "px": (at // 4) * 8 + high * 4 + lax.rem(at, 4)}

    exchange = functools.partial(Exchange, ny=ny, nx=nx, send=send_sem, recv=recv_sem)
    first = exchange(
        index=0, height=8, rows=(8, 112), cols=((24, 8), (0, 16)), planes=planes.at[0], packed=packed.at[0],
        turned=turned.at[0], row_in=row8.at[0], col_in=col_in.at[0], corner_in=corner8.at[0],
    )
    second = exchange(
        index=1, height=16, rows=(0, 112), cols=((16, 0), (0, 16)), planes=planes.at[1], packed=packed.at[1],
        turned=turned.at[1], row_in=row16, col_in=col_in.at[1], corner_in=corner16,
    )
    third = exchange(
        index=2, height=8, rows=(0, 120), cols=((16, 0), (8, 24)), planes=planes.at[2], packed=packed.at[2],
        turned=turned.at[2], row_in=row8.at[1], col_in=col_in.at[2], corner_in=corner8.at[1],
    )
    barrier = pltpu.get_barrier_semaphore()
    greeted = 0
    for dy in (ny - 1, 0, 1):
        for dx in (nx - 1, 0, 1):
            if dy or dx:
                to = {"py": lax.rem(py + dy, ny), "px": lax.rem(px + dx, nx)}
                pl.semaphore_signal(barrier, inc=1, device_id=to, device_id_type=pl.DeviceIdType.MESH)
                greeted += 1
    for step in range(1, 16):
        for to in (partner_one(step), partner_two(step)):
            pl.semaphore_signal(barrier, inc=1, device_id=to, device_id_type=pl.DeviceIdType.MESH)
            greeted += 1

    loads = [
        pltpu.make_async_copy(source, target, load_sem.at[i])
        for i, (source, target) in enumerate(
            [
                (measured_hbm, measured),
                (taps_hbm.at[0, 0, pl.ds(TAP, 3)], taps),
                (taps_x_hbm, taps_x),
                (taps_y_hbm, taps_y),
                (offsets_hbm, offsets),
                (mask_hbm, mask),
                (forward_hbm, forward_ref),
                (backward_hbm, backward_ref),
            ]
        )
    ]
    for load in loads:
        load.start()

    lane = lax.broadcasted_iota(jnp.int32, (PATCH, 128), 1)
    line = lax.broadcasted_iota(jnp.int32, (PATCH, 128), 0)
    owned_lane = (lane >= HALF) & (lane < PATCH - HALF)
    has_up, has_down, has_left, has_right = py > 0, py < ny - 1, px > 0, px < nx - 1
    low_y, high_y = jnp.where(has_up, 0, HALF), jnp.where(has_down, PATCH, PATCH - HALF)
    low_x, high_x = jnp.where(has_left, 0, HALF), jnp.where(has_right, PATCH, PATCH - HALF)
    inside = (line >= low_y) & (line < high_y) & (lane >= low_x) & (lane < high_x)

    loads[0].wait()
    lane14 = lax.broadcasted_iota(jnp.int32, (14, 128), 1)
    for m in range(4):
        planes[0, m, 0:HALF, :] = jnp.zeros((HALF, 128), F32)
        planes[0, m, PATCH - HALF : PATCH, :] = jnp.zeros((HALF, 128), F32)
        for k in range(8):
            if k < 7:
                high_part = measured[pl.ds(98 * m + k, 14, stride=7), :]
            if k == 0:
                both = high_part
            elif k == 7:
                both = measured[pl.ds(98 * m + 6, 14, stride=7), :]
            else:
                low_part = measured[pl.ds(98 * m + k - 1, 14, stride=7), :]
                both = jnp.where(lane14 >= 128 - 16 * k, low_part, high_part)
            planes[0, m, pl.ds(HALF + k, 14, stride=8), :] = roll(both, 16 * k + HALF)

    pl.semaphore_wait(barrier, greeted)
    first.start()

    for load in loads[1:5]:
        load.wait()
    shift_y, shift_x = offsets[0, 0, 0], offsets[0, 0, 1]
    pick_x = (
        lax.broadcasted_iota(jnp.int32, (KERNEL, 64), 1) == lax.broadcasted_iota(jnp.int32, (KERNEL, 64), 0) + shift_x
    )
    pick_y = (
        lax.broadcasted_iota(jnp.int32, (64, KERNEL), 0) == lax.broadcasted_iota(jnp.int32, (64, KERNEL), 1) + shift_y
    )
    pick_x = jnp.where(pick_x, 1.0, 0.0).astype(BF16)
    pick_y = jnp.where(pick_y, 1.0, 0.0).astype(BF16)
    placed = mm(taps[...].reshape(3 * KERNEL, KERNEL), pick_x).astype(BF16)
    kx = mm(placed, taps_x[...]).astype(BF16)
    side_by_side = jnp.concatenate([kx[t * KERNEL : (t + 1) * KERNEL] for t in range(3)], axis=1)
    kx = mm(pick_y, side_by_side).astype(BF16)
    kx = jnp.concatenate(
        [
            jnp.concatenate([kx[:, t * 256 + c * 128 : t * 256 + (c + 1) * 128] for t in range(3)], axis=1)
            for c in range(2)
        ],
        axis=0,
    )
    spectrum_ref[...] = mm(taps_y[...], kx) * F32(1.0 / (PATCH * PATCH))

    for load in loads[5:]:
        load.wait()
    weight = mask[...].astype(F32)

    def tile(left, right):
        return jnp.sum((left * right).reshape(-1, 8, 128), axis=0)

    owned = slice(HALF, PATCH - HALF)
    owned_core = owned_lane[owned]
    own_m = [[jnp.where(owned_core, planes[0, 2 * k + z, owned, :], 0.0) for z in range(PLANES)] for k in range(2)]

    def grams(left, right, pairs):
        return [sum(tile(left[i][z], right[j][z]) for z in range(PLANES)) for i, j in pairs]

    sums = grams(own_m, own_m, ((0, 0), (0, 1), (1, 1)))

    first.wait_recv()
    columns, upper, lower = first.sides()
    columns = jnp.concatenate([upper, columns[owned], lower], axis=0)
    window = [[None, None], [None, None]]
    for m in range(4):
        centre = jnp.concatenate([row8[0, 0, m], planes[0, m, owned, :], row8[0, 1, m]], axis=0)
        cells = jnp.where(owned_lane, centre, roll(columns, -16 - 32 * m))
        window[m // 2][m % 2] = jnp.where(inside, cells, 0.0)
    unit, factor = normalised(window)
    result = restored(blur(unit, spectrum_ref[...], forward_ref, backward_ref, True), factor)
    for m in range(4):
        planes[1, m] = result[m // 2][m % 2] * weight
    second.start()
    first.wait_send()

    second.wait_recv()
    columns, upper, lower = second.sides()
    upper, lower = jnp.where(has_up, upper, 0.0), jnp.where(has_down, lower, 0.0)
    columns = jnp.concatenate([columns[:16] + upper, columns[16:112], columns[112:] + lower], axis=0)
    edge_lane = ((lane < 16) & has_left) | ((lane >= 112) & has_right)
    second.wait_send()
    window = [[None, None], [None, None]]
    own_v = [[None, None], [None, None]]
    keep = jnp.where(inside, weight, 0.0)
    for m in range(4):
        cells = planes[1, m]
        up_rows = jnp.where(has_up, row16[0, m], 0.0)
        down_rows = jnp.where(has_down, row16[1, m], 0.0)
        cells = jnp.concatenate([cells[:16] + up_rows, cells[16:112], cells[112:] + down_rows], axis=0)
        cells = cells + jnp.where(edge_lane, roll(columns, -16 - 32 * m), 0.0)
        planes[1, m] = cells
        own_v[m // 2][m % 2] = jnp.where(owned_core, cells[owned], 0.0)
        window[m // 2][m % 2] = cells * keep
    sums += grams(own_v, own_v, ((0, 0), (0, 1), (1, 1)))
    unit, factor = normalised(window)
    result = restored(blur(unit, spectrum_ref[...], forward_ref, backward_ref, False), factor)
    for m in range(4):
        planes[2, m] = result[m // 2][m % 2]
    third.start()

    def to_flat(source, target):
        for m in range(4):
            for j in range(7):
                head = roll(source(m, pl.ds(HALF + j, 14, stride=8)), -16 * j - HALF)
                tail = roll(source(m, pl.ds(HALF + j + 1, 14, stride=8)), 104 - 16 * j)
                target[pl.ds(98 * m + j, 14, stride=7), :] = jnp.where(lane14 < 112 - 16 * j, head, tail)

    to_flat(lambda m, rows: planes[1, m, rows, :], object_flat)

    third.wait_recv()
    columns, upper, lower = third.sides()
    upper, lower = jnp.where(has_up, upper, 0.0), jnp.where(has_down, lower, 0.0)
    columns = jnp.concatenate([columns[:8], columns[8:16] + upper, columns[16:112], columns[112:120] + lower, columns[120:]], axis=0)
    third.wait_send()
    edge_lane = ((lane >= 8) & (lane < 16) & has_left) | ((lane >= 112) & (lane < 120) & has_right)
    own_f = [[None, None], [None, None]]
    for m in range(4):
        cells = planes[2, m]
        up_rows = jnp.where(has_up, row8[1, 0, m], 0.0)
        down_rows = jnp.where(has_down, row8[1, 1, m], 0.0)
        cells = jnp.concatenate([cells[8:16] + up_rows, cells[16:112], cells[112:120] + down_rows], axis=0)
        cells = cells + jnp.where(edge_lane[owned], roll(columns[owned], -16 - 32 * m), 0.0)
        cells = jnp.where(owned_core, cells, 0.0)
        planes[2, m, owned, :] = cells
        own_f[m // 2][m % 2] = cells
    sums += grams(own_f, own_f, ((0, 0), (0, 1), (1, 1)))
    sums += grams(own_f, own_m, ((0, 0), (0, 1), (1, 0), (1, 1)))

    line16 = lax.broadcasted_iota(jnp.int32, (16, 128), 0)
    lane16 = lax.broadcasted_iota(jnp.int32, (16, 128), 1)
    stacked = jnp.zeros((16, 128), F32)
    for q, values in enumerate(sums):
        stacked = jnp.where(line16 == q, jnp.sum(values, axis=0, keepdims=True), stacked)
    stacked = jnp.sum(stacked, axis=1, keepdims=True)
    mine = jnp.sum(jnp.where(line16 == lane16, stacked, 0.0), axis=0, keepdims=True)

    def all_sum(mine, out_ref, in_ref, place, partner, stage):
        out_ref[...] = mine
        in_ref[place] = mine
        copies = [
            pltpu.make_async_remote_copy(
                src_ref=out_ref,
                dst_ref=in_ref.at[place],
                send_sem=sum_send.at[stage, step],
                recv_sem=sum_recv.at[stage, step],
                device_id=partner(step),
                device_id_type=pl.DeviceIdType.MESH,
            )
            for step in range(1, 16)
        ]
        for copy in copies:
            copy.start()
        return copies

    copies = all_sum(mine, one_out, one_in, place_one, partner_one, 0)
    to_flat(lambda m, rows: planes[2, m, rows, :], forward_flat)
    for copy in copies:
        copy.wait()
    mine = jnp.sum(one_in[...], axis=0)
    copies = all_sum(mine, two_out, two_in, place_two, partner_two, 1)
    for copy in copies:
        copy.wait()
    cells_total = PLANES * CORE * CORE * ny * nx
    gathered = jnp.sum(two_in[...], axis=0) * F32(1.0 / cells_total)
    lane1 = lax.broadcasted_iota(jnp.int32, (1, 128), 1)
    m00, m01, m11, v00, v01, v11, f00, f01, f11, p00, p01, p10, p11 = [
        jnp.sum(jnp.where(lane1 == q, gathered, 0.0), axis=1, keepdims=True) for q in range(13)
    ]
    a, b, c = factor_of(m00, m01, m11)
    u00, u11 = 1.0 / a, 1.0 / c
    u01 = -b * u00 * u11
    w00 = u00 * u00 * v00
    w01 = u00 * (u01 * v00 + u11 * v01)
    w11 = u01 * u01 * v00 + 2.0 * u01 * u11 * v01 + u11 * u11 * v11
    alpha, beta, gamma = factor_of(w00, w01, w11)
    t00 = u00 / alpha
    t11 = u11 / gamma
    t01 = (u01 - beta * t00) / gamma
    x0, x1 = alpha * u00 + beta * u01, beta * u11
    y0, y1 = gamma * u01, gamma * u11

    def form(l, r):
        return (
            l[0] * (r[0] * f00 + r[1] * f01 - r[2] * p00 - r[3] * p01)
            + l[1] * (r[0] * f01 + r[1] * f11 - r[2] * p10 - r[3] * p11)
            - l[2] * (r[0] * p00 + r[1] * p10 - r[2] * m00 - r[3] * m01)
            - l[3] * (r[0] * p01 + r[1] * p11 - r[2] * m01 - r[3] * m11)
        )

    zero = jnp.zeros_like(a)
    z_first, z_second = (t00, zero, x0, x1), (t01, t11, y0, y1)
    rho, sigma, tau = factor_of(form(z_first, z_first), form(z_first, z_second), form(z_second, z_second))
    i0 = [value / rho for value in z_first]
    i1 = [(value - sigma * lead) / tau for value, lead in zip(z_second, i0)]

    half = FLAT // 2
    one, two = slice(0, half), slice(half, FLAT)
    v_one, v_two = object_flat[one, :], object_flat[two, :]
    f_one, f_two = forward_flat[one, :], forward_flat[two, :]
    m_one, m_two = measured[one, :], measured[two, :]
    object_ref[one, :] = t00 * v_one
    object_ref[two, :] = t01 * v_one + t11 * v_two
    image_ref[one, :] = i0[0] * f_one - i0[2] * m_one - i0[3] * m_two
    image_ref[two, :] = i1[0] * f_one + i1[1] * f_two - i1[2] * m_one - i1[3] * m_two
    down = lax.broadcasted_iota(jnp.int32, (2, 2, 3), 0)
    across = lax.broadcasted_iota(jnp.int32, (2, 2, 3), 1)
    which = lax.broadcasted_iota(jnp.int32, (2, 2, 3), 2)
    factors = jnp.zeros((2, 2, 3), F32)
    for i, triple in enumerate(((a, b, c), (alpha, beta, gamma), (rho, sigma, tau))):
        for (r, k), value in zip(((0, 0), (0, 1), (1, 1)), triple):
            here = (which == i) & (down == r) & (across == k)
            factors = jnp.where(here, value.reshape(1, 1, 1), factors)
    factors_ref[...] = factors


def store(object_vmem, image_vmem, factors_vmem, object_hbm, image_hbm, factors_hbm, sem):
    copies = [
        pltpu.make_async_copy(source, target, sem.at[i])
        for i, (source, target) in enumerate(
            ((object_vmem, object_hbm), (image_vmem, image_hbm), (factors_vmem, factors_hbm))
        )
    ]
    for copy in copies:
        copy.start()
    for copy in copies:
        copy.wait()


def body(measured, psf_taps, offsets, window_mask):
    ny, nx = lax.axis_size("py"), lax.axis_size("px")
    hbm = pl.BlockSpec(memory_space=pltpu.HBM)
    vmem = pl.BlockSpec(memory_space=pltpu.VMEM)
    operands = [measured.reshape(FLAT, 128), psf_taps, offsets, window_mask, *tables()]
    operands = [pltpu.with_memory_space_constraint(operand, pltpu.HBM) for operand in operands]
    results = pl.pallas_call(
        functools.partial(kernel, ny, nx),
        out_shape=(pltpu.VMEM((FLAT, 128), F32), pltpu.VMEM((FLAT, 128), F32), pltpu.VMEM((2, 2, 3), F32)),
        in_specs=[hbm] * 8,
        out_specs=(vmem, vmem, vmem),
        scratch_shapes=[
            pltpu.VMEM((FLAT, 128), F32),
            pltpu.SMEM((1, 1, 2), jnp.int32),
            pltpu.VMEM((3, KERNEL, KERNEL), BF16),
            pltpu.VMEM((PATCH, PATCH), jnp.int32),
            pltpu.VMEM((256, 256), BF16),
            pltpu.VMEM((256, 256), BF16),
            pltpu.VMEM((64, 256), BF16),
            pltpu.VMEM((256, 128), BF16),
            pltpu.VMEM((256, 384), F32),
            pltpu.VMEM((3, 4, PATCH, 128), F32),
            pltpu.VMEM((3, PATCH, 128), F32),
            pltpu.VMEM((3, 4, 32, PATCH), F32),
            pltpu.VMEM((2, 2, 4, 8, 128), F32),
            pltpu.VMEM((3, 4, 32, PATCH), F32),
            pltpu.VMEM((2, 4, 8, 128), F32),
            pltpu.VMEM((2, 4, 16, 128), F32),
            pltpu.VMEM((4, 16, 128), F32),
            pltpu.VMEM((FLAT, 128), F32),
            pltpu.VMEM((FLAT, 128), F32),
            pltpu.VMEM((1, 128), F32),
            pltpu.VMEM((16, 1, 128), F32),
            pltpu.VMEM((1, 128), F32),
            pltpu.VMEM((16, 1, 128), F32),
            pltpu.SemaphoreType.DMA((8,)),
            pltpu.SemaphoreType.DMA((3, 8)),
            pltpu.SemaphoreType.DMA((3, 8)),
            pltpu.SemaphoreType.DMA((2, 16)),
            pltpu.SemaphoreType.DMA((2, 16)),
        ],
        compiler_params=pltpu.CompilerParams(
            collective_id=0, has_side_effects=True, vmem_limit_bytes=48 * 1024 * 1024
        ),
        name="step",
    )(*operands)
    results = [pltpu.with_memory_space_constraint(result, pltpu.VMEM) for result in results]
    objects, images, factors = pl.pallas_call(
        store,
        out_shape=(pltpu.HBM((FLAT, 128), F32), pltpu.HBM((FLAT, 128), F32), pltpu.HBM((2, 2, 3), F32)),
        in_specs=[vmem] * 3,
        out_specs=(hbm, hbm, hbm),
        scratch_shapes=[pltpu.SemaphoreType.DMA((3,))],
        name="store",
    )(*results)
    shape = (2, PLANES, 1, 1, CORE * CORE)
    return objects.reshape(shape), images.reshape(shape), factors.transpose(2, 0, 1)


def solution(mesh):
    placed = (
        P(None, None, "py", "px", None),
        P("py", "px", None, None, None),
        P("py", "px", None),
        P("py", "px"),
    )
    return jax.shard_map(
        body,
        mesh=mesh,
        in_specs=placed,
        out_specs=(P(None, None, "py", "px", None), P(None, None, "py", "px", None), P()),
        check_vma=False,
    )
```

```python
import functools
import math

import jax
import jax.numpy as jnp
import numpy as np
from jax import lax
from jax.experimental import pallas as pl
from jax.experimental.pallas import tpu as pltpu
from jax.sharding import PartitionSpec as P

PLANES = 2
PATCH = 128
KERNEL = 32
HALF = 8
CORE = 112
FLAT = 2 * PLANES * CORE * CORE // 128
TAP = KERNEL // 2 - 1
EPSILON = 1e-06
F32 = jnp.float32
BF16 = jnp.bfloat16


def tables():
    ids = np.arange(PATCH)
    angle = 2 * np.pi * (np.outer(ids, ids) % PATCH) / PATCH
    cos, sin = np.cos(angle), -np.sin(angle)
    forward = np.block([[cos, sin], [-sin, cos]])
    places = np.arange(64) - KERNEL // 2
    angle = 2 * np.pi * (np.outer(places, ids) % PATCH) / PATCH
    cos, sin = np.cos(angle), -np.sin(angle)
    taps_x = np.concatenate([cos, sin], axis=1)
    taps_y = np.block([[cos.T, -sin.T], [sin.T, cos.T]])
    return [jnp.asarray(t, BF16) for t in (forward, forward.T, taps_x, taps_y)]


def mm(left, right):
    return jnp.dot(left, right, preferred_element_type=F32)


def roll(values, shift):
    shift = shift % 128
    return values if shift == 0 else pltpu.roll(values, shift, 1)


def total(values):
    return jnp.sum(jnp.sum(values, axis=0, keepdims=True), axis=1, keepdims=True)


class Exchange:
    def __init__(self, index, ny, nx, height, rows, cols, planes, packed, turned, row_in, col_in, corner_in, send, recv):
        self.index, self.height = index, height
        self.planes, self.packed, self.turned = planes, packed, turned
        self.row_in, self.col_in, self.corner_in = row_in, col_in, corner_in
        py, px = lax.axis_index("py"), lax.axis_index("px")
        up, down = lax.rem(py + ny - 1, ny), lax.rem(py + 1, ny)
        left, right = lax.rem(px + nx - 1, nx), lax.rem(px + 1, nx)
        has_up, has_down, has_left, has_right = py > 0, py < ny - 1, px > 0, px < nx - 1
        top, bottom = pl.ds(rows[0], height), pl.ds(rows[1], height)
        (left_from, left_to), (right_from, right_to) = cols
        plan = [
            (planes.at[:, top, :], row_in.at[1], up, px, has_up),
            (planes.at[:, bottom, :], row_in.at[0], down, px, has_down),
            (turned.at[:, pl.ds(left_from, height), :], col_in.at[:, pl.ds(left_to, height), :], py, left, has_left),
            (turned.at[:, pl.ds(right_from, height), :], col_in.at[:, pl.ds(right_to, height), :], py, right, has_right),
            (packed.at[top, :], corner_in.at[3], up, left, has_up & has_left),
            (packed.at[top, :], corner_in.at[2], up, right, has_up & has_right),
            (packed.at[bottom, :], corner_in.at[1], down, left, has_down & has_left),
            (packed.at[bottom, :], corner_in.at[0], down, right, has_down & has_right),
        ]
        self.copies = [
            pltpu.make_async_remote_copy(
                src_ref=source,
                dst_ref=target,
                send_sem=send.at[index, i],
                recv_sem=recv.at[index, i],
                device_id={"py": to_y, "px": to_x},
                device_id_type=pl.DeviceIdType.MESH,
            )
            for i, (source, target, to_y, to_x, _) in enumerate(plan)
        ]
        self.there = [there for *_, there in plan]
        self.back = [self.there[i] for i in (1, 0, 3, 2, 7, 6, 5, 4)]

    def start(self):
        lane = lax.broadcasted_iota(jnp.int32, (PATCH, 128), 1)
        packed = roll(self.planes[0], 16)
        for m in range(1, 2 * PLANES):
            packed = jnp.where(lane >= 32 * m, roll(self.planes[m], 16 + 32 * m), packed)
        self.packed[...] = packed
        for i in range(4, 8):
            pl.when(self.there[i])(self.copies[i].start)
        self.turned[...] = packed.T.reshape(2 * PLANES, 32, PATCH)
        for i in (2, 3, 0, 1):
            pl.when(self.there[i])(self.copies[i].start)

    def wait_recv(self):
        for copy, there in zip(self.copies, self.back):
            pl.when(there)(copy.wait_recv)

    def wait_send(self):
        for copy, there in zip(self.copies, self.there):
            pl.when(there)(copy.wait_send)

    def sides(self):
        columns = self.col_in[...].reshape(4 * 32, PATCH).T
        lane = lax.broadcasted_iota(jnp.int32, (self.height, 128), 1)
        is_left = lax.rem(lane, 32) >= 16
        upper = jnp.where(is_left, roll(self.corner_in[0], 16), roll(self.corner_in[1], -16))
        lower = jnp.where(is_left, roll(self.corner_in[2], 16), roll(self.corner_in[3], -16))
        return columns, upper, lower


def normalised(cells):
    s00 = sum(total(cells[0][z] * cells[0][z]) for z in range(PLANES))
    s01 = sum(total(cells[0][z] * cells[1][z]) for z in range(PLANES))
    s11 = sum(total(cells[1][z] * cells[1][z]) for z in range(PLANES))
    tiny = F32(1e-30)
    q0 = lax.rsqrt(jnp.maximum(s00, tiny))
    cross = s01 * q0
    q1 = lax.rsqrt(jnp.maximum(s11 - cross * cross, s11 * F32(1e-6) + tiny))
    first = [cells[0][z] * q0 for z in range(PLANES)]
    second = [(cells[1][z] - cross * first[z]) * q1 for z in range(PLANES)]
    return (first, second), (1.0 / q0, cross, 1.0 / q1)


def blur(cells, spectrum, forward_ref, backward_ref, adjoint):
    half = PATCH
    table, turned = forward_ref[...], backward_ref[...]
    values = jnp.concatenate(
        [jnp.concatenate([cells[k][z].astype(BF16) for k in range(2)], axis=1) for z in range(PLANES)], axis=0
    )
    along_x = mm(values, table).astype(BF16)
    swapped = jnp.concatenate(
        [
            jnp.concatenate([along_x[z * half : (z + 1) * half, c * half : (c + 1) * half] for z in range(PLANES)], axis=1)
            for c in range(2)
        ],
        axis=0,
    )
    along_y = mm(turned, swapped)
    re = [along_y[:half, z * half : (z + 1) * half] for z in range(PLANES)]
    im = [along_y[half:, z * half : (z + 1) * half] for z in range(PLANES)]
    tap_re = [spectrum[:half, t * half : (t + 1) * half] for t in range(3)]
    tap_im = [spectrum[half:, t * half : (t + 1) * half] for t in range(3)]
    sign = -1.0 if adjoint else 1.0
    out_re, out_im = [], []
    for z_out in range(PLANES):
        sum_re = sum_im = None
        for z_in in range(PLANES):
            depth = 1 + (z_in - z_out) if adjoint else 1 - (z_in - z_out)
            a, b = tap_re[depth], sign * tap_im[depth]
            part_re = re[z_in] * a - im[z_in] * b
            part_im = re[z_in] * b + im[z_in] * a
            sum_re = part_re if sum_re is None else sum_re + part_re
            sum_im = part_im if sum_im is None else sum_im + part_im
        out_re.append(sum_re.astype(BF16))
        out_im.append(sum_im.astype(BF16))
    product = jnp.concatenate([jnp.concatenate(out_re, axis=1), jnp.concatenate(out_im, axis=1)], axis=0)
    back_y = mm(table, product).astype(BF16)
    swapped = jnp.concatenate(
        [
            jnp.concatenate([back_y[c * half : (c + 1) * half, z * half : (z + 1) * half] for c in range(2)], axis=1)
            for z in range(PLANES)
        ],
        axis=0,
    )
    back_x = mm(swapped, turned)
    return [[back_x[z * half : (z + 1) * half, k * half : (k + 1) * half] for z in range(PLANES)] for k in range(2)]


def restored(cells, factor):
    first = [factor[0] * cells[0][z] for z in range(PLANES)]
    second = [factor[2] * cells[1][z] + factor[1] * cells[0][z] for z in range(PLANES)]
    return first, second


def factor_of(g00, g01, g11):
    r00 = jnp.sqrt(jnp.maximum(g00, 0.0) + EPSILON)
    r01 = g01 / r00
    r11 = jnp.sqrt(jnp.maximum(g11 - r01 * r01, 0.0) + EPSILON)
    return r00, r01, r11


def kernel(
    ny, nx,
    measured_hbm, taps_hbm, offsets_hbm, mask_hbm, forward_hbm, backward_hbm, taps_x_hbm, taps_y_hbm,
    object_ref, image_ref, factors_ref,
    measured, offsets, taps, mask, forward_ref, backward_ref, taps_x, taps_y,
    spectrum_ref, planes, packed, turned, row8, col_in, corner8, row16, corner16,
    object_flat, forward_flat,
    one_out, one_in, two_out, two_in,
    load_sem, send_sem, recv_sem, sum_send, sum_recv,
):
    py, px = lax.axis_index("py"), lax.axis_index("px")
    row, high, column = px // 8, lax.rem(px // 4, 2), lax.rem(px, 4)
    place_one, place_two = high * ny + py, row * 4 + column

    def partner_one(step):
        at = lax.rem(place_one + step, 16)
        return {"py": lax.rem(at, ny), "px": row * 8 + (at // ny) * 4 + column}

    def partner_two(step):
        at = lax.rem(place_two + step, 16)
        return {"py": py, "px": (at // 4) * 8 + high * 4 + lax.rem(at, 4)}

    exchange = functools.partial(Exchange, ny=ny, nx=nx, send=send_sem, recv=recv_sem)
    first = exchange(
        index=0, height=8, rows=(8, 112), cols=((24, 8), (0, 16)), planes=planes.at[0], packed=packed.at[0],
        turned=turned.at[0], row_in=row8.at[0], col_in=col_in.at[0], corner_in=corner8.at[0],
    )
    second = exchange(
        index=1, height=16, rows=(0, 112), cols=((16, 0), (0, 16)), planes=planes.at[1], packed=packed.at[1],
        turned=turned.at[1], row_in=row16, col_in=col_in.at[1], corner_in=corner16,
    )
    third = exchange(
        index=2, height=8, rows=(0, 120), cols=((16, 0), (8, 24)), planes=planes.at[2], packed=packed.at[2],
        turned=turned.at[2], row_in=row8.at[1], col_in=col_in.at[2], corner_in=corner8.at[1],
    )
    barrier = pltpu.get_barrier_semaphore()
    has_up, has_down, has_left, has_right = py > 0, py < ny - 1, px > 0, px < nx - 1
    greeted = jnp.int32(30)
    for dx, has_x in ((nx - 1, has_left), (1, has_right), (0, None)):
        for dy, has_y in ((ny - 1, has_up), (1, has_down), (0, None)):
            if dx or dy:
                there = has_x if has_y is None else has_y if has_x is None else has_x & has_y
                to = {"py": lax.rem(py + dy, ny), "px": lax.rem(px + dx, nx)}
                greeted += there.astype(jnp.int32)

                @pl.when(there)
                def _(to=to):
                    pl.semaphore_signal(barrier, inc=1, device_id=to, device_id_type=pl.DeviceIdType.MESH)

    loads = [
        pltpu.make_async_copy(source, target, load_sem.at[i])
        for i, (source, target) in enumerate(
            [
                (measured_hbm, measured),
                (taps_hbm.at[0, 0, pl.ds(TAP, 3)], taps),
                (taps_x_hbm, taps_x),
                (taps_y_hbm, taps_y),
                (offsets_hbm, offsets),
                (mask_hbm, mask),
                (forward_hbm, forward_ref),
                (backward_hbm, backward_ref),
            ]
        )
    ]
    for load in loads:
        load.start()

    for step in range(1, 16):
        for to in (partner_one(step), partner_two(step)):
            pl.semaphore_signal(barrier, inc=1, device_id=to, device_id_type=pl.DeviceIdType.MESH)

    lane = lax.broadcasted_iota(jnp.int32, (PATCH, 128), 1)
    line = lax.broadcasted_iota(jnp.int32, (PATCH, 128), 0)
    owned_lane = (lane >= HALF) & (lane < PATCH - HALF)
    low_y, high_y = jnp.where(has_up, 0, HALF), jnp.where(has_down, PATCH, PATCH - HALF)
    low_x, high_x = jnp.where(has_left, 0, HALF), jnp.where(has_right, PATCH, PATCH - HALF)
    inside = (line >= low_y) & (line < high_y) & (lane >= low_x) & (lane < high_x)

    loads[0].wait()
    lane14 = lax.broadcasted_iota(jnp.int32, (14, 128), 1)
    for m in range(4):
        planes[0, m, 0:HALF, :] = jnp.zeros((HALF, 128), F32)
        planes[0, m, PATCH - HALF : PATCH, :] = jnp.zeros((HALF, 128), F32)
        for k in range(8):
            if k < 7:
                high_part = measured[pl.ds(98 * m + k, 14, stride=7), :]
            if k == 0:
                both = high_part
            elif k == 7:
                both = measured[pl.ds(98 * m + 6, 14, stride=7), :]
            else:
                low_part = measured[pl.ds(98 * m + k - 1, 14, stride=7), :]
                both = jnp.where(lane14 >= 128 - 16 * k, low_part, high_part)
            planes[0, m, pl.ds(HALF + k, 14, stride=8), :] = roll(both, 16 * k + HALF)

    pl.semaphore_wait(barrier, greeted)
    first.start()

    for load in loads[1:5]:
        load.wait()
    shift_y, shift_x = offsets[0, 0, 0], offsets[0, 0, 1]
    pick_x = (
        lax.broadcasted_iota(jnp.int32, (KERNEL, 64), 1) == lax.broadcasted_iota(jnp.int32, (KERNEL, 64), 0) + shift_x
    )
    pick_y = (
        lax.broadcasted_iota(jnp.int32, (64, KERNEL), 0) == lax.broadcasted_iota(jnp.int32, (64, KERNEL), 1) + shift_y
    )
    pick_x = jnp.where(pick_x, 1.0, 0.0).astype(BF16)
    pick_y = jnp.where(pick_y, 1.0, 0.0).astype(BF16)
    placed = mm(taps[...].reshape(3 * KERNEL, KERNEL), pick_x).astype(BF16)
    kx = mm(placed, taps_x[...]).astype(BF16)
    side_by_side = jnp.concatenate([kx[t * KERNEL : (t + 1) * KERNEL] for t in range(3)], axis=1)
    kx = mm(pick_y, side_by_side).astype(BF16)
    kx = jnp.concatenate(
        [
            jnp.concatenate([kx[:, t * 256 + c * 128 : t * 256 + (c + 1) * 128] for t in range(3)], axis=1)
            for c in range(2)
        ],
        axis=0,
    )
    spectrum_ref[...] = mm(taps_y[...], kx) * F32(1.0 / (PATCH * PATCH))

    for load in loads[5:]:
        load.wait()
    weight = mask[...].astype(F32)

    def tile(left, right):
        return jnp.sum((left * right).reshape(-1, 8, 128), axis=0)

    owned = slice(HALF, PATCH - HALF)
    owned_core = owned_lane[owned]
    own_m = [[jnp.where(owned_core, planes[0, 2 * k + z, owned, :], 0.0) for z in range(PLANES)] for k in range(2)]

    def grams(left, right, pairs):
        return [sum(tile(left[i][z], right[j][z]) for z in range(PLANES)) for i, j in pairs]

    sums = grams(own_m, own_m, ((0, 0), (0, 1), (1, 1)))

    first.wait_recv()
    columns, upper, lower = first.sides()
    columns = jnp.concatenate([upper, columns[owned], lower], axis=0)
    window = [[None, None], [None, None]]
    for m in range(4):
        centre = jnp.concatenate([row8[0, 0, m], planes[0, m, owned, :], row8[0, 1, m]], axis=0)
        cells = jnp.where(owned_lane, centre, roll(columns, -16 - 32 * m))
        window[m // 2][m % 2] = jnp.where(inside, cells, 0.0)
    unit, factor = normalised(window)
    result = restored(blur(unit, spectrum_ref[...], forward_ref, backward_ref, True), factor)
    for m in range(4):
        planes[1, m] = result[m // 2][m % 2] * weight
    second.start()
    first.wait_send()

    second.wait_recv()
    columns, upper, lower = second.sides()
    upper, lower = jnp.where(has_up, upper, 0.0), jnp.where(has_down, lower, 0.0)
    columns = jnp.concatenate([columns[:16] + upper, columns[16:112], columns[112:] + lower], axis=0)
    edge_lane = ((lane < 16) & has_left) | ((lane >= 112) & has_right)
    second.wait_send()
    window = [[None, None], [None, None]]
    own_v = [[None, None], [None, None]]
    keep = jnp.where(inside, weight, 0.0)
    for m in range(4):
        cells = planes[1, m]
        up_rows = jnp.where(has_up, row16[0, m], 0.0)
        down_rows = jnp.where(has_down, row16[1, m], 0.0)
        cells = jnp.concatenate([cells[:16] + up_rows, cells[16:112], cells[112:] + down_rows], axis=0)
        cells = cells + jnp.where(edge_lane, roll(columns, -16 - 32 * m), 0.0)
        planes[1, m] = cells
        own_v[m // 2][m % 2] = jnp.where(owned_core, cells[owned], 0.0)
        window[m // 2][m % 2] = cells * keep
    sums += grams(own_v, own_v, ((0, 0), (0, 1), (1, 1)))
    unit, factor = normalised(window)
    result = restored(blur(unit, spectrum_ref[...], forward_ref, backward_ref, False), factor)
    for m in range(4):
        planes[2, m] = result[m // 2][m % 2]
    third.start()

    def to_flat(source, target):
        for m in range(4):
            for j in range(7):
                head = roll(source(m, pl.ds(HALF + j, 14, stride=8)), -16 * j - HALF)
                tail = roll(source(m, pl.ds(HALF + j + 1, 14, stride=8)), 104 - 16 * j)
                target[pl.ds(98 * m + j, 14, stride=7), :] = jnp.where(lane14 < 112 - 16 * j, head, tail)

    to_flat(lambda m, rows: planes[1, m, rows, :], object_flat)

    third.wait_recv()
    columns, upper, lower = third.sides()
    upper, lower = jnp.where(has_up, upper, 0.0), jnp.where(has_down, lower, 0.0)
    columns = jnp.concatenate([columns[:8], columns[8:16] + upper, columns[16:112], columns[112:120] + lower, columns[120:]], axis=0)
    third.wait_send()
    edge_lane = ((lane >= 8) & (lane < 16) & has_left) | ((lane >= 112) & (lane < 120) & has_right)
    own_f = [[None, None], [None, None]]
    for m in range(4):
        cells = planes[2, m]
        up_rows = jnp.where(has_up, row8[1, 0, m], 0.0)
        down_rows = jnp.where(has_down, row8[1, 1, m], 0.0)
        cells = jnp.concatenate([cells[8:16] + up_rows, cells[16:112], cells[112:120] + down_rows], axis=0)
        cells = cells + jnp.where(edge_lane[owned], roll(columns[owned], -16 - 32 * m), 0.0)
        cells = jnp.where(owned_core, cells, 0.0)
        planes[2, m, owned, :] = cells
        own_f[m // 2][m % 2] = cells
    sums += grams(own_f, own_f, ((0, 0), (0, 1), (1, 1)))
    sums += grams(own_f, own_m, ((0, 0), (0, 1), (1, 0), (1, 1)))

    line16 = lax.broadcasted_iota(jnp.int32, (16, 128), 0)
    lane16 = lax.broadcasted_iota(jnp.int32, (16, 128), 1)
    stacked = jnp.zeros((16, 128), F32)
    for q, values in enumerate(sums):
        stacked = jnp.where(line16 == q, jnp.sum(values, axis=0, keepdims=True), stacked)
    stacked = jnp.sum(stacked, axis=1, keepdims=True)
    mine = jnp.sum(jnp.where(line16 == lane16, stacked, 0.0), axis=0, keepdims=True)

    def all_sum(mine, out_ref, in_ref, place, partner, stage):
        out_ref[...] = mine
        in_ref[place] = mine
        copies = [
            pltpu.make_async_remote_copy(
                src_ref=out_ref,
                dst_ref=in_ref.at[place],
                send_sem=sum_send.at[stage, step],
                recv_sem=sum_recv.at[stage, step],
                device_id=partner(step),
                device_id_type=pl.DeviceIdType.MESH,
            )
            for step in range(1, 16)
        ]
        for copy in copies:
            copy.start()
        return copies

    copies = all_sum(mine, one_out, one_in, place_one, partner_one, 0)
    to_flat(lambda m, rows: planes[2, m, rows, :], forward_flat)
    for copy in copies:
        copy.wait()
    mine = jnp.sum(one_in[...], axis=0)
    copies = all_sum(mine, two_out, two_in, place_two, partner_two, 1)
    for copy in copies:
        copy.wait()
    cells_total = PLANES * CORE * CORE * ny * nx
    gathered = jnp.sum(two_in[...], axis=0) * F32(1.0 / cells_total)
    lane1 = lax.broadcasted_iota(jnp.int32, (1, 128), 1)
    m00, m01, m11, v00, v01, v11, f00, f01, f11, p00, p01, p10, p11 = [
        jnp.sum(jnp.where(lane1 == q, gathered, 0.0), axis=1, keepdims=True) for q in range(13)
    ]
    a, b, c = factor_of(m00, m01, m11)
    u00, u11 = 1.0 / a, 1.0 / c
    u01 = -b * u00 * u11
    w00 = u00 * u00 * v00
    w01 = u00 * (u01 * v00 + u11 * v01)
    w11 = u01 * u01 * v00 + 2.0 * u01 * u11 * v01 + u11 * u11 * v11
    alpha, beta, gamma = factor_of(w00, w01, w11)
    t00 = u00 / alpha
    t11 = u11 / gamma
    t01 = (u01 - beta * t00) / gamma
    x0, x1 = alpha * u00 + beta * u01, beta * u11
    y0, y1 = gamma * u01, gamma * u11

    def form(l, r):
        return (
            l[0] * (r[0] * f00 + r[1] * f01 - r[2] * p00 - r[3] * p01)
            + l[1] * (r[0] * f01 + r[1] * f11 - r[2] * p10 - r[3] * p11)
            - l[2] * (r[0] * p00 + r[1] * p10 - r[2] * m00 - r[3] * m01)
            - l[3] * (r[0] * p01 + r[1] * p11 - r[2] * m01 - r[3] * m11)
        )

    zero = jnp.zeros_like(a)
    z_first, z_second = (t00, zero, x0, x1), (t01, t11, y0, y1)
    rho, sigma, tau = factor_of(form(z_first, z_first), form(z_first, z_second), form(z_second, z_second))
    i0 = [value / rho for value in z_first]
    i1 = [(value - sigma * lead) / tau for value, lead in zip(z_second, i0)]

    half = FLAT // 2
    one, two = slice(0, half), slice(half, FLAT)
    v_one, v_two = object_flat[one, :], object_flat[two, :]
    f_one, f_two = forward_flat[one, :], forward_flat[two, :]
    m_one, m_two = measured[one, :], measured[two, :]
    object_ref[one, :] = t00 * v_one
    object_ref[two, :] = t01 * v_one + t11 * v_two
    image_ref[one, :] = i0[0] * f_one - i0[2] * m_one - i0[3] * m_two
    image_ref[two, :] = i1[0] * f_one + i1[1] * f_two - i1[2] * m_one - i1[3] * m_two
    down = lax.broadcasted_iota(jnp.int32, (2, 2, 3), 0)
    across = lax.broadcasted_iota(jnp.int32, (2, 2, 3), 1)
    which = lax.broadcasted_iota(jnp.int32, (2, 2, 3), 2)
    factors = jnp.zeros((2, 2, 3), F32)
    for i, triple in enumerate(((a, b, c), (alpha, beta, gamma), (rho, sigma, tau))):
        for (r, k), value in zip(((0, 0), (0, 1), (1, 1)), triple):
            here = (which == i) & (down == r) & (across == k)
            factors = jnp.where(here, value.reshape(1, 1, 1), factors)
    factors_ref[...] = factors


def store(object_vmem, image_vmem, factors_vmem, object_hbm, image_hbm, factors_hbm, sem):
    copies = [
        pltpu.make_async_copy(source, target, sem.at[i])
        for i, (source, target) in enumerate(
            ((object_vmem, object_hbm), (image_vmem, image_hbm), (factors_vmem, factors_hbm))
        )
    ]
    for copy in copies:
        copy.start()
    for copy in copies:
        copy.wait()


def body(measured, psf_taps, offsets, window_mask):
    ny, nx = lax.axis_size("py"), lax.axis_size("px")
    hbm = pl.BlockSpec(memory_space=pltpu.HBM)
    vmem = pl.BlockSpec(memory_space=pltpu.VMEM)
    operands = [measured.reshape(FLAT, 128), psf_taps, offsets, window_mask, *tables()]
    operands = [pltpu.with_memory_space_constraint(operand, pltpu.HBM) for operand in operands]
    results = pl.pallas_call(
        functools.partial(kernel, ny, nx),
        out_shape=(pltpu.VMEM((FLAT, 128), F32), pltpu.VMEM((FLAT, 128), F32), pltpu.VMEM((2, 2, 3), F32)),
        in_specs=[hbm] * 8,
        out_specs=(vmem, vmem, vmem),
        scratch_shapes=[
            pltpu.VMEM((FLAT, 128), F32),
            pltpu.SMEM((1, 1, 2), jnp.int32),
            pltpu.VMEM((3, KERNEL, KERNEL), BF16),
            pltpu.VMEM((PATCH, PATCH), jnp.int32),
            pltpu.VMEM((256, 256), BF16),
            pltpu.VMEM((256, 256), BF16),
            pltpu.VMEM((64, 256), BF16),
            pltpu.VMEM((256, 128), BF16),
            pltpu.VMEM((256, 384), F32),
            pltpu.VMEM((3, 4, PATCH, 128), F32),
            pltpu.VMEM((3, PATCH, 128), F32),
            pltpu.VMEM((3, 4, 32, PATCH), F32),
            pltpu.VMEM((2, 2, 4, 8, 128), F32),
            pltpu.VMEM((3, 4, 32, PATCH), F32),
            pltpu.VMEM((2, 4, 8, 128), F32),
            pltpu.VMEM((2, 4, 16, 128), F32),
            pltpu.VMEM((4, 16, 128), F32),
            pltpu.VMEM((FLAT, 128), F32),
            pltpu.VMEM((FLAT, 128), F32),
            pltpu.VMEM((1, 128), F32),
            pltpu.VMEM((16, 1, 128), F32),
            pltpu.VMEM((1, 128), F32),
            pltpu.VMEM((16, 1, 128), F32),
            pltpu.SemaphoreType.DMA((8,)),
            pltpu.SemaphoreType.DMA((3, 8)),
            pltpu.SemaphoreType.DMA((3, 8)),
            pltpu.SemaphoreType.DMA((2, 16)),
            pltpu.SemaphoreType.DMA((2, 16)),
        ],
        compiler_params=pltpu.CompilerParams(
            collective_id=0, has_side_effects=True, vmem_limit_bytes=48 * 1024 * 1024
        ),
        name="step",
    )(*operands)
    results = [pltpu.with_memory_space_constraint(result, pltpu.VMEM) for result in results]
    objects, images, factors = pl.pallas_call(
        store,
        out_shape=(pltpu.HBM((FLAT, 128), F32), pltpu.HBM((FLAT, 128), F32), pltpu.HBM((2, 2, 3), F32)),
        in_specs=[vmem] * 3,
        out_specs=(hbm, hbm, hbm),
        scratch_shapes=[pltpu.SemaphoreType.DMA((3,))],
        name="store",
    )(*results)
    shape = (2, PLANES, 1, 1, CORE * CORE)
    return objects.reshape(shape), images.reshape(shape), factors.transpose(2, 0, 1)


def solution(mesh):
    placed = (
        P(None, None, "py", "px", None),
        P("py", "px", None, None, None),
        P("py", "px", None),
        P("py", "px"),
    )
    return jax.shard_map(
        body,
        mesh=mesh,
        in_specs=placed,
        out_specs=(P(None, None, "py", "px", None), P(None, None, "py", "px", None), P()),
        check_vma=False,
    )
```

```python
import functools
import math

import jax
import jax.numpy as jnp
import numpy as np
from jax import lax
from jax.experimental import pallas as pl
from jax.experimental.pallas import tpu as pltpu
from jax.sharding import PartitionSpec as P

PLANES = 2
PATCH = 128
KERNEL = 32
HALF = 8
CORE = 112
FLAT = 2 * PLANES * CORE * CORE // 128
TAP = KERNEL // 2 - 1
EPSILON = 1e-06
F32 = jnp.float32
BF16 = jnp.bfloat16


def tables():
    ids = np.arange(PATCH)
    angle = 2 * np.pi * (np.outer(ids, ids) % PATCH) / PATCH
    cos, sin = np.cos(angle), -np.sin(angle)
    forward = np.block([[cos, sin], [-sin, cos]])
    places = np.arange(64) - KERNEL // 2
    angle = 2 * np.pi * (np.outer(places, ids) % PATCH) / PATCH
    cos, sin = np.cos(angle), -np.sin(angle)
    taps_x = np.concatenate([cos, sin], axis=1)
    taps_y = np.block([[cos.T, -sin.T], [sin.T, cos.T]])
    return [jnp.asarray(t, BF16) for t in (forward, forward.T, taps_x, taps_y)]


def mm(left, right):
    return jnp.dot(left, right, preferred_element_type=F32)


def roll(values, shift):
    shift = shift % 128
    return values if shift == 0 else pltpu.roll(values, shift, 1)


def total(values):
    return jnp.sum(jnp.sum(values, axis=0, keepdims=True), axis=1, keepdims=True)


class Exchange:
    def __init__(self, index, ny, nx, height, rows, cols_out, cols_in, outs, ins, send, recv):
        self.height, self.rows, self.cols_out, self.cols_in = height, rows, cols_out, cols_in
        self.row_out, self.col_out, self.corner_out = (ref.at[index] for ref in outs)
        self.row_in, self.col_in, self.corner_in = (ref.at[index] for ref in ins)
        py, px = lax.axis_index("py"), lax.axis_index("px")
        up, down = lax.rem(py + ny - 1, ny), lax.rem(py + 1, ny)
        left, right = lax.rem(px + nx - 1, nx), lax.rem(px + 1, nx)
        has_up, has_down, has_left, has_right = py > 0, py < ny - 1, px > 0, px < nx - 1
        strip = pl.ds(0, 4 * height)
        top, bottom = (pl.ds(0, 16), pl.ds(16, 16)) if height == 16 else (pl.ds(0, 16), pl.ds(0, 16))
        plan = [
            (self.row_out.at[0, strip], self.row_in.at[1, strip], up, px, has_up),
            (self.row_out.at[1, strip], self.row_in.at[0, strip], down, px, has_down),
            (self.col_out.at[0, strip], self.col_in.at[1, strip], py, left, has_left),
            (self.col_out.at[1, strip], self.col_in.at[0, strip], py, right, has_right),
            (self.corner_out.at[top], self.corner_in.at[3], up, left, has_up & has_left),
            (self.corner_out.at[top], self.corner_in.at[2], up, right, has_up & has_right),
            (self.corner_out.at[bottom], self.corner_in.at[1], down, left, has_down & has_left),
            (self.corner_out.at[bottom], self.corner_in.at[0], down, right, has_down & has_right),
        ]
        self.copies = [
            pltpu.make_async_remote_copy(
                src_ref=source,
                dst_ref=target,
                send_sem=send.at[index, i],
                recv_sem=recv.at[index, i],
                device_id={"py": to_y, "px": to_x},
                device_id_type=pl.DeviceIdType.MESH,
            )
            for i, (source, target, to_y, to_x, _) in enumerate(plan)
        ]
        self.there = [there for *_, there in plan]
        self.back = [self.there[i] for i in (1, 0, 3, 2, 7, 6, 5, 4)]

    def pack(self, planes, starting=False):
        def start(*which):
            for i in which if starting else ():
                pl.when(self.there[i])(self.copies[i].start)

        lane = lax.broadcasted_iota(jnp.int32, (PATCH, 128), 1)
        height, (top, bottom) = self.height, self.rows
        packed = roll(planes[0], 16)
        for m in range(1, 2 * PLANES):
            packed = jnp.where(lane >= 32 * m, roll(planes[m], 16 + 32 * m), packed)
        ends = jnp.concatenate([packed[top : top + height], packed[bottom : bottom + height]], axis=0)
        self.corner_out[0 : 2 * height, :] = ends.astype(BF16)
        start(4, 5, 6, 7)
        turned = packed.T
        for side, first in enumerate(self.cols_out):
            strips = [turned[32 * m + first : 32 * m + first + height] for m in range(2 * PLANES)]
            self.col_out[side, 0 : 4 * height, :] = jnp.concatenate(strips, axis=0).astype(BF16)
        start(2, 3)
        for side, first in enumerate(self.rows):
            strips = [planes[m][first : first + height] for m in range(2 * PLANES)]
            self.row_out[side, 0 : 4 * height, :] = jnp.concatenate(strips, axis=0).astype(BF16)
        start(0, 1)

    def start(self):
        for i in (4, 5, 6, 7, 2, 3, 0, 1):
            pl.when(self.there[i])(self.copies[i].start)

    def wait_recv(self):
        for copy, there in zip(self.copies, self.back):
            pl.when(there)(copy.wait_recv)

    def wait_send(self):
        for copy, there in zip(self.copies, self.there):
            pl.when(there)(copy.wait_send)

    def row_strips(self):
        height = self.height
        both = [self.row_in[side, 0 : 4 * height, :].astype(F32) for side in range(2)]
        return [[strips[m * height : (m + 1) * height] for m in range(2 * PLANES)] for strips in both]

    def sides(self):
        height = self.height
        both = [self.col_in[side, 0 : 4 * height, :].astype(F32) for side in range(2)]
        pieces = []
        for m in range(2 * PLANES):
            slots = [both[1][m * height : (m + 1) * height] for _ in range(32 // height)]
            slots[self.cols_in // height] = both[0][m * height : (m + 1) * height]
            pieces += slots
        columns = jnp.concatenate(pieces, axis=0).T
        lane = lax.broadcasted_iota(jnp.int32, (height, 128), 1)
        is_left = lax.rem(lane, 32) >= 16
        corner = [self.corner_in[i].astype(F32) for i in range(4)]
        if height == 8:
            corner = [corner[0][8:], corner[1][8:], corner[2][:8], corner[3][:8]]
        upper = jnp.where(is_left, roll(corner[0], 16), roll(corner[1], -16))
        lower = jnp.where(is_left, roll(corner[2], 16), roll(corner[3], -16))
        return columns, upper, lower


def normaliser(s00, s01, s11):
    tiny = F32(1e-30)
    q0 = lax.rsqrt(jnp.maximum(s00, tiny))
    cross = s01 * q0
    q1 = lax.rsqrt(jnp.maximum(s11 - cross * cross, s11 * F32(1e-6) + tiny))
    return (q0, cross, q1), (1.0 / q0, cross, 1.0 / q1)


def normalised(cells, scalars):
    q0, cross, q1 = scalars
    first = [cells[0][z] * q0 for z in range(PLANES)]
    second = [(cells[1][z] - cross * first[z]) * q1 for z in range(PLANES)]
    return first, second


def blur(cells, spectrum, forward_ref, backward_ref, adjoint):
    half = PATCH
    table, turned = forward_ref[...], backward_ref[...]
    values = jnp.concatenate(
        [jnp.concatenate([cells[k][z].astype(BF16) for k in range(2)], axis=1) for z in range(PLANES)], axis=0
    )
    along_x = mm(values, table).astype(BF16)
    swapped = jnp.concatenate(
        [
            jnp.concatenate([along_x[z * half : (z + 1) * half, c * half : (c + 1) * half] for z in range(PLANES)], axis=1)
            for c in range(2)
        ],
        axis=0,
    )
    along_y = mm(turned, swapped)
    re = [along_y[:half, z * half : (z + 1) * half] for z in range(PLANES)]
    im = [along_y[half:, z * half : (z + 1) * half] for z in range(PLANES)]
    tap_re = [spectrum[:half, t * half : (t + 1) * half] for t in range(3)]
    tap_im = [spectrum[half:, t * half : (t + 1) * half] for t in range(3)]
    sign = -1.0 if adjoint else 1.0
    out_re, out_im = [], []
    for z_out in range(PLANES):
        sum_re = sum_im = None
        for z_in in range(PLANES):
            depth = 1 + (z_in - z_out) if adjoint else 1 - (z_in - z_out)
            a, b = tap_re[depth], sign * tap_im[depth]
            part_re = re[z_in] * a - im[z_in] * b
            part_im = re[z_in] * b + im[z_in] * a
            sum_re = part_re if sum_re is None else sum_re + part_re
            sum_im = part_im if sum_im is None else sum_im + part_im
        out_re.append(sum_re.astype(BF16))
        out_im.append(sum_im.astype(BF16))
    product = jnp.concatenate([jnp.concatenate(out_re, axis=1), jnp.concatenate(out_im, axis=1)], axis=0)
    back_y = mm(table, product).astype(BF16)
    swapped = jnp.concatenate(
        [
            jnp.concatenate([back_y[c * half : (c + 1) * half, z * half : (z + 1) * half] for c in range(2)], axis=1)
            for z in range(PLANES)
        ],
        axis=0,
    )
    back_x = mm(swapped, turned)
    return [[back_x[z * half : (z + 1) * half, k * half : (k + 1) * half] for z in range(PLANES)] for k in range(2)]


def restored(cells, factor):
    first = [factor[0] * cells[0][z] for z in range(PLANES)]
    second = [factor[2] * cells[1][z] + factor[1] * cells[0][z] for z in range(PLANES)]
    return first, second


def factor_of(g00, g01, g11):
    r00 = jnp.sqrt(jnp.maximum(g00, 0.0) + EPSILON)
    r01 = g01 / r00
    r11 = jnp.sqrt(jnp.maximum(g11 - r01 * r01, 0.0) + EPSILON)
    return r00, r01, r11


def kernel(
    ny, nx,
    measured_hbm, taps_hbm, offsets_hbm, mask_hbm, forward_hbm, backward_hbm, taps_x_hbm, taps_y_hbm,
    object_ref, image_ref, factors_ref,
    measured, offsets, taps, mask, forward_ref, backward_ref, taps_x, taps_y,
    spectrum_ref, planes, row_out, col_out, corner_out, row_in, col_in, corner_in,
    object_flat, forward_flat,
    one_out, one_in, two_out, two_in,
    load_sem, send_sem, recv_sem, sum_send, sum_recv,
):
    py, px = lax.axis_index("py"), lax.axis_index("px")
    row, high, column = px // 8, lax.rem(px // 4, 2), lax.rem(px, 4)
    place_one, place_two = high * ny + py, row * 4 + column

    def partner_one(step):
        at = lax.rem(place_one + step, 16)
        return {"py": lax.rem(at, ny), "px": row * 8 + (at // ny) * 4 + column}

    def partner_two(step):
        at = lax.rem(place_two + step, 16)
        return {"py": py, "px": (at // 4) * 8 + high * 4 + lax.rem(at, 4)}

    exchange = functools.partial(
        Exchange, ny=ny, nx=nx, outs=(row_out, col_out, corner_out), ins=(row_in, col_in, corner_in),
        send=send_sem, recv=recv_sem,
    )
    first = exchange(index=0, height=8, rows=(8, 112), cols_out=(24, 0), cols_in=16)
    second = exchange(index=1, height=16, rows=(0, 112), cols_out=(16, 0), cols_in=16)
    third = exchange(index=2, height=8, rows=(0, 120), cols_out=(16, 8), cols_in=24)
    barrier = pltpu.get_barrier_semaphore()
    has_up, has_down, has_left, has_right = py > 0, py < ny - 1, px > 0, px < nx - 1
    greeted = jnp.int32(30)
    for dx, has_x in ((nx - 1, has_left), (1, has_right), (0, None)):
        for dy, has_y in ((ny - 1, has_up), (1, has_down), (0, None)):
            if dx or dy:
                there = has_x if has_y is None else has_y if has_x is None else has_x & has_y
                to = {"py": lax.rem(py + dy, ny), "px": lax.rem(px + dx, nx)}
                greeted += there.astype(jnp.int32)

                @pl.when(there)
                def _(to=to):
                    pl.semaphore_signal(barrier, inc=1, device_id=to, device_id_type=pl.DeviceIdType.MESH)

    loads = [
        pltpu.make_async_copy(source, target, load_sem.at[i])
        for i, (source, target) in enumerate(
            [
                (measured_hbm, measured),
                (taps_hbm.at[0, 0, pl.ds(TAP, 3)], taps),
                (taps_x_hbm, taps_x),
                (taps_y_hbm, taps_y),
                (offsets_hbm, offsets),
                (mask_hbm, mask),
                (forward_hbm, forward_ref),
                (backward_hbm, backward_ref),
            ]
        )
    ]
    for load in loads:
        load.start()

    for step in range(1, 16):
        for to in (partner_one(step), partner_two(step)):
            pl.semaphore_signal(barrier, inc=1, device_id=to, device_id_type=pl.DeviceIdType.MESH)

    lane = lax.broadcasted_iota(jnp.int32, (PATCH, 128), 1)
    line = lax.broadcasted_iota(jnp.int32, (PATCH, 128), 0)
    owned_lane = (lane >= HALF) & (lane < PATCH - HALF)
    low_y, high_y = jnp.where(has_up, 0, HALF), jnp.where(has_down, PATCH, PATCH - HALF)
    low_x, high_x = jnp.where(has_left, 0, HALF), jnp.where(has_right, PATCH, PATCH - HALF)
    inside = (line >= low_y) & (line < high_y) & (lane >= low_x) & (lane < high_x)

    loads[0].wait()
    lane14 = lax.broadcasted_iota(jnp.int32, (14, 128), 1)
    for m in range(4):
        planes[0, m, 0:HALF, :] = jnp.zeros((HALF, 128), F32)
        planes[0, m, PATCH - HALF : PATCH, :] = jnp.zeros((HALF, 128), F32)
        for k in range(8):
            if k < 7:
                high_part = measured[pl.ds(98 * m + k, 14, stride=7), :]
            if k == 0:
                both = high_part
            elif k == 7:
                both = measured[pl.ds(98 * m + 6, 14, stride=7), :]
            else:
                low_part = measured[pl.ds(98 * m + k - 1, 14, stride=7), :]
                both = jnp.where(lane14 >= 128 - 16 * k, low_part, high_part)
            planes[0, m, pl.ds(HALF + k, 14, stride=8), :] = roll(both, 16 * k + HALF)

    first.pack([planes[0, m] for m in range(4)])
    pl.semaphore_wait(barrier, greeted)
    first.start()

    for load in loads[1:5]:
        load.wait()
    shift_y, shift_x = offsets[0, 0, 0], offsets[0, 0, 1]
    pick_x = (
        lax.broadcasted_iota(jnp.int32, (KERNEL, 64), 1) == lax.broadcasted_iota(jnp.int32, (KERNEL, 64), 0) + shift_x
    )
    pick_y = (
        lax.broadcasted_iota(jnp.int32, (64, KERNEL), 0) == lax.broadcasted_iota(jnp.int32, (64, KERNEL), 1) + shift_y
    )
    pick_x = jnp.where(pick_x, 1.0, 0.0).astype(BF16)
    pick_y = jnp.where(pick_y, 1.0, 0.0).astype(BF16)
    placed = mm(taps[...].reshape(3 * KERNEL, KERNEL), pick_x).astype(BF16)
    kx = mm(placed, taps_x[...]).astype(BF16)
    side_by_side = jnp.concatenate([kx[t * KERNEL : (t + 1) * KERNEL] for t in range(3)], axis=1)
    kx = mm(pick_y, side_by_side).astype(BF16)
    kx = jnp.concatenate(
        [
            jnp.concatenate([kx[:, t * 256 + c * 128 : t * 256 + (c + 1) * 128] for t in range(3)], axis=1)
            for c in range(2)
        ],
        axis=0,
    )
    spectrum_ref[...] = mm(taps_y[...], kx) * F32(1.0 / (PATCH * PATCH))

    for load in loads[5:]:
        load.wait()
    weight = mask[...].astype(F32)

    def tile(left, right):
        return jnp.sum((left * right).reshape(-1, 8, 128), axis=0)

    owned = slice(HALF, PATCH - HALF)
    owned_core = owned_lane[owned]
    own_m = [[jnp.where(owned_core, planes[0, 2 * k + z, owned, :], 0.0) for z in range(PLANES)] for k in range(2)]

    def grams(left, right, pairs):
        return [sum(tile(left[i][z], right[j][z]) for z in range(PLANES)) for i, j in pairs]

    sums = grams(own_m, own_m, ((0, 0), (0, 1), (1, 1)))

    def scalars_of(tiles):
        return normaliser(*(total(values) for values in tiles))

    scalars, factor = scalars_of(sums)
    first.wait_recv()
    columns, upper, lower = first.sides()
    up_rows, down_rows = first.row_strips()
    columns = jnp.concatenate([upper, columns[owned], lower], axis=0)
    window = [[None, None], [None, None]]
    for m in range(4):
        centre = jnp.concatenate([up_rows[m], planes[0, m, owned, :], down_rows[m]], axis=0)
        cells = jnp.where(owned_lane, centre, roll(columns, -16 - 32 * m))
        window[m // 2][m % 2] = jnp.where(inside, cells, 0.0)
    result = restored(blur(normalised(window, scalars), spectrum_ref[...], forward_ref, backward_ref, True), factor)
    result = [result[m // 2][m % 2] * weight for m in range(4)]
    second.pack(result, starting=True)
    for m in range(4):
        planes[1, m] = result[m]
    pairs = ((0, 0), (0, 1), (1, 1))
    scalars, factor = scalars_of(grams((result[:2], result[2:]), (result[:2], result[2:]), pairs))

    second.wait_recv()
    columns, upper, lower = second.sides()
    up_rows, down_rows = second.row_strips()
    upper, lower = jnp.where(has_up, upper, 0.0), jnp.where(has_down, lower, 0.0)
    columns = jnp.concatenate([columns[:16] + upper, columns[16:112], columns[112:] + lower], axis=0)
    edge_lane = ((lane < 16) & has_left) | ((lane >= 112) & has_right)
    window = [[None, None], [None, None]]
    keep = jnp.where(inside, weight, 0.0)
    for m in range(4):
        cells = planes[1, m]
        above, below = jnp.where(has_up, up_rows[m], 0.0), jnp.where(has_down, down_rows[m], 0.0)
        cells = jnp.concatenate([cells[:16] + above, cells[16:112], cells[112:] + below], axis=0)
        cells = cells + jnp.where(edge_lane, roll(columns, -16 - 32 * m), 0.0)
        planes[1, m] = cells
        window[m // 2][m % 2] = cells * keep
    result = restored(blur(normalised(window, scalars), spectrum_ref[...], forward_ref, backward_ref, False), factor)
    result = [result[m // 2][m % 2] for m in range(4)]
    third.pack(result, starting=True)
    for m in range(4):
        planes[2, m] = result[m]
    own_v = [[jnp.where(owned_core, planes[1, 2 * k + z, owned, :], 0.0) for z in range(PLANES)] for k in range(2)]
    sums += grams(own_v, own_v, pairs)

    def to_flat(source, target):
        for m in range(4):
            for j in range(7):
                head = roll(source(m, pl.ds(HALF + j, 14, stride=8)), -16 * j - HALF)
                tail = roll(source(m, pl.ds(HALF + j + 1, 14, stride=8)), 104 - 16 * j)
                target[pl.ds(98 * m + j, 14, stride=7), :] = jnp.where(lane14 < 112 - 16 * j, head, tail)

    to_flat(lambda m, rows: planes[1, m, rows, :], object_flat)

    third.wait_recv()
    columns, upper, lower = third.sides()
    upper, lower = jnp.where(has_up, upper, 0.0), jnp.where(has_down, lower, 0.0)
    columns = jnp.concatenate([columns[:8], columns[8:16] + upper, columns[16:112], columns[112:120] + lower, columns[120:]], axis=0)
    up_rows, down_rows = third.row_strips()
    edge_lane = ((lane >= 8) & (lane < 16) & has_left) | ((lane >= 112) & (lane < 120) & has_right)
    own_f = [[None, None], [None, None]]
    for m in range(4):
        cells = planes[2, m]
        above, below = jnp.where(has_up, up_rows[m], 0.0), jnp.where(has_down, down_rows[m], 0.0)
        cells = jnp.concatenate([cells[8:16] + above, cells[16:112], cells[112:120] + below], axis=0)
        cells = cells + jnp.where(edge_lane[owned], roll(columns[owned], -16 - 32 * m), 0.0)
        cells = jnp.where(owned_core, cells, 0.0)
        planes[2, m, owned, :] = cells
        own_f[m // 2][m % 2] = cells
    sums += grams(own_f, own_f, ((0, 0), (0, 1), (1, 1)))
    sums += grams(own_f, own_m, ((0, 0), (0, 1), (1, 0), (1, 1)))

    line16 = lax.broadcasted_iota(jnp.int32, (16, 128), 0)
    lane16 = lax.broadcasted_iota(jnp.int32, (16, 128), 1)
    stacked = jnp.zeros((16, 128), F32)
    for q, values in enumerate(sums):
        stacked = jnp.where(line16 == q, jnp.sum(values, axis=0, keepdims=True), stacked)
    stacked = jnp.sum(stacked, axis=1, keepdims=True)
    mine = jnp.sum(jnp.where(line16 == lane16, stacked, 0.0), axis=0, keepdims=True)

    def all_sum(mine, out_ref, in_ref, place, partner, stage):
        out_ref[...] = mine
        in_ref[place] = mine
        copies = [
            pltpu.make_async_remote_copy(
                src_ref=out_ref,
                dst_ref=in_ref.at[place],
                send_sem=sum_send.at[stage, step],
                recv_sem=sum_recv.at[stage, step],
                device_id=partner(step),
                device_id_type=pl.DeviceIdType.MESH,
            )
            for step in range(1, 16)
        ]
        for copy in copies:
            copy.start()
        return copies

    copies = all_sum(mine, one_out, one_in, place_one, partner_one, 0)
    to_flat(lambda m, rows: planes[2, m, rows, :], forward_flat)
    for copy in copies:
        copy.wait_recv()
    mine = jnp.sum(one_in[...], axis=0)
    sent = copies
    copies = all_sum(mine, two_out, two_in, place_two, partner_two, 1)
    for phase in (first, second, third):
        phase.wait_send()
    for copy in sent:
        copy.wait_send()
    for copy in copies:
        copy.wait()
    cells_total = PLANES * CORE * CORE * ny * nx
    gathered = jnp.sum(two_in[...], axis=0) * F32(1.0 / cells_total)
    lane1 = lax.broadcasted_iota(jnp.int32, (1, 128), 1)
    m00, m01, m11, v00, v01, v11, f00, f01, f11, p00, p01, p10, p11 = [
        jnp.sum(jnp.where(lane1 == q, gathered, 0.0), axis=1, keepdims=True) for q in range(13)
    ]
    a, b, c = factor_of(m00, m01, m11)
    u00, u11 = 1.0 / a, 1.0 / c
    u01 = -b * u00 * u11
    w00 = u00 * u00 * v00
    w01 = u00 * (u01 * v00 + u11 * v01)
    w11 = u01 * u01 * v00 + 2.0 * u01 * u11 * v01 + u11 * u11 * v11
    alpha, beta, gamma = factor_of(w00, w01, w11)
    t00 = u00 / alpha
    t11 = u11 / gamma
    t01 = (u01 - beta * t00) / gamma
    x0, x1 = alpha * u00 + beta * u01, beta * u11
    y0, y1 = gamma * u01, gamma * u11

    def form(l, r):
        return (
            l[0] * (r[0] * f00 + r[1] * f01 - r[2] * p00 - r[3] * p01)
            + l[1] * (r[0] * f01 + r[1] * f11 - r[2] * p10 - r[3] * p11)
            - l[2] * (r[0] * p00 + r[1] * p10 - r[2] * m00 - r[3] * m01)
            - l[3] * (r[0] * p01 + r[1] * p11 - r[2] * m01 - r[3] * m11)
        )

    zero = jnp.zeros_like(a)
    z_first, z_second = (t00, zero, x0, x1), (t01, t11, y0, y1)
    rho, sigma, tau = factor_of(form(z_first, z_first), form(z_first, z_second), form(z_second, z_second))
    i0 = [value / rho for value in z_first]
    i1 = [(value - sigma * lead) / tau for value, lead in zip(z_second, i0)]

    half = FLAT // 2
    one, two = slice(0, half), slice(half, FLAT)
    v_one, v_two = object_flat[one, :], object_flat[two, :]
    f_one, f_two = forward_flat[one, :], forward_flat[two, :]
    m_one, m_two = measured[one, :], measured[two, :]
    object_ref[one, :] = t00 * v_one
    object_ref[two, :] = t01 * v_one + t11 * v_two
    image_ref[one, :] = i0[0] * f_one - i0[2] * m_one - i0[3] * m_two
    image_ref[two, :] = i1[0] * f_one + i1[1] * f_two - i1[2] * m_one - i1[3] * m_two
    down = lax.broadcasted_iota(jnp.int32, (2, 2, 3), 0)
    across = lax.broadcasted_iota(jnp.int32, (2, 2, 3), 1)
    which = lax.broadcasted_iota(jnp.int32, (2, 2, 3), 2)
    factors = jnp.zeros((2, 2, 3), F32)
    for i, triple in enumerate(((a, b, c), (alpha, beta, gamma), (rho, sigma, tau))):
        for (r, k), value in zip(((0, 0), (0, 1), (1, 1)), triple):
            here = (which == i) & (down == r) & (across == k)
            factors = jnp.where(here, value.reshape(1, 1, 1), factors)
    factors_ref[...] = factors


def store(object_vmem, image_vmem, factors_vmem, object_hbm, image_hbm, factors_hbm, sem):
    copies = [
        pltpu.make_async_copy(source, target, sem.at[i])
        for i, (source, target) in enumerate(
            ((object_vmem, object_hbm), (image_vmem, image_hbm), (factors_vmem, factors_hbm))
        )
    ]
    for copy in copies:
        copy.start()
    for copy in copies:
        copy.wait()


def body(measured, psf_taps, offsets, window_mask):
    ny, nx = lax.axis_size("py"), lax.axis_size("px")
    hbm = pl.BlockSpec(memory_space=pltpu.HBM)
    vmem = pl.BlockSpec(memory_space=pltpu.VMEM)
    operands = [measured.reshape(FLAT, 128), psf_taps, offsets, window_mask, *tables()]
    operands = [pltpu.with_memory_space_constraint(operand, pltpu.HBM) for operand in operands]
    results = pl.pallas_call(
        functools.partial(kernel, ny, nx),
        out_shape=(pltpu.VMEM((FLAT, 128), F32), pltpu.VMEM((FLAT, 128), F32), pltpu.VMEM((2, 2, 3), F32)),
        in_specs=[hbm] * 8,
        out_specs=(vmem, vmem, vmem),
        scratch_shapes=[
            pltpu.VMEM((FLAT, 128), F32),
            pltpu.SMEM((1, 1, 2), jnp.int32),
            pltpu.VMEM((3, KERNEL, KERNEL), BF16),
            pltpu.VMEM((PATCH, PATCH), jnp.int32),
            pltpu.VMEM((256, 256), BF16),
            pltpu.VMEM((256, 256), BF16),
            pltpu.VMEM((64, 256), BF16),
            pltpu.VMEM((256, 128), BF16),
            pltpu.VMEM((256, 384), F32),
            pltpu.VMEM((3, 4, PATCH, 128), F32),
            pltpu.VMEM((3, 2, 64, 128), BF16),
            pltpu.VMEM((3, 2, 64, 128), BF16),
            pltpu.VMEM((3, 32, 128), BF16),
            pltpu.VMEM((3, 2, 64, 128), BF16),
            pltpu.VMEM((3, 2, 64, 128), BF16),
            pltpu.VMEM((3, 4, 16, 128), BF16),
            pltpu.VMEM((FLAT, 128), F32),
            pltpu.VMEM((FLAT, 128), F32),
            pltpu.VMEM((1, 128), F32),
            pltpu.VMEM((16, 1, 128), F32),
            pltpu.VMEM((1, 128), F32),
            pltpu.VMEM((16, 1, 128), F32),
            pltpu.SemaphoreType.DMA((8,)),
            pltpu.SemaphoreType.DMA((3, 8)),
            pltpu.SemaphoreType.DMA((3, 8)),
            pltpu.SemaphoreType.DMA((2, 16)),
            pltpu.SemaphoreType.DMA((2, 16)),
        ],
        compiler_params=pltpu.CompilerParams(
            collective_id=0, has_side_effects=True, vmem_limit_bytes=48 * 1024 * 1024
        ),
        name="step",
    )(*operands)
    results = [pltpu.with_memory_space_constraint(result, pltpu.VMEM) for result in results]
    objects, images, factors = pl.pallas_call(
        store,
        out_shape=(pltpu.HBM((FLAT, 128), F32), pltpu.HBM((FLAT, 128), F32), pltpu.HBM((2, 2, 3), F32)),
        in_specs=[vmem] * 3,
        out_specs=(hbm, hbm, hbm),
        scratch_shapes=[pltpu.SemaphoreType.DMA((3,))],
        name="store",
    )(*results)
    shape = (2, PLANES, 1, 1, CORE * CORE)
    return objects.reshape(shape), images.reshape(shape), factors.transpose(2, 0, 1)


def solution(mesh):
    placed = (
        P(None, None, "py", "px", None),
        P("py", "px", None, None, None),
        P("py", "px", None),
        P("py", "px"),
    )
    return jax.shard_map(
        body,
        mesh=mesh,
        in_specs=placed,
        out_specs=(P(None, None, "py", "px", None), P(None, None, "py", "px", None), P()),
        check_vma=False,
    )
```

```python
import functools
import math

import jax
import jax.numpy as jnp
import numpy as np
from jax import lax
from jax.experimental import pallas as pl
from jax.experimental.pallas import tpu as pltpu
from jax.sharding import PartitionSpec as P

PLANES = 2
PATCH = 128
KERNEL = 32
HALF = 8
CORE = 112
FLAT = 2 * PLANES * CORE * CORE // 128
TAP = KERNEL // 2 - 1
EPSILON = 1e-06
F32 = jnp.float32
BF16 = jnp.bfloat16


def tables():
    ids = np.arange(PATCH)
    angle = 2 * np.pi * (np.outer(ids, ids) % PATCH) / PATCH
    cos, sin = np.cos(angle), -np.sin(angle)
    forward = np.block([[cos, sin], [-sin, cos]])
    places = np.arange(64) - KERNEL // 2
    angle = 2 * np.pi * (np.outer(places, ids) % PATCH) / PATCH
    cos, sin = np.cos(angle), -np.sin(angle)
    taps_x = np.concatenate([cos, sin], axis=1)
    taps_y = np.block([[cos.T, -sin.T], [sin.T, cos.T]])
    return [jnp.asarray(t, BF16) for t in (forward, forward.T, taps_x, taps_y)]


def mm(left, right):
    return jnp.dot(left, right, preferred_element_type=F32)


def roll(values, shift):
    shift = shift % 128
    return values if shift == 0 else pltpu.roll(values, shift, 1)


def total(values):
    return jnp.sum(jnp.sum(values, axis=0, keepdims=True), axis=1, keepdims=True)


class Exchange:
    def __init__(self, index, ny, nx, height, rows, cols_out, cols_in, outs, ins, send, recv):
        self.height, self.rows, self.cols_out, self.cols_in = height, rows, cols_out, cols_in
        self.row_out, self.col_out, self.corner_out = (ref.at[index] for ref in outs)
        self.row_in, self.col_in, self.corner_in = (ref.at[index] for ref in ins)
        py, px = lax.axis_index("py"), lax.axis_index("px")
        up, down = lax.rem(py + ny - 1, ny), lax.rem(py + 1, ny)
        left, right = lax.rem(px + nx - 1, nx), lax.rem(px + 1, nx)
        has_up, has_down, has_left, has_right = py > 0, py < ny - 1, px > 0, px < nx - 1
        strip = pl.ds(0, 4 * height)
        top, bottom = (pl.ds(0, 16), pl.ds(16, 16)) if height == 16 else (pl.ds(0, 16), pl.ds(0, 16))
        plan = [
            (self.row_out.at[0, strip], self.row_in.at[1, strip], up, px, has_up),
            (self.row_out.at[1, strip], self.row_in.at[0, strip], down, px, has_down),
            (self.col_out.at[0, strip], self.col_in.at[1, strip], py, left, has_left),
            (self.col_out.at[1, strip], self.col_in.at[0, strip], py, right, has_right),
            (self.corner_out.at[top], self.corner_in.at[3], up, left, has_up & has_left),
            (self.corner_out.at[top], self.corner_in.at[2], up, right, has_up & has_right),
            (self.corner_out.at[bottom], self.corner_in.at[1], down, left, has_down & has_left),
            (self.corner_out.at[bottom], self.corner_in.at[0], down, right, has_down & has_right),
        ]
        self.copies = [
            pltpu.make_async_remote_copy(
                src_ref=source,
                dst_ref=target,
                send_sem=send.at[index, i],
                recv_sem=recv.at[index, i],
                device_id={"py": to_y, "px": to_x},
                device_id_type=pl.DeviceIdType.MESH,
            )
            for i, (source, target, to_y, to_x, _) in enumerate(plan)
        ]
        self.there = [there for *_, there in plan]
        self.back = [self.there[i] for i in (1, 0, 3, 2, 7, 6, 5, 4)]

    def begin(self, *which):
        for i in which:
            pl.when(self.there[i])(self.copies[i].start)

    def pack_columns(self, strip_of):
        for side, first in enumerate(self.cols_out):
            strips = [strip_of(m)[first : first + self.height] for m in range(2 * PLANES)]
            self.col_out[side, 0 : 4 * self.height, :] = jnp.concatenate(strips, axis=0).astype(BF16)

    def pack_rows(self, planes):
        height = self.height
        lane = lax.broadcasted_iota(jnp.int32, (height, 128), 1)
        ends = []
        for side, first in enumerate(self.rows):
            strips = [planes[m][first : first + height] for m in range(2 * PLANES)]
            self.row_out[side, 0 : 4 * height, :] = jnp.concatenate(strips, axis=0).astype(BF16)
            packed = roll(strips[0], 16)
            for m in range(1, 2 * PLANES):
                packed = jnp.where(lane >= 32 * m, roll(strips[m], 16 + 32 * m), packed)
            ends.append(packed)
        self.corner_out[0 : 2 * height, :] = jnp.concatenate(ends, axis=0).astype(BF16)

    def wait_recv(self):
        for copy, there in zip(self.copies, self.back):
            pl.when(there)(copy.wait_recv)

    def wait_send(self):
        for copy, there in zip(self.copies, self.there):
            pl.when(there)(copy.wait_send)

    def row_strips(self):
        height = self.height
        both = [self.row_in[side, 0 : 4 * height, :].astype(F32) for side in range(2)]
        return [[strips[m * height : (m + 1) * height] for m in range(2 * PLANES)] for strips in both]

    def sides(self):
        height = self.height
        both = [self.col_in[side, 0 : 4 * height, :].astype(F32) for side in range(2)]
        pieces = []
        for m in range(2 * PLANES):
            slots = [both[1][m * height : (m + 1) * height] for _ in range(32 // height)]
            slots[self.cols_in // height] = both[0][m * height : (m + 1) * height]
            pieces += slots
        columns = jnp.concatenate(pieces, axis=0).T
        lane = lax.broadcasted_iota(jnp.int32, (height, 128), 1)
        is_left = lax.rem(lane, 32) >= 16
        corner = [self.corner_in[i].astype(F32) for i in range(4)]
        if height == 8:
            corner = [corner[0][8:], corner[1][8:], corner[2][:8], corner[3][:8]]
        upper = jnp.where(is_left, roll(corner[0], 16), roll(corner[1], -16))
        lower = jnp.where(is_left, roll(corner[2], 16), roll(corner[3], -16))
        return columns, upper, lower


def normaliser(s00, s01, s11):
    tiny = F32(1e-30)
    q0 = lax.rsqrt(jnp.maximum(s00, tiny))
    cross = s01 * q0
    q1 = lax.rsqrt(jnp.maximum(s11 - cross * cross, s11 * F32(1e-6) + tiny))
    return (q0, cross, q1), (1.0 / q0, cross, 1.0 / q1)


def normalised(cells, scalars):
    q0, cross, q1 = scalars
    first = [cells[0][z] * q0 for z in range(PLANES)]
    second = [(cells[1][z] - cross * first[z]) * q1 for z in range(PLANES)]
    return first, second


def blur(cells, spectrum, forward_ref, backward_ref, adjoint, send_ends):
    half = PATCH
    table, turned = forward_ref[...], backward_ref[...]
    values = jnp.concatenate(
        [jnp.concatenate([cells[k][z].astype(BF16) for k in range(2)], axis=1) for z in range(PLANES)], axis=0
    )
    along_x = mm(values, table).astype(BF16)
    swapped = jnp.concatenate(
        [
            jnp.concatenate([along_x[z * half : (z + 1) * half, c * half : (c + 1) * half] for z in range(PLANES)], axis=1)
            for c in range(2)
        ],
        axis=0,
    )
    along_y = mm(turned, swapped)
    re = [along_y[:half, z * half : (z + 1) * half] for z in range(PLANES)]
    im = [along_y[half:, z * half : (z + 1) * half] for z in range(PLANES)]
    tap_re = [spectrum[:half, t * half : (t + 1) * half] for t in range(3)]
    tap_im = [spectrum[half:, t * half : (t + 1) * half] for t in range(3)]
    sign = -1.0 if adjoint else 1.0
    out_re, out_im = [], []
    for z_out in range(PLANES):
        sum_re = sum_im = None
        for z_in in range(PLANES):
            depth = 1 + (z_in - z_out) if adjoint else 1 - (z_in - z_out)
            a, b = tap_re[depth], sign * tap_im[depth]
            part_re = re[z_in] * a - im[z_in] * b
            part_im = re[z_in] * b + im[z_in] * a
            sum_re = part_re if sum_re is None else sum_re + part_re
            sum_im = part_im if sum_im is None else sum_im + part_im
        out_re.append(sum_re.astype(BF16))
        out_im.append(sum_im.astype(BF16))
    product = jnp.concatenate([jnp.concatenate(out_re, axis=1), jnp.concatenate(out_im, axis=1)], axis=0)
    back_y = mm(table, product).astype(BF16)
    swapped = jnp.concatenate(
        [
            jnp.concatenate([back_y[c * half : (c + 1) * half, z * half : (z + 1) * half] for c in range(2)], axis=1)
            for z in range(PLANES)
        ],
        axis=0,
    )
    ends = [table[at : at + 16] for k in range(2) for at in (k * half + half - 16, k * half)]
    ends = lax.dot_general(
        jnp.concatenate(ends, axis=0), swapped, (((1,), (1,)), ((), ())), preferred_element_type=F32
    )
    ends = [[ends[32 * k : 32 * (k + 1), z * half : (z + 1) * half] for z in range(PLANES)] for k in range(2)]
    send_ends(ends)
    back_x = mm(swapped, turned)
    return [[back_x[z * half : (z + 1) * half, k * half : (k + 1) * half] for z in range(PLANES)] for k in range(2)]


def restored(cells, factor):
    first = [factor[0] * cells[0][z] for z in range(PLANES)]
    second = [factor[2] * cells[1][z] + factor[1] * cells[0][z] for z in range(PLANES)]
    return first, second


def factor_of(g00, g01, g11):
    r00 = jnp.sqrt(jnp.maximum(g00, 0.0) + EPSILON)
    r01 = g01 / r00
    r11 = jnp.sqrt(jnp.maximum(g11 - r01 * r01, 0.0) + EPSILON)
    return r00, r01, r11


def kernel(
    ny, nx,
    measured_hbm, taps_hbm, offsets_hbm, mask_hbm, forward_hbm, backward_hbm, taps_x_hbm, taps_y_hbm,
    object_ref, image_ref, factors_ref,
    measured, offsets, taps, mask, forward_ref, backward_ref, taps_x, taps_y,
    spectrum_ref, planes, row_out, col_out, corner_out, row_in, col_in, corner_in,
    object_flat, forward_flat,
    one_out, one_in, two_out, two_in,
    load_sem, send_sem, recv_sem, sum_send, sum_recv,
):
    py, px = lax.axis_index("py"), lax.axis_index("px")
    row, high, column = px // 8, lax.rem(px // 4, 2), lax.rem(px, 4)
    place_one, place_two = high * ny + py, row * 4 + column

    def partner_one(step):
        at = lax.rem(place_one + step, 16)
        return {"py": lax.rem(at, ny), "px": row * 8 + (at // ny) * 4 + column}

    def partner_two(step):
        at = lax.rem(place_two + step, 16)
        return {"py": py, "px": (at // 4) * 8 + high * 4 + lax.rem(at, 4)}

    exchange = functools.partial(
        Exchange, ny=ny, nx=nx, outs=(row_out, col_out, corner_out), ins=(row_in, col_in, corner_in),
        send=send_sem, recv=recv_sem,
    )
    first = exchange(index=0, height=8, rows=(8, 112), cols_out=(24, 0), cols_in=16)
    second = exchange(index=1, height=16, rows=(0, 112), cols_out=(16, 0), cols_in=16)
    third = exchange(index=2, height=8, rows=(0, 120), cols_out=(16, 8), cols_in=24)
    barrier = pltpu.get_barrier_semaphore()
    has_up, has_down, has_left, has_right = py > 0, py < ny - 1, px > 0, px < nx - 1
    greeted = jnp.int32(30)
    for dx, has_x in ((nx - 1, has_left), (1, has_right), (0, None)):
        for dy, has_y in ((ny - 1, has_up), (1, has_down), (0, None)):
            if dx or dy:
                there = has_x if has_y is None else has_y if has_x is None else has_x & has_y
                to = {"py": lax.rem(py + dy, ny), "px": lax.rem(px + dx, nx)}
                greeted += there.astype(jnp.int32)

                @pl.when(there)
                def _(to=to):
                    pl.semaphore_signal(barrier, inc=1, device_id=to, device_id_type=pl.DeviceIdType.MESH)

    loads = [
        pltpu.make_async_copy(source, target, load_sem.at[i])
        for i, (source, target) in enumerate(
            [
                (measured_hbm, measured),
                (taps_hbm.at[0, 0, pl.ds(TAP, 3)], taps),
                (taps_x_hbm, taps_x),
                (taps_y_hbm, taps_y),
                (offsets_hbm, offsets),
                (mask_hbm, mask),
                (forward_hbm, forward_ref),
                (backward_hbm, backward_ref),
            ]
        )
    ]
    for load in loads:
        load.start()

    for step in range(1, 16):
        for to in (partner_one(step), partner_two(step)):
            pl.semaphore_signal(barrier, inc=1, device_id=to, device_id_type=pl.DeviceIdType.MESH)

    lane = lax.broadcasted_iota(jnp.int32, (PATCH, 128), 1)
    line = lax.broadcasted_iota(jnp.int32, (PATCH, 128), 0)
    owned_lane = (lane >= HALF) & (lane < PATCH - HALF)
    low_y, high_y = jnp.where(has_up, 0, HALF), jnp.where(has_down, PATCH, PATCH - HALF)
    low_x, high_x = jnp.where(has_left, 0, HALF), jnp.where(has_right, PATCH, PATCH - HALF)
    inside = (line >= low_y) & (line < high_y) & (lane >= low_x) & (lane < high_x)

    loads[0].wait()
    lane14 = lax.broadcasted_iota(jnp.int32, (14, 128), 1)
    for m in range(4):
        planes[0, m, 0:HALF, :] = jnp.zeros((HALF, 128), F32)
        planes[0, m, PATCH - HALF : PATCH, :] = jnp.zeros((HALF, 128), F32)
        for k in range(8):
            if k < 7:
                high_part = measured[pl.ds(98 * m + k, 14, stride=7), :]
            if k == 0:
                both = high_part
            elif k == 7:
                both = measured[pl.ds(98 * m + 6, 14, stride=7), :]
            else:
                low_part = measured[pl.ds(98 * m + k - 1, 14, stride=7), :]
                both = jnp.where(lane14 >= 128 - 16 * k, low_part, high_part)
            planes[0, m, pl.ds(HALF + k, 14, stride=8), :] = roll(both, 16 * k + HALF)

    measured_planes = [planes[0, m] for m in range(4)]
    packed = roll(measured_planes[0], 16)
    for m in range(1, 4):
        packed = jnp.where(lane >= 32 * m, roll(measured_planes[m], 16 + 32 * m), packed)
    packed = packed.T
    first.pack_columns(lambda m: packed[32 * m : 32 * (m + 1)])
    first.pack_rows(measured_planes)
    pl.semaphore_wait(barrier, greeted)
    first.begin(4, 5, 6, 7, 2, 3, 0, 1)

    for load in loads[1:5]:
        load.wait()
    shift_y, shift_x = offsets[0, 0, 0], offsets[0, 0, 1]
    pick_x = (
        lax.broadcasted_iota(jnp.int32, (KERNEL, 64), 1) == lax.broadcasted_iota(jnp.int32, (KERNEL, 64), 0) + shift_x
    )
    pick_y = (
        lax.broadcasted_iota(jnp.int32, (64, KERNEL), 0) == lax.broadcasted_iota(jnp.int32, (64, KERNEL), 1) + shift_y
    )
    pick_x = jnp.where(pick_x, 1.0, 0.0).astype(BF16)
    pick_y = jnp.where(pick_y, 1.0, 0.0).astype(BF16)
    placed = mm(taps[...].reshape(3 * KERNEL, KERNEL), pick_x).astype(BF16)
    kx = mm(placed, taps_x[...]).astype(BF16)
    side_by_side = jnp.concatenate([kx[t * KERNEL : (t + 1) * KERNEL] for t in range(3)], axis=1)
    kx = mm(pick_y, side_by_side).astype(BF16)
    kx = jnp.concatenate(
        [
            jnp.concatenate([kx[:, t * 256 + c * 128 : t * 256 + (c + 1) * 128] for t in range(3)], axis=1)
            for c in range(2)
        ],
        axis=0,
    )
    spectrum_ref[...] = mm(taps_y[...], kx) * F32(1.0 / (PATCH * PATCH))

    for load in loads[5:]:
        load.wait()
    weight = mask[...].astype(F32)
    weight_ends = weight.T
    weight_ends = jnp.concatenate([weight_ends[PATCH - 16 :], weight_ends[:16]], axis=0)

    def tile(left, right):
        return jnp.sum((left * right).reshape(-1, 8, 128), axis=0)

    owned = slice(HALF, PATCH - HALF)
    owned_core = owned_lane[owned]
    own_m = [[jnp.where(owned_core, planes[0, 2 * k + z, owned, :], 0.0) for z in range(PLANES)] for k in range(2)]

    def grams(left, right, pairs):
        return [sum(tile(left[i][z], right[j][z]) for z in range(PLANES)) for i, j in pairs]

    sums = grams(own_m, own_m, ((0, 0), (0, 1), (1, 1)))

    def scalars_of(tiles):
        return normaliser(*(total(values) for values in tiles))

    scalars, factor = scalars_of(sums)
    first.wait_recv()
    columns, upper, lower = first.sides()
    up_rows, down_rows = first.row_strips()
    columns = jnp.concatenate([upper, columns[owned], lower], axis=0)
    window = [[None, None], [None, None]]
    for m in range(4):
        centre = jnp.concatenate([up_rows[m], planes[0, m, owned, :], down_rows[m]], axis=0)
        cells = jnp.where(owned_lane, centre, roll(columns, -16 - 32 * m))
        window[m // 2][m % 2] = jnp.where(inside, cells, 0.0)
    def send_second(ends):
        ends = restored(ends, factor)
        second.pack_columns(lambda m: ends[m // 2][m % 2] * weight_ends)
        second.begin(2, 3)

    unit = normalised(window, scalars)
    result = restored(blur(unit, spectrum_ref[...], forward_ref, backward_ref, True, send_second), factor)
    result = [result[m // 2][m % 2] * weight for m in range(4)]
    second.pack_rows(result)
    second.begin(4, 5, 6, 7, 0, 1)
    for m in range(4):
        planes[1, m] = result[m]
    pairs = ((0, 0), (0, 1), (1, 1))
    scalars, next_factor = scalars_of(grams((result[:2], result[2:]), (result[:2], result[2:]), pairs))

    second.wait_recv()
    columns, upper, lower = second.sides()
    up_rows, down_rows = second.row_strips()
    upper, lower = jnp.where(has_up, upper, 0.0), jnp.where(has_down, lower, 0.0)
    columns = jnp.concatenate([columns[:16] + upper, columns[16:112], columns[112:] + lower], axis=0)
    edge_lane = ((lane < 16) & has_left) | ((lane >= 112) & has_right)
    window = [[None, None], [None, None]]
    keep = jnp.where(inside, weight, 0.0)
    for m in range(4):
        cells = planes[1, m]
        above, below = jnp.where(has_up, up_rows[m], 0.0), jnp.where(has_down, down_rows[m], 0.0)
        cells = jnp.concatenate([cells[:16] + above, cells[16:112], cells[112:] + below], axis=0)
        cells = cells + jnp.where(edge_lane, roll(columns, -16 - 32 * m), 0.0)
        planes[1, m] = cells
        window[m // 2][m % 2] = cells * keep
    def send_third(ends):
        ends = restored(ends, next_factor)
        third.pack_columns(lambda m: ends[m // 2][m % 2])
        third.begin(2, 3)

    unit = normalised(window, scalars)
    result = restored(blur(unit, spectrum_ref[...], forward_ref, backward_ref, False, send_third), next_factor)
    result = [result[m // 2][m % 2] for m in range(4)]
    third.pack_rows(result)
    third.begin(4, 5, 6, 7, 0, 1)
    for m in range(4):
        planes[2, m] = result[m]
    own_v = [[jnp.where(owned_core, planes[1, 2 * k + z, owned, :], 0.0) for z in range(PLANES)] for k in range(2)]
    sums += grams(own_v, own_v, pairs)

    def to_flat(source, target):
        for m in range(4):
            for j in range(7):
                head = roll(source(m, pl.ds(HALF + j, 14, stride=8)), -16 * j - HALF)
                tail = roll(source(m, pl.ds(HALF + j + 1, 14, stride=8)), 104 - 16 * j)
                target[pl.ds(98 * m + j, 14, stride=7), :] = jnp.where(lane14 < 112 - 16 * j, head, tail)

    to_flat(lambda m, rows: planes[1, m, rows, :], object_flat)

    third.wait_recv()
    columns, upper, lower = third.sides()
    upper, lower = jnp.where(has_up, upper, 0.0), jnp.where(has_down, lower, 0.0)
    columns = jnp.concatenate([columns[:8], columns[8:16] + upper, columns[16:112], columns[112:120] + lower, columns[120:]], axis=0)
    up_rows, down_rows = third.row_strips()
    edge_lane = ((lane >= 8) & (lane < 16) & has_left) | ((lane >= 112) & (lane < 120) & has_right)
    own_f = [[None, None], [None, None]]
    for m in range(4):
        cells = planes[2, m]
        above, below = jnp.where(has_up, up_rows[m], 0.0), jnp.where(has_down, down_rows[m], 0.0)
        cells = jnp.concatenate([cells[8:16] + above, cells[16:112], cells[112:120] + below], axis=0)
        cells = cells + jnp.where(edge_lane[owned], roll(columns[owned], -16 - 32 * m), 0.0)
        cells = jnp.where(owned_core, cells, 0.0)
        planes[2, m, owned, :] = cells
        own_f[m // 2][m % 2] = cells
    sums += grams(own_f, own_f, ((0, 0), (0, 1), (1, 1)))
    sums += grams(own_f, own_m, ((0, 0), (0, 1), (1, 0), (1, 1)))

    line16 = lax.broadcasted_iota(jnp.int32, (16, 128), 0)
    lane16 = lax.broadcasted_iota(jnp.int32, (16, 128), 1)
    stacked = jnp.zeros((16, 128), F32)
    for q, values in enumerate(sums):
        stacked = jnp.where(line16 == q, jnp.sum(values, axis=0, keepdims=True), stacked)
    stacked = jnp.sum(stacked, axis=1, keepdims=True)
    mine = jnp.sum(jnp.where(line16 == lane16, stacked, 0.0), axis=0, keepdims=True)

    def all_sum(mine, out_ref, in_ref, place, partner, stage):
        out_ref[...] = mine
        in_ref[place] = mine
        copies = [
            pltpu.make_async_remote_copy(
                src_ref=out_ref,
                dst_ref=in_ref.at[place],
                send_sem=sum_send.at[stage, step],
                recv_sem=sum_recv.at[stage, step],
                device_id=partner(step),
                device_id_type=pl.DeviceIdType.MESH,
            )
            for step in range(1, 16)
        ]
        for copy in copies:
            copy.start()
        return copies

    copies = all_sum(mine, one_out, one_in, place_one, partner_one, 0)
    to_flat(lambda m, rows: planes[2, m, rows, :], forward_flat)
    for copy in copies:
        copy.wait_recv()
    mine = jnp.sum(one_in[...], axis=0)
    sent = copies
    copies = all_sum(mine, two_out, two_in, place_two, partner_two, 1)
    for phase in (first, second, third):
        phase.wait_send()
    for copy in sent:
        copy.wait_send()
    for copy in copies:
        copy.wait()
    cells_total = PLANES * CORE * CORE * ny * nx
    gathered = jnp.sum(two_in[...], axis=0) * F32(1.0 / cells_total)
    lane1 = lax.broadcasted_iota(jnp.int32, (1, 128), 1)
    m00, m01, m11, v00, v01, v11, f00, f01, f11, p00, p01, p10, p11 = [
        jnp.sum(jnp.where(lane1 == q, gathered, 0.0), axis=1, keepdims=True) for q in range(13)
    ]
    a, b, c = factor_of(m00, m01, m11)
    u00, u11 = 1.0 / a, 1.0 / c
    u01 = -b * u00 * u11
    w00 = u00 * u00 * v00
    w01 = u00 * (u01 * v00 + u11 * v01)
    w11 = u01 * u01 * v00 + 2.0 * u01 * u11 * v01 + u11 * u11 * v11
    alpha, beta, gamma = factor_of(w00, w01, w11)
    t00 = u00 / alpha
    t11 = u11 / gamma
    t01 = (u01 - beta * t00) / gamma
    x0, x1 = alpha * u00 + beta * u01, beta * u11
    y0, y1 = gamma * u01, gamma * u11

    def form(l, r):
        return (
            l[0] * (r[0] * f00 + r[1] * f01 - r[2] * p00 - r[3] * p01)
            + l[1] * (r[0] * f01 + r[1] * f11 - r[2] * p10 - r[3] * p11)
            - l[2] * (r[0] * p00 + r[1] * p10 - r[2] * m00 - r[3] * m01)
            - l[3] * (r[0] * p01 + r[1] * p11 - r[2] * m01 - r[3] * m11)
        )

    zero = jnp.zeros_like(a)
    z_first, z_second = (t00, zero, x0, x1), (t01, t11, y0, y1)
    rho, sigma, tau = factor_of(form(z_first, z_first), form(z_first, z_second), form(z_second, z_second))
    i0 = [value / rho for value in z_first]
    i1 = [(value - sigma * lead) / tau for value, lead in zip(z_second, i0)]

    half = FLAT // 2
    one, two = slice(0, half), slice(half, FLAT)
    v_one, v_two = object_flat[one, :], object_flat[two, :]
    f_one, f_two = forward_flat[one, :], forward_flat[two, :]
    m_one, m_two = measured[one, :], measured[two, :]
    object_ref[one, :] = t00 * v_one
    object_ref[two, :] = t01 * v_one + t11 * v_two
    image_ref[one, :] = i0[0] * f_one - i0[2] * m_one - i0[3] * m_two
    image_ref[two, :] = i1[0] * f_one + i1[1] * f_two - i1[2] * m_one - i1[3] * m_two
    down = lax.broadcasted_iota(jnp.int32, (2, 2, 3), 0)
    across = lax.broadcasted_iota(jnp.int32, (2, 2, 3), 1)
    which = lax.broadcasted_iota(jnp.int32, (2, 2, 3), 2)
    factors = jnp.zeros((2, 2, 3), F32)
    for i, triple in enumerate(((a, b, c), (alpha, beta, gamma), (rho, sigma, tau))):
        for (r, k), value in zip(((0, 0), (0, 1), (1, 1)), triple):
            here = (which == i) & (down == r) & (across == k)
            factors = jnp.where(here, value.reshape(1, 1, 1), factors)
    factors_ref[...] = factors


def store(object_vmem, image_vmem, factors_vmem, object_hbm, image_hbm, factors_hbm, sem):
    copies = [
        pltpu.make_async_copy(source, target, sem.at[i])
        for i, (source, target) in enumerate(
            ((object_vmem, object_hbm), (image_vmem, image_hbm), (factors_vmem, factors_hbm))
        )
    ]
    for copy in copies:
        copy.start()
    for copy in copies:
        copy.wait()


def body(measured, psf_taps, offsets, window_mask):
    ny, nx = lax.axis_size("py"), lax.axis_size("px")
    hbm = pl.BlockSpec(memory_space=pltpu.HBM)
    vmem = pl.BlockSpec(memory_space=pltpu.VMEM)
    operands = [measured.reshape(FLAT, 128), psf_taps, offsets, window_mask, *tables()]
    operands = [pltpu.with_memory_space_constraint(operand, pltpu.HBM) for operand in operands]
    results = pl.pallas_call(
        functools.partial(kernel, ny, nx),
        out_shape=(pltpu.VMEM((FLAT, 128), F32), pltpu.VMEM((FLAT, 128), F32), pltpu.VMEM((2, 2, 3), F32)),
        in_specs=[hbm] * 8,
        out_specs=(vmem, vmem, vmem),
        scratch_shapes=[
            pltpu.VMEM((FLAT, 128), F32),
            pltpu.SMEM((1, 1, 2), jnp.int32),
            pltpu.VMEM((3, KERNEL, KERNEL), BF16),
            pltpu.VMEM((PATCH, PATCH), jnp.int32),
            pltpu.VMEM((256, 256), BF16),
            pltpu.VMEM((256, 256), BF16),
            pltpu.VMEM((64, 256), BF16),
            pltpu.VMEM((256, 128), BF16),
            pltpu.VMEM((256, 384), F32),
            pltpu.VMEM((3, 4, PATCH, 128), F32),
            pltpu.VMEM((3, 2, 64, 128), BF16),
            pltpu.VMEM((3, 2, 64, 128), BF16),
            pltpu.VMEM((3, 32, 128), BF16),
            pltpu.VMEM((3, 2, 64, 128), BF16),
            pltpu.VMEM((3, 2, 64, 128), BF16),
            pltpu.VMEM((3, 4, 16, 128), BF16),
            pltpu.VMEM((FLAT, 128), F32),
            pltpu.VMEM((FLAT, 128), F32),
            pltpu.VMEM((1, 128), F32),
            pltpu.VMEM((16, 1, 128), F32),
            pltpu.VMEM((1, 128), F32),
            pltpu.VMEM((16, 1, 128), F32),
            pltpu.SemaphoreType.DMA((8,)),
            pltpu.SemaphoreType.DMA((3, 8)),
            pltpu.SemaphoreType.DMA((3, 8)),
            pltpu.SemaphoreType.DMA((2, 16)),
            pltpu.SemaphoreType.DMA((2, 16)),
        ],
        compiler_params=pltpu.CompilerParams(
            collective_id=0, has_side_effects=True, vmem_limit_bytes=48 * 1024 * 1024
        ),
        name="step",
    )(*operands)
    results = [pltpu.with_memory_space_constraint(result, pltpu.VMEM) for result in results]
    objects, images, factors = pl.pallas_call(
        store,
        out_shape=(pltpu.HBM((FLAT, 128), F32), pltpu.HBM((FLAT, 128), F32), pltpu.HBM((2, 2, 3), F32)),
        in_specs=[vmem] * 3,
        out_specs=(hbm, hbm, hbm),
        scratch_shapes=[pltpu.SemaphoreType.DMA((3,))],
        name="store",
    )(*results)
    shape = (2, PLANES, 1, 1, CORE * CORE)
    return objects.reshape(shape), images.reshape(shape), factors.transpose(2, 0, 1)


def solution(mesh):
    placed = (
        P(None, None, "py", "px", None),
        P("py", "px", None, None, None),
        P("py", "px", None),
        P("py", "px"),
    )
    return jax.shard_map(
        body,
        mesh=mesh,
        in_specs=placed,
        out_specs=(P(None, None, "py", "px", None), P(None, None, "py", "px", None), P()),
        check_vma=False,
    )
```

```python
import functools
import math

import jax
import jax.numpy as jnp
import numpy as np
from jax import lax
from jax.experimental import pallas as pl
from jax.experimental.pallas import tpu as pltpu
from jax.sharding import PartitionSpec as P

PLANES = 2
PATCH = 128
KERNEL = 32
HALF = 8
CORE = 112
FLAT = 2 * PLANES * CORE * CORE // 128
TAP = KERNEL // 2 - 1
EPSILON = 1e-06
F32 = jnp.float32
BF16 = jnp.bfloat16


def tables():
    ids = np.arange(PATCH)
    angle = 2 * np.pi * (np.outer(ids, ids) % PATCH) / PATCH
    cos, sin = np.cos(angle), -np.sin(angle)
    forward = np.block([[cos, sin], [-sin, cos]])
    places = np.arange(64) - KERNEL // 2
    angle = 2 * np.pi * (np.outer(places, ids) % PATCH) / PATCH
    cos, sin = np.cos(angle), -np.sin(angle)
    taps_x = np.concatenate([cos, sin], axis=1)
    taps_y = np.block([[cos.T, -sin.T], [sin.T, cos.T]])
    return [jnp.asarray(t, BF16) for t in (forward, forward.T, taps_x, taps_y)]


def mm(left, right):
    return jnp.dot(left, right, preferred_element_type=F32)


def roll(values, shift):
    shift = shift % 128
    return values if shift == 0 else pltpu.roll(values, shift, 1)


def total(values):
    return jnp.sum(jnp.sum(values, axis=0, keepdims=True), axis=1, keepdims=True)


class Exchange:
    def __init__(self, index, ny, nx, height, rows, cols_out, cols_in, outs, ins, send, recv):
        self.height, self.rows, self.cols_out, self.cols_in = height, rows, cols_out, cols_in
        self.row_out, self.col_out, self.corner_out = (ref.at[index] for ref in outs)
        self.row_in, self.col_in, self.corner_in = (ref.at[index] for ref in ins)
        py, px = lax.axis_index("py"), lax.axis_index("px")
        up, down = lax.rem(py + ny - 1, ny), lax.rem(py + 1, ny)
        left, right = lax.rem(px + nx - 1, nx), lax.rem(px + 1, nx)
        has_up, has_down, has_left, has_right = py > 0, py < ny - 1, px > 0, px < nx - 1
        strip = pl.ds(0, 4 * height)
        top, bottom = (pl.ds(0, 16), pl.ds(16, 16)) if height == 16 else (pl.ds(0, 16), pl.ds(0, 16))
        plan = [
            (self.row_out.at[0, strip], self.row_in.at[1, strip], up, px, has_up),
            (self.row_out.at[1, strip], self.row_in.at[0, strip], down, px, has_down),
            (self.col_out.at[0, strip], self.col_in.at[1, strip], py, left, has_left),
            (self.col_out.at[1, strip], self.col_in.at[0, strip], py, right, has_right),
            (self.corner_out.at[top], self.corner_in.at[3], up, left, has_up & has_left),
            (self.corner_out.at[top], self.corner_in.at[2], up, right, has_up & has_right),
            (self.corner_out.at[bottom], self.corner_in.at[1], down, left, has_down & has_left),
            (self.corner_out.at[bottom], self.corner_in.at[0], down, right, has_down & has_right),
        ]
        self.copies = [
            pltpu.make_async_remote_copy(
                src_ref=source,
                dst_ref=target,
                send_sem=send.at[index, i],
                recv_sem=recv.at[index, i],
                device_id={"py": to_y, "px": to_x},
                device_id_type=pl.DeviceIdType.MESH,
            )
            for i, (source, target, to_y, to_x, _) in enumerate(plan)
        ]
        self.there = [there for *_, there in plan]
        self.back = [self.there[i] for i in (1, 0, 3, 2, 7, 6, 5, 4)]

    def begin(self, *which):
        for i in which:
            pl.when(self.there[i])(self.copies[i].start)

    def pack_columns(self, strip_of):
        for side, first in enumerate(self.cols_out):
            strips = [strip_of(m)[first : first + self.height] for m in range(2 * PLANES)]
            self.col_out[side, 0 : 4 * self.height, :] = jnp.concatenate(strips, axis=0).astype(BF16)

    def pack_rows(self, planes):
        height = self.height
        lane = lax.broadcasted_iota(jnp.int32, (height, 128), 1)
        ends = []
        for side, first in enumerate(self.rows):
            strips = [planes[m][first : first + height] for m in range(2 * PLANES)]
            self.row_out[side, 0 : 4 * height, :] = jnp.concatenate(strips, axis=0).astype(BF16)
            packed = roll(strips[0], 16)
            for m in range(1, 2 * PLANES):
                packed = jnp.where(lane >= 32 * m, roll(strips[m], 16 + 32 * m), packed)
            ends.append(packed)
        self.corner_out[0 : 2 * height, :] = jnp.concatenate(ends, axis=0).astype(BF16)

    def wait_recv(self):
        for copy, there in zip(self.copies, self.back):
            pl.when(there)(copy.wait_recv)

    def wait_send(self):
        for copy, there in zip(self.copies, self.there):
            pl.when(there)(copy.wait_send)

    def row_strips(self):
        height = self.height
        both = [self.row_in[side, 0 : 4 * height, :].astype(F32) for side in range(2)]
        return [[strips[m * height : (m + 1) * height] for m in range(2 * PLANES)] for strips in both]

    def sides(self):
        height = self.height
        both = [self.col_in[side, 0 : 4 * height, :].astype(F32) for side in range(2)]
        pieces = []
        for m in range(2 * PLANES):
            slots = [both[1][m * height : (m + 1) * height] for _ in range(32 // height)]
            slots[self.cols_in // height] = both[0][m * height : (m + 1) * height]
            pieces += slots
        columns = jnp.concatenate(pieces, axis=0).T
        lane = lax.broadcasted_iota(jnp.int32, (height, 128), 1)
        is_left = lax.rem(lane, 32) >= 16
        corner = [self.corner_in[i].astype(F32) for i in range(4)]
        if height == 8:
            corner = [corner[0][8:], corner[1][8:], corner[2][:8], corner[3][:8]]
        upper = jnp.where(is_left, roll(corner[0], 16), roll(corner[1], -16))
        lower = jnp.where(is_left, roll(corner[2], 16), roll(corner[3], -16))
        return columns, upper, lower


def normaliser(s00, s01, s11):
    tiny = F32(1e-30)
    q0 = lax.rsqrt(jnp.maximum(s00, tiny))
    cross = s01 * q0
    q1 = lax.rsqrt(jnp.maximum(s11 - cross * cross, s11 * F32(1e-6) + tiny))
    return (q0, cross, q1), (1.0 / q0, cross, 1.0 / q1)


def normalised(cells, scalars):
    q0, cross, q1 = scalars
    first = [cells[0][z] * q0 for z in range(PLANES)]
    second = [(cells[1][z] - cross * first[z]) * q1 for z in range(PLANES)]
    return first, second


def blur(cells, spectrum, forward_ref, backward_ref, adjoint, send_ends):
    half = PATCH
    table, turned = forward_ref[...], backward_ref[...]
    values = jnp.concatenate(
        [jnp.concatenate([cells[k][z].astype(BF16) for k in range(2)], axis=1) for z in range(PLANES)], axis=0
    )
    along_x = mm(values, table).astype(BF16)
    swapped = jnp.concatenate(
        [
            jnp.concatenate([along_x[z * half : (z + 1) * half, c * half : (c + 1) * half] for z in range(PLANES)], axis=1)
            for c in range(2)
        ],
        axis=0,
    )
    along_y = mm(turned, swapped)
    re = [along_y[:half, z * half : (z + 1) * half] for z in range(PLANES)]
    im = [along_y[half:, z * half : (z + 1) * half] for z in range(PLANES)]
    tap_re = [spectrum[:half, t * half : (t + 1) * half] for t in range(3)]
    tap_im = [spectrum[half:, t * half : (t + 1) * half] for t in range(3)]
    sign = -1.0 if adjoint else 1.0
    out_re, out_im = [], []
    for z_out in range(PLANES):
        sum_re = sum_im = None
        for z_in in range(PLANES):
            depth = 1 + (z_in - z_out) if adjoint else 1 - (z_in - z_out)
            a, b = tap_re[depth], sign * tap_im[depth]
            part_re = re[z_in] * a - im[z_in] * b
            part_im = re[z_in] * b + im[z_in] * a
            sum_re = part_re if sum_re is None else sum_re + part_re
            sum_im = part_im if sum_im is None else sum_im + part_im
        out_re.append(sum_re.astype(BF16))
        out_im.append(sum_im.astype(BF16))
    product = jnp.concatenate([jnp.concatenate(out_re, axis=1), jnp.concatenate(out_im, axis=1)], axis=0)
    back_y = mm(table, product).astype(BF16)
    swapped = jnp.concatenate(
        [
            jnp.concatenate([back_y[c * half : (c + 1) * half, z * half : (z + 1) * half] for c in range(2)], axis=1)
            for z in range(PLANES)
        ],
        axis=0,
    )
    ends = [table[at : at + 16] for k in range(2) for at in (k * half + half - 16, k * half)]
    ends = lax.dot_general(
        jnp.concatenate(ends, axis=0), swapped, (((1,), (1,)), ((), ())), preferred_element_type=F32
    )
    ends = [[ends[32 * k : 32 * (k + 1), z * half : (z + 1) * half] for z in range(PLANES)] for k in range(2)]
    send_ends(ends)
    back_x = mm(swapped, turned)
    return [[back_x[z * half : (z + 1) * half, k * half : (k + 1) * half] for z in range(PLANES)] for k in range(2)]


def restored(cells, factor):
    first = [factor[0] * cells[0][z] for z in range(PLANES)]
    second = [factor[2] * cells[1][z] + factor[1] * cells[0][z] for z in range(PLANES)]
    return first, second


def factor_of(g00, g01, g11):
    s00 = jnp.maximum(g00, 0.0) + EPSILON
    i00 = lax.rsqrt(s00)
    r01 = g01 * i00
    s11 = jnp.maximum(g11 - r01 * r01, 0.0) + EPSILON
    i11 = lax.rsqrt(s11)
    return (s00 * i00, r01, s11 * i11), (i00, i11)


def kernel(
    ny, nx,
    measured_hbm, taps_hbm, offsets_hbm, mask_hbm, forward_hbm, backward_hbm, taps_x_hbm, taps_y_hbm,
    object_ref, image_ref, factors_ref,
    measured, offsets, taps, mask, forward_ref, backward_ref, taps_x, taps_y,
    spectrum_ref, planes, row_out, col_out, corner_out, row_in, col_in, corner_in,
    object_flat, forward_flat,
    one_out, one_in, two_out, two_in,
    load_sem, send_sem, recv_sem, sum_send, sum_recv,
):
    py, px = lax.axis_index("py"), lax.axis_index("px")
    row, high, column = px // 8, lax.rem(px // 4, 2), lax.rem(px, 4)
    place_one, place_two = high * ny + py, row * 4 + column

    def partner_one(step):
        at = lax.rem(place_one + step, 16)
        return {"py": lax.rem(at, ny), "px": row * 8 + (at // ny) * 4 + column}

    def partner_two(step):
        at = lax.rem(place_two + step, 16)
        return {"py": py, "px": (at // 4) * 8 + high * 4 + lax.rem(at, 4)}

    exchange = functools.partial(
        Exchange, ny=ny, nx=nx, outs=(row_out, col_out, corner_out), ins=(row_in, col_in, corner_in),
        send=send_sem, recv=recv_sem,
    )
    first = exchange(index=0, height=8, rows=(8, 112), cols_out=(24, 0), cols_in=16)
    second = exchange(index=1, height=16, rows=(0, 112), cols_out=(16, 0), cols_in=16)
    third = exchange(index=2, height=8, rows=(0, 120), cols_out=(16, 8), cols_in=24)
    barrier = pltpu.get_barrier_semaphore()
    has_up, has_down, has_left, has_right = py > 0, py < ny - 1, px > 0, px < nx - 1
    greeted = jnp.int32(30)
    for dx, has_x in ((nx - 1, has_left), (1, has_right), (0, None)):
        for dy, has_y in ((ny - 1, has_up), (1, has_down), (0, None)):
            if dx or dy:
                there = has_x if has_y is None else has_y if has_x is None else has_x & has_y
                to = {"py": lax.rem(py + dy, ny), "px": lax.rem(px + dx, nx)}
                greeted += there.astype(jnp.int32)

                @pl.when(there)
                def _(to=to):
                    pl.semaphore_signal(barrier, inc=1, device_id=to, device_id_type=pl.DeviceIdType.MESH)

    loads = [
        pltpu.make_async_copy(source, target, load_sem.at[i])
        for i, (source, target) in enumerate(
            [
                (measured_hbm, measured),
                (taps_hbm.at[0, 0, pl.ds(TAP, 3)], taps),
                (taps_x_hbm, taps_x),
                (taps_y_hbm, taps_y),
                (offsets_hbm, offsets),
                (mask_hbm, mask),
                (forward_hbm, forward_ref),
                (backward_hbm, backward_ref),
            ]
        )
    ]
    for load in loads:
        load.start()

    for step in range(1, 16):
        for to in (partner_one(step), partner_two(step)):
            pl.semaphore_signal(barrier, inc=1, device_id=to, device_id_type=pl.DeviceIdType.MESH)

    lane = lax.broadcasted_iota(jnp.int32, (PATCH, 128), 1)
    line = lax.broadcasted_iota(jnp.int32, (PATCH, 128), 0)
    owned_lane = (lane >= HALF) & (lane < PATCH - HALF)
    low_y, high_y = jnp.where(has_up, 0, HALF), jnp.where(has_down, PATCH, PATCH - HALF)
    low_x, high_x = jnp.where(has_left, 0, HALF), jnp.where(has_right, PATCH, PATCH - HALF)
    inside = (line >= low_y) & (line < high_y) & (lane >= low_x) & (lane < high_x)

    loads[0].wait()
    lane14 = lax.broadcasted_iota(jnp.int32, (14, 128), 1)
    for m in range(4):
        planes[0, m, 0:HALF, :] = jnp.zeros((HALF, 128), F32)
        planes[0, m, PATCH - HALF : PATCH, :] = jnp.zeros((HALF, 128), F32)
        for k in range(8):
            if k < 7:
                high_part = measured[pl.ds(98 * m + k, 14, stride=7), :]
            if k == 0:
                both = high_part
            elif k == 7:
                both = measured[pl.ds(98 * m + 6, 14, stride=7), :]
            else:
                low_part = measured[pl.ds(98 * m + k - 1, 14, stride=7), :]
                both = jnp.where(lane14 >= 128 - 16 * k, low_part, high_part)
            planes[0, m, pl.ds(HALF + k, 14, stride=8), :] = roll(both, 16 * k + HALF)

    measured_planes = [planes[0, m] for m in range(4)]
    packed = roll(measured_planes[0], 16)
    for m in range(1, 4):
        packed = jnp.where(lane >= 32 * m, roll(measured_planes[m], 16 + 32 * m), packed)
    packed = packed.T
    first.pack_columns(lambda m: packed[32 * m : 32 * (m + 1)])
    first.pack_rows(measured_planes)
    pl.semaphore_wait(barrier, greeted)
    first.begin(2, 3, 4, 5, 6, 7, 0, 1)

    for load in loads[1:5]:
        load.wait()
    shift_y, shift_x = offsets[0, 0, 0], offsets[0, 0, 1]
    pick_x = (
        lax.broadcasted_iota(jnp.int32, (KERNEL, 64), 1) == lax.broadcasted_iota(jnp.int32, (KERNEL, 64), 0) + shift_x
    )
    pick_y = (
        lax.broadcasted_iota(jnp.int32, (64, KERNEL), 0) == lax.broadcasted_iota(jnp.int32, (64, KERNEL), 1) + shift_y
    )
    pick_x = jnp.where(pick_x, 1.0, 0.0).astype(BF16)
    pick_y = jnp.where(pick_y, 1.0, 0.0).astype(BF16)
    placed = mm(taps[...].reshape(3 * KERNEL, KERNEL), pick_x).astype(BF16)
    kx = mm(placed, taps_x[...]).astype(BF16)
    side_by_side = jnp.concatenate([kx[t * KERNEL : (t + 1) * KERNEL] for t in range(3)], axis=1)
    kx = mm(pick_y, side_by_side).astype(BF16)
    kx = jnp.concatenate(
        [
            jnp.concatenate([kx[:, t * 256 + c * 128 : t * 256 + (c + 1) * 128] for t in range(3)], axis=1)
            for c in range(2)
        ],
        axis=0,
    )
    spectrum_ref[...] = mm(taps_y[...], kx) * F32(1.0 / (PATCH * PATCH))

    for load in loads[5:]:
        load.wait()
    weight = mask[...].astype(F32)
    weight_ends = weight.T
    weight_ends = jnp.concatenate([weight_ends[PATCH - 16 :], weight_ends[:16]], axis=0)

    def tile(left, right):
        return jnp.sum((left * right).reshape(-1, 8, 128), axis=0)

    owned = slice(HALF, PATCH - HALF)
    owned_core = owned_lane[owned]
    own_m = [[jnp.where(owned_core, planes[0, 2 * k + z, owned, :], 0.0) for z in range(PLANES)] for k in range(2)]

    def grams(left, right, pairs):
        return [sum(tile(left[i][z], right[j][z]) for z in range(PLANES)) for i, j in pairs]

    sums = grams(own_m, own_m, ((0, 0), (0, 1), (1, 1)))

    def scalars_of(tiles):
        return normaliser(*(total(values) for values in tiles))

    scalars, factor = scalars_of(sums)
    first.wait_recv()
    columns, upper, lower = first.sides()
    up_rows, down_rows = first.row_strips()
    columns = jnp.concatenate([upper, columns[owned], lower], axis=0)
    window = [[None, None], [None, None]]
    for m in range(4):
        centre = jnp.concatenate([up_rows[m], planes[0, m, owned, :], down_rows[m]], axis=0)
        cells = jnp.where(owned_lane, centre, roll(columns, -16 - 32 * m))
        window[m // 2][m % 2] = jnp.where(inside, cells, 0.0)
    def send_second(ends):
        ends = restored(ends, factor)
        second.pack_columns(lambda m: ends[m // 2][m % 2] * weight_ends)
        second.begin(2, 3)

    unit = normalised(window, scalars)
    result = restored(blur(unit, spectrum_ref[...], forward_ref, backward_ref, True, send_second), factor)
    result = [result[m // 2][m % 2] * weight for m in range(4)]
    second.pack_rows(result)
    second.begin(4, 5, 6, 7, 0, 1)
    for m in range(4):
        planes[1, m] = result[m]
    pairs = ((0, 0), (0, 1), (1, 1))
    scalars, next_factor = scalars_of(grams((result[:2], result[2:]), (result[:2], result[2:]), pairs))

    second.wait_recv()
    columns, upper, lower = second.sides()
    up_rows, down_rows = second.row_strips()
    upper, lower = jnp.where(has_up, upper, 0.0), jnp.where(has_down, lower, 0.0)
    columns = jnp.concatenate([columns[:16] + upper, columns[16:112], columns[112:] + lower], axis=0)
    edge_lane = ((lane < 16) & has_left) | ((lane >= 112) & has_right)
    window = [[None, None], [None, None]]
    keep = jnp.where(inside, weight, 0.0)
    for m in range(4):
        cells = planes[1, m]
        above, below = jnp.where(has_up, up_rows[m], 0.0), jnp.where(has_down, down_rows[m], 0.0)
        cells = jnp.concatenate([cells[:16] + above, cells[16:112], cells[112:] + below], axis=0)
        cells = cells + jnp.where(edge_lane, roll(columns, -16 - 32 * m), 0.0)
        planes[1, m] = cells
        window[m // 2][m % 2] = cells * keep
    def send_third(ends):
        ends = restored(ends, next_factor)
        third.pack_columns(lambda m: ends[m // 2][m % 2])
        third.begin(2, 3)

    unit = normalised(window, scalars)
    result = restored(blur(unit, spectrum_ref[...], forward_ref, backward_ref, False, send_third), next_factor)
    result = [result[m // 2][m % 2] for m in range(4)]
    third.pack_rows(result)
    third.begin(4, 5, 6, 7, 0, 1)
    for m in range(4):
        planes[2, m] = result[m]
    own_v = [[jnp.where(owned_core, planes[1, 2 * k + z, owned, :], 0.0) for z in range(PLANES)] for k in range(2)]
    sums += grams(own_v, own_v, pairs)

    def to_flat(source, target):
        for m in range(4):
            for j in range(7):
                head = roll(source(m, pl.ds(HALF + j, 14, stride=8)), -16 * j - HALF)
                tail = roll(source(m, pl.ds(HALF + j + 1, 14, stride=8)), 104 - 16 * j)
                target[pl.ds(98 * m + j, 14, stride=7), :] = jnp.where(lane14 < 112 - 16 * j, head, tail)

    to_flat(lambda m, rows: planes[1, m, rows, :], object_flat)

    third.wait_recv()
    columns, upper, lower = third.sides()
    upper, lower = jnp.where(has_up, upper, 0.0), jnp.where(has_down, lower, 0.0)
    columns = jnp.concatenate([columns[:8], columns[8:16] + upper, columns[16:112], columns[112:120] + lower, columns[120:]], axis=0)
    up_rows, down_rows = third.row_strips()
    edge_lane = ((lane >= 8) & (lane < 16) & has_left) | ((lane >= 112) & (lane < 120) & has_right)
    own_f = [[None, None], [None, None]]
    for m in range(4):
        cells = planes[2, m]
        above, below = jnp.where(has_up, up_rows[m], 0.0), jnp.where(has_down, down_rows[m], 0.0)
        cells = jnp.concatenate([cells[8:16] + above, cells[16:112], cells[112:120] + below], axis=0)
        cells = cells + jnp.where(edge_lane[owned], roll(columns[owned], -16 - 32 * m), 0.0)
        cells = jnp.where(owned_core, cells, 0.0)
        planes[2, m, owned, :] = cells
        own_f[m // 2][m % 2] = cells
    sums += grams(own_f, own_f, ((0, 0), (0, 1), (1, 1)))
    sums += grams(own_f, own_m, ((0, 0), (0, 1), (1, 0), (1, 1)))

    line16 = lax.broadcasted_iota(jnp.int32, (16, 128), 0)
    lane16 = lax.broadcasted_iota(jnp.int32, (16, 128), 1)
    stacked = jnp.zeros((16, 128), F32)
    for q, values in enumerate(sums):
        stacked = jnp.where(line16 == q, jnp.sum(values, axis=0, keepdims=True), stacked)
    stacked = jnp.sum(stacked, axis=1, keepdims=True)
    mine = jnp.sum(jnp.where(line16 == lane16, stacked, 0.0), axis=0, keepdims=True)

    def all_sum(mine, out_ref, in_ref, place, partner, stage):
        out_ref[...] = mine
        in_ref[place] = mine
        copies = [
            pltpu.make_async_remote_copy(
                src_ref=out_ref,
                dst_ref=in_ref.at[place],
                send_sem=sum_send.at[stage, step],
                recv_sem=sum_recv.at[stage, step],
                device_id=partner(step),
                device_id_type=pl.DeviceIdType.MESH,
            )
            for step in range(1, 16)
        ]
        for copy in copies:
            copy.start()
        return copies

    copies = all_sum(mine, one_out, one_in, place_one, partner_one, 0)
    to_flat(lambda m, rows: planes[2, m, rows, :], forward_flat)
    for copy in copies:
        copy.wait_recv()
    mine = jnp.sum(one_in[...], axis=0)
    sent = copies
    copies = all_sum(mine, two_out, two_in, place_two, partner_two, 1)
    for phase in (first, second, third):
        phase.wait_send()
    for copy in sent:
        copy.wait_send()
    for copy in copies:
        copy.wait()
    cells_total = PLANES * CORE * CORE * ny * nx
    gathered = jnp.sum(two_in[...], axis=0) * F32(1.0 / cells_total)
    lane1 = lax.broadcasted_iota(jnp.int32, (1, 128), 1)
    m00, m01, m11, v00, v01, v11, f00, f01, f11, p00, p01, p10, p11 = [
        jnp.sum(jnp.where(lane1 == q, gathered, 0.0), axis=1, keepdims=True) for q in range(13)
    ]
    (a, b, c), (u00, u11) = factor_of(m00, m01, m11)
    u01 = -b * u00 * u11
    w00 = u00 * u00 * v00
    w01 = u00 * (u01 * v00 + u11 * v01)
    w11 = u01 * u01 * v00 + 2.0 * u01 * u11 * v01 + u11 * u11 * v11
    (alpha, beta, gamma), (per_alpha, per_gamma) = factor_of(w00, w01, w11)
    t00 = u00 * per_alpha
    t11 = u11 * per_gamma
    t01 = (u01 - beta * t00) * per_gamma
    x0, x1 = alpha * u00 + beta * u01, beta * u11
    y0, y1 = gamma * u01, gamma * u11

    def form(l, r):
        return (
            l[0] * (r[0] * f00 + r[1] * f01 - r[2] * p00 - r[3] * p01)
            + l[1] * (r[0] * f01 + r[1] * f11 - r[2] * p10 - r[3] * p11)
            - l[2] * (r[0] * p00 + r[1] * p10 - r[2] * m00 - r[3] * m01)
            - l[3] * (r[0] * p01 + r[1] * p11 - r[2] * m01 - r[3] * m11)
        )

    zero = jnp.zeros_like(a)
    z_first, z_second = (t00, zero, x0, x1), (t01, t11, y0, y1)
    (rho, sigma, tau), (per_rho, per_tau) = factor_of(
        form(z_first, z_first), form(z_first, z_second), form(z_second, z_second)
    )
    i0 = [value * per_rho for value in z_first]
    i1 = [(value - sigma * lead) * per_tau for value, lead in zip(z_second, i0)]

    half = FLAT // 2
    one, two = slice(0, half), slice(half, FLAT)
    v_one, v_two = object_flat[one, :], object_flat[two, :]
    f_one, f_two = forward_flat[one, :], forward_flat[two, :]
    m_one, m_two = measured[one, :], measured[two, :]
    object_ref[one, :] = t00 * v_one
    object_ref[two, :] = t01 * v_one + t11 * v_two
    image_ref[one, :] = i0[0] * f_one - i0[2] * m_one - i0[3] * m_two
    image_ref[two, :] = i1[0] * f_one + i1[1] * f_two - i1[2] * m_one - i1[3] * m_two
    down = lax.broadcasted_iota(jnp.int32, (2, 2, 3), 0)
    across = lax.broadcasted_iota(jnp.int32, (2, 2, 3), 1)
    which = lax.broadcasted_iota(jnp.int32, (2, 2, 3), 2)
    factors = jnp.zeros((2, 2, 3), F32)
    for i, triple in enumerate(((a, b, c), (alpha, beta, gamma), (rho, sigma, tau))):
        for (r, k), value in zip(((0, 0), (0, 1), (1, 1)), triple):
            here = (which == i) & (down == r) & (across == k)
            factors = jnp.where(here, value.reshape(1, 1, 1), factors)
    factors_ref[...] = factors


def store(object_vmem, image_vmem, factors_vmem, object_hbm, image_hbm, factors_hbm, sem):
    copies = [
        pltpu.make_async_copy(source, target, sem.at[i])
        for i, (source, target) in enumerate(
            ((object_vmem, object_hbm), (image_vmem, image_hbm), (factors_vmem, factors_hbm))
        )
    ]
    for copy in copies:
        copy.start()
    for copy in copies:
        copy.wait()


def body(measured, psf_taps, offsets, window_mask):
    ny, nx = lax.axis_size("py"), lax.axis_size("px")
    hbm = pl.BlockSpec(memory_space=pltpu.HBM)
    vmem = pl.BlockSpec(memory_space=pltpu.VMEM)
    operands = [measured.reshape(FLAT, 128), psf_taps, offsets, window_mask, *tables()]
    operands = [pltpu.with_memory_space_constraint(operand, pltpu.HBM) for operand in operands]
    results = pl.pallas_call(
        functools.partial(kernel, ny, nx),
        out_shape=(pltpu.VMEM((FLAT, 128), F32), pltpu.VMEM((FLAT, 128), F32), pltpu.VMEM((2, 2, 3), F32)),
        in_specs=[hbm] * 8,
        out_specs=(vmem, vmem, vmem),
        scratch_shapes=[
            pltpu.VMEM((FLAT, 128), F32),
            pltpu.SMEM((1, 1, 2), jnp.int32),
            pltpu.VMEM((3, KERNEL, KERNEL), BF16),
            pltpu.VMEM((PATCH, PATCH), jnp.int32),
            pltpu.VMEM((256, 256), BF16),
            pltpu.VMEM((256, 256), BF16),
            pltpu.VMEM((64, 256), BF16),
            pltpu.VMEM((256, 128), BF16),
            pltpu.VMEM((256, 384), F32),
            pltpu.VMEM((3, 4, PATCH, 128), F32),
            pltpu.VMEM((3, 2, 64, 128), BF16),
            pltpu.VMEM((3, 2, 64, 128), BF16),
            pltpu.VMEM((3, 32, 128), BF16),
            pltpu.VMEM((3, 2, 64, 128), BF16),
            pltpu.VMEM((3, 2, 64, 128), BF16),
            pltpu.VMEM((3, 4, 16, 128), BF16),
            pltpu.VMEM((FLAT, 128), F32),
            pltpu.VMEM((FLAT, 128), F32),
            pltpu.VMEM((1, 128), F32),
            pltpu.VMEM((16, 1, 128), F32),
            pltpu.VMEM((1, 128), F32),
            pltpu.VMEM((16, 1, 128), F32),
            pltpu.SemaphoreType.DMA((8,)),
            pltpu.SemaphoreType.DMA((3, 8)),
            pltpu.SemaphoreType.DMA((3, 8)),
            pltpu.SemaphoreType.DMA((2, 16)),
            pltpu.SemaphoreType.DMA((2, 16)),
        ],
        compiler_params=pltpu.CompilerParams(
            collective_id=0, has_side_effects=True, vmem_limit_bytes=48 * 1024 * 1024
        ),
        name="step",
    )(*operands)
    results = [pltpu.with_memory_space_constraint(result, pltpu.VMEM) for result in results]
    objects, images, factors = pl.pallas_call(
        store,
        out_shape=(pltpu.HBM((FLAT, 128), F32), pltpu.HBM((FLAT, 128), F32), pltpu.HBM((2, 2, 3), F32)),
        in_specs=[vmem] * 3,
        out_specs=(hbm, hbm, hbm),
        scratch_shapes=[pltpu.SemaphoreType.DMA((3,))],
        name="store",
    )(*results)
    shape = (2, PLANES, 1, 1, CORE * CORE)
    return objects.reshape(shape), images.reshape(shape), factors.transpose(2, 0, 1)


def solution(mesh):
    placed = (
        P(None, None, "py", "px", None),
        P("py", "px", None, None, None),
        P("py", "px", None),
        P("py", "px"),
    )
    return jax.shard_map(
        body,
        mesh=mesh,
        in_specs=placed,
        out_specs=(P(None, None, "py", "px", None), P(None, None, "py", "px", None), P()),
        check_vma=False,
    )
```

```python
import functools
import math

import jax
import jax.numpy as jnp
import numpy as np
from jax import lax
from jax.experimental import pallas as pl
from jax.experimental.pallas import tpu as pltpu
from jax.sharding import PartitionSpec as P

PLANES = 2
PATCH = 128
KERNEL = 32
HALF = 8
CORE = 112
FLAT = 2 * PLANES * CORE * CORE // 128
TAP = KERNEL // 2 - 1
EPSILON = 1e-06
F32 = jnp.float32
BF16 = jnp.bfloat16


def tables():
    ids = np.arange(PATCH)
    angle = 2 * np.pi * (np.outer(ids, ids) % PATCH) / PATCH
    cos, sin = np.cos(angle), -np.sin(angle)
    forward = np.block([[cos, sin], [-sin, cos]])
    places = np.arange(64) - KERNEL // 2
    angle = 2 * np.pi * (np.outer(places, ids) % PATCH) / PATCH
    cos, sin = np.cos(angle), -np.sin(angle)
    taps_x = np.concatenate([cos, sin], axis=1)
    taps_y = np.block([[cos.T, -sin.T], [sin.T, cos.T]])
    return [jnp.asarray(t, BF16) for t in (forward, forward.T, taps_x, taps_y)]


def mm(left, right):
    return jnp.dot(left, right, preferred_element_type=F32)


def roll(values, shift):
    shift = shift % 128
    return values if shift == 0 else pltpu.roll(values, shift, 1)


def total(values):
    return jnp.sum(jnp.sum(values, axis=0, keepdims=True), axis=1, keepdims=True)


class Exchange:
    def __init__(self, index, ny, nx, height, rows, cols_out, cols_in, outs, ins, send, recv):
        self.height, self.rows, self.cols_out, self.cols_in = height, rows, cols_out, cols_in
        self.row_out, self.col_out, self.corner_out = (ref.at[index] for ref in outs)
        self.row_in, self.col_in, self.corner_in = (ref.at[index] for ref in ins)
        py, px = lax.axis_index("py"), lax.axis_index("px")
        up, down = lax.rem(py + ny - 1, ny), lax.rem(py + 1, ny)
        left, right = lax.rem(px + nx - 1, nx), lax.rem(px + 1, nx)
        has_up, has_down, has_left, has_right = py > 0, py < ny - 1, px > 0, px < nx - 1
        strip = pl.ds(0, 4 * height)
        top, bottom = (pl.ds(0, 16), pl.ds(16, 16)) if height == 16 else (pl.ds(0, 16), pl.ds(0, 16))
        plan = [
            (self.row_out.at[0, strip], self.row_in.at[1, strip], up, px, has_up),
            (self.row_out.at[1, strip], self.row_in.at[0, strip], down, px, has_down),
            (self.col_out.at[0, strip], self.col_in.at[1, strip], py, left, has_left),
            (self.col_out.at[1, strip], self.col_in.at[0, strip], py, right, has_right),
            (self.corner_out.at[top], self.corner_in.at[3], up, left, has_up & has_left),
            (self.corner_out.at[top], self.corner_in.at[2], up, right, has_up & has_right),
            (self.corner_out.at[bottom], self.corner_in.at[1], down, left, has_down & has_left),
            (self.corner_out.at[bottom], self.corner_in.at[0], down, right, has_down & has_right),
        ]
        self.copies = [
            pltpu.make_async_remote_copy(
                src_ref=source,
                dst_ref=target,
                send_sem=send.at[index, i],
                recv_sem=recv.at[index, i],
                device_id={"py": to_y, "px": to_x},
                device_id_type=pl.DeviceIdType.MESH,
            )
            for i, (source, target, to_y, to_x, _) in enumerate(plan)
        ]
        self.there = [there for *_, there in plan]
        self.back = [self.there[i] for i in (1, 0, 3, 2, 7, 6, 5, 4)]

    def begin(self, *which):
        for i in which:
            pl.when(self.there[i])(self.copies[i].start)

    def pack_columns(self, strip_of):
        for side, first in enumerate(self.cols_out):
            strips = [strip_of(m)[first : first + self.height] for m in range(2 * PLANES)]
            self.col_out[side, 0 : 4 * self.height, :] = jnp.concatenate(strips, axis=0).astype(BF16)

    def pack_rows(self, planes):
        height = self.height
        lane = lax.broadcasted_iota(jnp.int32, (height, 128), 1)
        ends = []
        for side, first in enumerate(self.rows):
            strips = [planes[m][first : first + height] for m in range(2 * PLANES)]
            self.row_out[side, 0 : 4 * height, :] = jnp.concatenate(strips, axis=0).astype(BF16)
            packed = roll(strips[0], 16)
            for m in range(1, 2 * PLANES):
                packed = jnp.where(lane >= 32 * m, roll(strips[m], 16 + 32 * m), packed)
            ends.append(packed)
        self.corner_out[0 : 2 * height, :] = jnp.concatenate(ends, axis=0).astype(BF16)

    def wait_recv(self):
        for copy, there in zip(self.copies, self.back):
            pl.when(there)(copy.wait_recv)

    def wait_send(self):
        for copy, there in zip(self.copies, self.there):
            pl.when(there)(copy.wait_send)

    def row_strips(self):
        height = self.height
        both = [self.row_in[side, 0 : 4 * height, :].astype(F32) for side in range(2)]
        return [[strips[m * height : (m + 1) * height] for m in range(2 * PLANES)] for strips in both]

    def sides(self):
        height = self.height
        both = [self.col_in[side, 0 : 4 * height, :].astype(F32) for side in range(2)]
        pieces = []
        for m in range(2 * PLANES):
            slots = [both[1][m * height : (m + 1) * height] for _ in range(32 // height)]
            slots[self.cols_in // height] = both[0][m * height : (m + 1) * height]
            pieces += slots
        columns = jnp.concatenate(pieces, axis=0).T
        lane = lax.broadcasted_iota(jnp.int32, (height, 128), 1)
        is_left = lax.rem(lane, 32) >= 16
        corner = [self.corner_in[i].astype(F32) for i in range(4)]
        if height == 8:
            corner = [corner[0][8:], corner[1][8:], corner[2][:8], corner[3][:8]]
        upper = jnp.where(is_left, roll(corner[0], 16), roll(corner[1], -16))
        lower = jnp.where(is_left, roll(corner[2], 16), roll(corner[3], -16))
        return columns, upper, lower


def normaliser(s00, s01, s11):
    tiny = F32(1e-30)
    q0 = lax.rsqrt(jnp.maximum(s00, tiny))
    cross = s01 * q0
    q1 = lax.rsqrt(jnp.maximum(s11 - cross * cross, s11 * F32(1e-6) + tiny))
    return (q0, cross, q1), (1.0 / q0, cross, 1.0 / q1)


def normalised(cells, scalars):
    q0, cross, q1 = scalars
    first = [cells[0][z] * q0 for z in range(PLANES)]
    second = [(cells[1][z] - cross * first[z]) * q1 for z in range(PLANES)]
    return first, second


def blur(cells, spectrum, forward_ref, backward_ref, adjoint, send_ends):
    half = PATCH
    table, turned = forward_ref[...], backward_ref[...]
    values = jnp.concatenate(
        [jnp.concatenate([cells[k][z].astype(BF16) for k in range(2)], axis=1) for z in range(PLANES)], axis=0
    )
    along_x = mm(values, table).astype(BF16)
    swapped = jnp.concatenate(
        [
            jnp.concatenate([along_x[z * half : (z + 1) * half, c * half : (c + 1) * half] for z in range(PLANES)], axis=1)
            for c in range(2)
        ],
        axis=0,
    )
    along_y = mm(turned, swapped)
    re = [along_y[:half, z * half : (z + 1) * half] for z in range(PLANES)]
    im = [along_y[half:, z * half : (z + 1) * half] for z in range(PLANES)]
    tap_re = [spectrum[:half, t * half : (t + 1) * half] for t in range(3)]
    tap_im = [spectrum[half:, t * half : (t + 1) * half] for t in range(3)]
    sign = -1.0 if adjoint else 1.0
    out_re, out_im = [], []
    for z_out in range(PLANES):
        sum_re = sum_im = None
        for z_in in range(PLANES):
            depth = 1 + (z_in - z_out) if adjoint else 1 - (z_in - z_out)
            a, b = tap_re[depth], sign * tap_im[depth]
            part_re = re[z_in] * a - im[z_in] * b
            part_im = re[z_in] * b + im[z_in] * a
            sum_re = part_re if sum_re is None else sum_re + part_re
            sum_im = part_im if sum_im is None else sum_im + part_im
        out_re.append(sum_re.astype(BF16))
        out_im.append(sum_im.astype(BF16))
    product = jnp.concatenate([jnp.concatenate(out_re, axis=1), jnp.concatenate(out_im, axis=1)], axis=0)
    back_y = mm(table, product).astype(BF16)
    swapped = jnp.concatenate(
        [
            jnp.concatenate([back_y[c * half : (c + 1) * half, z * half : (z + 1) * half] for c in range(2)], axis=1)
            for z in range(PLANES)
        ],
        axis=0,
    )
    ends = [table[at : at + 16] for k in range(2) for at in (k * half + half - 16, k * half)]
    ends = lax.dot_general(
        jnp.concatenate(ends, axis=0), swapped, (((1,), (1,)), ((), ())), preferred_element_type=F32
    )
    ends = [[ends[32 * k : 32 * (k + 1), z * half : (z + 1) * half] for z in range(PLANES)] for k in range(2)]
    send_ends(ends)
    back_x = mm(swapped, turned)
    return [[back_x[z * half : (z + 1) * half, k * half : (k + 1) * half] for z in range(PLANES)] for k in range(2)]


def restored(cells, factor):
    first = [factor[0] * cells[0][z] for z in range(PLANES)]
    second = [factor[2] * cells[1][z] + factor[1] * cells[0][z] for z in range(PLANES)]
    return first, second


def factor_of(g00, g01, g11):
    s00 = jnp.maximum(g00, 0.0) + EPSILON
    i00 = lax.rsqrt(s00)
    r01 = g01 * i00
    s11 = jnp.maximum(g11 - r01 * r01, 0.0) + EPSILON
    i11 = lax.rsqrt(s11)
    return (s00 * i00, r01, s11 * i11), (i00, i11)


def kernel(
    ny, nx,
    measured_hbm, taps_hbm, offsets_hbm, mask_hbm, forward_hbm, backward_hbm, taps_x_hbm, taps_y_hbm,
    object_ref, image_ref, factors_ref,
    measured, offsets, taps, mask, forward_ref, backward_ref, taps_x, taps_y,
    spectrum_ref, planes, row_out, col_out, corner_out, row_in, col_in, corner_in,
    object_flat, forward_flat,
    one_out, one_in, two_out, two_in,
    load_sem, send_sem, recv_sem, sum_send, sum_recv,
):
    py, px = lax.axis_index("py"), lax.axis_index("px")
    row, high, column = px // 8, lax.rem(px // 4, 2), lax.rem(px, 4)
    place_one, place_two = high * ny + py, row * 4 + column

    def partner_one(step):
        at = lax.rem(place_one + step, 16)
        return {"py": lax.rem(at, ny), "px": row * 8 + (at // ny) * 4 + column}

    def partner_two(step):
        at = lax.rem(place_two + step, 16)
        return {"py": py, "px": (at // 4) * 8 + high * 4 + lax.rem(at, 4)}

    exchange = functools.partial(
        Exchange, ny=ny, nx=nx, outs=(row_out, col_out, corner_out), ins=(row_in, col_in, corner_in),
        send=send_sem, recv=recv_sem,
    )
    first = exchange(index=0, height=8, rows=(8, 112), cols_out=(24, 0), cols_in=16)
    second = exchange(index=1, height=16, rows=(0, 112), cols_out=(16, 0), cols_in=16)
    third = exchange(index=2, height=8, rows=(0, 120), cols_out=(16, 8), cols_in=24)
    barrier = pltpu.get_barrier_semaphore()
    has_up, has_down, has_left, has_right = py > 0, py < ny - 1, px > 0, px < nx - 1
    greeted = jnp.int32(30)
    for dx, has_x in ((nx - 1, has_left), (1, has_right), (0, None)):
        for dy, has_y in ((ny - 1, has_up), (1, has_down), (0, None)):
            if dx or dy:
                there = has_x if has_y is None else has_y if has_x is None else has_x & has_y
                to = {"py": lax.rem(py + dy, ny), "px": lax.rem(px + dx, nx)}
                greeted += there.astype(jnp.int32)

                @pl.when(there)
                def _(to=to):
                    pl.semaphore_signal(barrier, inc=1, device_id=to, device_id_type=pl.DeviceIdType.MESH)

    loads = [
        pltpu.make_async_copy(source, target, load_sem.at[i])
        for i, (source, target) in enumerate(
            [
                (measured_hbm, measured),
                (taps_hbm.at[0, 0, pl.ds(TAP, 3)], taps),
                (taps_x_hbm, taps_x),
                (taps_y_hbm, taps_y),
                (offsets_hbm, offsets),
                (mask_hbm, mask),
                (forward_hbm, forward_ref),
                (backward_hbm, backward_ref),
            ]
        )
    ]
    for load in loads:
        load.start()

    for step in range(1, 16):
        for to in (partner_one(step), partner_two(step)):
            pl.semaphore_signal(barrier, inc=1, device_id=to, device_id_type=pl.DeviceIdType.MESH)

    lane = lax.broadcasted_iota(jnp.int32, (PATCH, 128), 1)
    line = lax.broadcasted_iota(jnp.int32, (PATCH, 128), 0)
    owned_lane = (lane >= HALF) & (lane < PATCH - HALF)
    low_y, high_y = jnp.where(has_up, 0, HALF), jnp.where(has_down, PATCH, PATCH - HALF)
    low_x, high_x = jnp.where(has_left, 0, HALF), jnp.where(has_right, PATCH, PATCH - HALF)
    inside = (line >= low_y) & (line < high_y) & (lane >= low_x) & (lane < high_x)

    loads[0].wait()
    lane14 = lax.broadcasted_iota(jnp.int32, (14, 128), 1)
    for m in range(4):
        planes[0, m, 0:HALF, :] = jnp.zeros((HALF, 128), F32)
        planes[0, m, PATCH - HALF : PATCH, :] = jnp.zeros((HALF, 128), F32)
        for k in range(8):
            if k < 7:
                high_part = measured[pl.ds(98 * m + k, 14, stride=7), :]
            if k == 0:
                both = high_part
            elif k == 7:
                both = measured[pl.ds(98 * m + 6, 14, stride=7), :]
            else:
                low_part = measured[pl.ds(98 * m + k - 1, 14, stride=7), :]
                both = jnp.where(lane14 >= 128 - 16 * k, low_part, high_part)
            planes[0, m, pl.ds(HALF + k, 14, stride=8), :] = roll(both, 16 * k + HALF)

    measured_planes = [planes[0, m] for m in range(4)]
    packed = roll(measured_planes[0], 16)
    for m in range(1, 4):
        packed = jnp.where(lane >= 32 * m, roll(measured_planes[m], 16 + 32 * m), packed)
    packed = packed.T
    first.pack_columns(lambda m: packed[32 * m : 32 * (m + 1)])
    first.pack_rows(measured_planes)
    pl.semaphore_wait(barrier, greeted)
    first.begin(2, 3, 4, 5, 6, 7, 0, 1)

    for load in loads[1:5]:
        load.wait()
    shift_y, shift_x = offsets[0, 0, 0], offsets[0, 0, 1]
    pick_x = (
        lax.broadcasted_iota(jnp.int32, (KERNEL, 64), 1) == lax.broadcasted_iota(jnp.int32, (KERNEL, 64), 0) + shift_x
    )
    pick_y = (
        lax.broadcasted_iota(jnp.int32, (64, KERNEL), 0) == lax.broadcasted_iota(jnp.int32, (64, KERNEL), 1) + shift_y
    )
    pick_x = jnp.where(pick_x, 1.0, 0.0).astype(BF16)
    pick_y = jnp.where(pick_y, 1.0, 0.0).astype(BF16)
    placed = mm(taps[...].reshape(3 * KERNEL, KERNEL), pick_x).astype(BF16)
    kx = mm(placed, taps_x[...]).astype(BF16)
    side_by_side = jnp.concatenate([kx[t * KERNEL : (t + 1) * KERNEL] for t in range(3)], axis=1)
    kx = mm(pick_y, side_by_side).astype(BF16)
    kx = jnp.concatenate(
        [
            jnp.concatenate([kx[:, t * 256 + c * 128 : t * 256 + (c + 1) * 128] for t in range(3)], axis=1)
            for c in range(2)
        ],
        axis=0,
    )
    spectrum_ref[...] = mm(taps_y[...], kx) * F32(1.0 / (PATCH * PATCH))

    for load in loads[5:]:
        load.wait()
    weight = mask[...].astype(F32)
    weight_ends = weight.T
    weight_ends = jnp.concatenate([weight_ends[PATCH - 16 :], weight_ends[:16]], axis=0)

    def tile(left, right):
        return jnp.sum((left * right).reshape(-1, 8, 128), axis=0)

    owned = slice(HALF, PATCH - HALF)
    owned_core = owned_lane[owned]
    own_m = [[jnp.where(owned_core, planes[0, 2 * k + z, owned, :], 0.0) for z in range(PLANES)] for k in range(2)]

    def grams(left, right, pairs):
        return [sum(tile(left[i][z], right[j][z]) for z in range(PLANES)) for i, j in pairs]

    sums = grams(own_m, own_m, ((0, 0), (0, 1), (1, 1)))

    def scalars_of(tiles):
        return normaliser(*(total(values) for values in tiles))

    scalars, factor = scalars_of(sums)
    first.wait_recv()
    columns, upper, lower = first.sides()
    up_rows, down_rows = first.row_strips()
    columns = jnp.concatenate([upper, columns[owned], lower], axis=0)
    window = [[None, None], [None, None]]
    for m in range(4):
        centre = jnp.concatenate([up_rows[m], planes[0, m, owned, :], down_rows[m]], axis=0)
        cells = jnp.where(owned_lane, centre, roll(columns, -16 - 32 * m))
        window[m // 2][m % 2] = jnp.where(inside, cells, 0.0)
    def send_second(ends):
        ends = restored(ends, factor)
        second.pack_columns(lambda m: ends[m // 2][m % 2] * weight_ends)
        second.begin(2, 3)

    unit = normalised(window, scalars)
    result = restored(blur(unit, spectrum_ref[...], forward_ref, backward_ref, True, send_second), factor)
    result = [result[m // 2][m % 2] * weight for m in range(4)]
    second.pack_rows(result)
    second.begin(4, 5, 6, 7, 0, 1)
    for m in range(4):
        planes[1, m] = result[m]
    pairs = ((0, 0), (0, 1), (1, 1))
    scalars, next_factor = scalars_of(grams((result[:2], result[2:]), (result[:2], result[2:]), pairs))

    second.wait_recv()
    columns, upper, lower = second.sides()
    up_rows, down_rows = second.row_strips()
    upper, lower = jnp.where(has_up, upper, 0.0), jnp.where(has_down, lower, 0.0)
    columns = jnp.concatenate([columns[:16] + upper, columns[16:112], columns[112:] + lower], axis=0)
    edge_lane = ((lane < 16) & has_left) | ((lane >= 112) & has_right)
    window = [[None, None], [None, None]]
    keep = jnp.where(inside, weight, 0.0)
    for m in range(4):
        cells = planes[1, m]
        above, below = jnp.where(has_up, up_rows[m], 0.0), jnp.where(has_down, down_rows[m], 0.0)
        cells = jnp.concatenate([cells[:16] + above, cells[16:112], cells[112:] + below], axis=0)
        cells = cells + jnp.where(edge_lane, roll(columns, -16 - 32 * m), 0.0)
        planes[1, m] = cells
        window[m // 2][m % 2] = cells * keep
    def send_third(ends):
        ends = restored(ends, next_factor)
        third.pack_columns(lambda m: ends[m // 2][m % 2])
        third.begin(2, 3)

    unit = normalised(window, scalars)
    result = restored(blur(unit, spectrum_ref[...], forward_ref, backward_ref, False, send_third), next_factor)
    result = [result[m // 2][m % 2] for m in range(4)]
    third.pack_rows(result)
    third.begin(4, 5, 6, 7, 0, 1)
    for m in range(4):
        planes[2, m] = result[m]
    own_v = [[jnp.where(owned_core, planes[1, 2 * k + z, owned, :], 0.0) for z in range(PLANES)] for k in range(2)]
    sums += grams(own_v, own_v, pairs)

    def to_flat(source, target):
        for m in range(4):
            for j in range(7):
                head = roll(source(m, pl.ds(HALF + j, 14, stride=8)), -16 * j - HALF)
                tail = roll(source(m, pl.ds(HALF + j + 1, 14, stride=8)), 104 - 16 * j)
                target[pl.ds(98 * m + j, 14, stride=7), :] = jnp.where(lane14 < 112 - 16 * j, head, tail)

    to_flat(lambda m, rows: planes[1, m, rows, :], object_flat)

    third.wait_recv()
    columns, upper, lower = third.sides()
    upper, lower = jnp.where(has_up, upper, 0.0), jnp.where(has_down, lower, 0.0)
    columns = jnp.concatenate([columns[:8], columns[8:16] + upper, columns[16:112], columns[112:120] + lower, columns[120:]], axis=0)
    up_rows, down_rows = third.row_strips()
    edge_lane = ((lane >= 8) & (lane < 16) & has_left) | ((lane >= 112) & (lane < 120) & has_right)
    own_f = [[None, None], [None, None]]
    for m in range(4):
        cells = planes[2, m]
        above, below = jnp.where(has_up, up_rows[m], 0.0), jnp.where(has_down, down_rows[m], 0.0)
        cells = jnp.concatenate([cells[8:16] + above, cells[16:112], cells[112:120] + below], axis=0)
        cells = cells + jnp.where(edge_lane[owned], roll(columns[owned], -16 - 32 * m), 0.0)
        cells = jnp.where(owned_core, cells, 0.0)
        planes[2, m, owned, :] = cells
        own_f[m // 2][m % 2] = cells
    sums += grams(own_f, own_f, ((0, 0), (0, 1), (1, 1)))
    sums += grams(own_f, own_m, ((0, 0), (0, 1), (1, 0), (1, 1)))

    line16 = lax.broadcasted_iota(jnp.int32, (16, 128), 0)
    lane16 = lax.broadcasted_iota(jnp.int32, (16, 128), 1)
    stacked = jnp.zeros((16, 128), F32)
    for q, values in enumerate(sums):
        stacked = jnp.where(line16 == q, jnp.sum(values, axis=0, keepdims=True), stacked)
    stacked = jnp.sum(stacked, axis=1, keepdims=True)
    mine = jnp.sum(jnp.where(line16 == lane16, stacked, 0.0), axis=0, keepdims=True)

    def all_sum(mine, out_ref, in_ref, place, partner, stage):
        out_ref[...] = mine
        in_ref[place] = mine
        copies = [
            pltpu.make_async_remote_copy(
                src_ref=out_ref,
                dst_ref=in_ref.at[place],
                send_sem=sum_send.at[stage, step],
                recv_sem=sum_recv.at[stage, step],
                device_id=partner(step),
                device_id_type=pl.DeviceIdType.MESH,
            )
            for step in range(1, 16)
        ]
        for copy in copies:
            copy.start()
        return copies

    copies = all_sum(mine, one_out, one_in, place_one, partner_one, 0)
    to_flat(lambda m, rows: planes[2, m, rows, :], forward_flat)
    for copy in copies:
        copy.wait_recv()
    mine = jnp.sum(one_in[...], axis=0)
    sent = copies
    copies = all_sum(mine, two_out, two_in, place_two, partner_two, 1)
    for phase in (first, second, third):
        phase.wait_send()
    for copy in sent:
        copy.wait_send()
    for copy in copies:
        copy.wait()
    cells_total = PLANES * CORE * CORE * ny * nx
    gathered = jnp.sum(two_in[...], axis=0) * F32(1.0 / cells_total)
    lane1 = lax.broadcasted_iota(jnp.int32, (1, 128), 1)
    m00, m01, m11, v00, v01, v11, f00, f01, f11, p00, p01, p10, p11 = [
        jnp.sum(jnp.where(lane1 == q, gathered, 0.0), axis=1, keepdims=True) for q in range(13)
    ]
    (a, b, c), (u00, u11) = factor_of(m00, m01, m11)
    u01 = -b * u00 * u11
    w00 = u00 * u00 * v00
    w01 = u00 * (u01 * v00 + u11 * v01)
    w11 = u01 * u01 * v00 + 2.0 * u01 * u11 * v01 + u11 * u11 * v11
    (alpha, beta, gamma), (per_alpha, per_gamma) = factor_of(w00, w01, w11)
    t00 = u00 * per_alpha
    t11 = u11 * per_gamma
    t01 = (u01 - beta * t00) * per_gamma
    x0, x1 = alpha * u00 + beta * u01, beta * u11
    y0, y1 = gamma * u01, gamma * u11

    def form(l, r):
        return (
            l[0] * (r[0] * f00 + r[1] * f01 - r[2] * p00 - r[3] * p01)
            + l[1] * (r[0] * f01 + r[1] * f11 - r[2] * p10 - r[3] * p11)
            - l[2] * (r[0] * p00 + r[1] * p10 - r[2] * m00 - r[3] * m01)
            - l[3] * (r[0] * p01 + r[1] * p11 - r[2] * m01 - r[3] * m11)
        )

    zero = jnp.zeros_like(a)
    z_first, z_second = (t00, zero, x0, x1), (t01, t11, y0, y1)
    (rho, sigma, tau), (per_rho, per_tau) = factor_of(
        form(z_first, z_first), form(z_first, z_second), form(z_second, z_second)
    )
    i0 = [value * per_rho for value in z_first]
    i1 = [(value - sigma * lead) * per_tau for value, lead in zip(z_second, i0)]

    half = FLAT // 2
    one, two = slice(0, half), slice(half, FLAT)
    v_one, v_two = object_flat[one, :], object_flat[two, :]
    f_one, f_two = forward_flat[one, :], forward_flat[two, :]
    m_one, m_two = measured[one, :], measured[two, :]
    object_ref[one, :] = t00 * v_one
    object_ref[two, :] = t01 * v_one + t11 * v_two
    image_ref[one, :] = i0[0] * f_one - i0[2] * m_one - i0[3] * m_two
    image_ref[two, :] = i1[0] * f_one + i1[1] * f_two - i1[2] * m_one - i1[3] * m_two
    down = lax.broadcasted_iota(jnp.int32, (2, 2, 3), 0)
    across = lax.broadcasted_iota(jnp.int32, (2, 2, 3), 1)
    which = lax.broadcasted_iota(jnp.int32, (2, 2, 3), 2)
    factors = jnp.zeros((2, 2, 3), F32)
    for i, triple in enumerate(((a, b, c), (alpha, beta, gamma), (rho, sigma, tau))):
        for (r, k), value in zip(((0, 0), (0, 1), (1, 1)), triple):
            here = (which == i) & (down == r) & (across == k)
            factors = jnp.where(here, value.reshape(1, 1, 1), factors)
    factors_ref[...] = factors


def store(object_vmem, image_vmem, factors_vmem, object_hbm, image_hbm, factors_hbm, sem):
    pairs = [(factors_vmem, factors_hbm)]
    for first, last in ((0, 104), (104, 200), (200, 296), (296, FLAT)):
        rows = pl.ds(first, last - first)
        pairs += [(object_vmem.at[rows], object_hbm.at[rows]), (image_vmem.at[rows], image_hbm.at[rows])]
    copies = [pltpu.make_async_copy(source, target, sem.at[i]) for i, (source, target) in enumerate(pairs)]
    for copy in copies:
        copy.start()
    for copy in copies:
        copy.wait()


def body(measured, psf_taps, offsets, window_mask):
    ny, nx = lax.axis_size("py"), lax.axis_size("px")
    hbm = pl.BlockSpec(memory_space=pltpu.HBM)
    vmem = pl.BlockSpec(memory_space=pltpu.VMEM)
    operands = [measured.reshape(FLAT, 128), psf_taps, offsets, window_mask, *tables()]
    operands = [pltpu.with_memory_space_constraint(operand, pltpu.HBM) for operand in operands]
    results = pl.pallas_call(
        functools.partial(kernel, ny, nx),
        out_shape=(pltpu.VMEM((FLAT, 128), F32), pltpu.VMEM((FLAT, 128), F32), pltpu.VMEM((2, 2, 3), F32)),
        in_specs=[hbm] * 8,
        out_specs=(vmem, vmem, vmem),
        scratch_shapes=[
            pltpu.VMEM((FLAT, 128), F32),
            pltpu.SMEM((1, 1, 2), jnp.int32),
            pltpu.VMEM((3, KERNEL, KERNEL), BF16),
            pltpu.VMEM((PATCH, PATCH), jnp.int32),
            pltpu.VMEM((256, 256), BF16),
            pltpu.VMEM((256, 256), BF16),
            pltpu.VMEM((64, 256), BF16),
            pltpu.VMEM((256, 128), BF16),
            pltpu.VMEM((256, 384), F32),
            pltpu.VMEM((3, 4, PATCH, 128), F32),
            pltpu.VMEM((3, 2, 64, 128), BF16),
            pltpu.VMEM((3, 2, 64, 128), BF16),
            pltpu.VMEM((3, 32, 128), BF16),
            pltpu.VMEM((3, 2, 64, 128), BF16),
            pltpu.VMEM((3, 2, 64, 128), BF16),
            pltpu.VMEM((3, 4, 16, 128), BF16),
            pltpu.VMEM((FLAT, 128), F32),
            pltpu.VMEM((FLAT, 128), F32),
            pltpu.VMEM((1, 128), F32),
            pltpu.VMEM((16, 1, 128), F32),
            pltpu.VMEM((1, 128), F32),
            pltpu.VMEM((16, 1, 128), F32),
            pltpu.SemaphoreType.DMA((8,)),
            pltpu.SemaphoreType.DMA((3, 8)),
            pltpu.SemaphoreType.DMA((3, 8)),
            pltpu.SemaphoreType.DMA((2, 16)),
            pltpu.SemaphoreType.DMA((2, 16)),
        ],
        compiler_params=pltpu.CompilerParams(
            collective_id=0, has_side_effects=True, vmem_limit_bytes=48 * 1024 * 1024
        ),
        name="step",
    )(*operands)
    results = [pltpu.with_memory_space_constraint(result, pltpu.VMEM) for result in results]
    objects, images, factors = pl.pallas_call(
        store,
        out_shape=(pltpu.HBM((FLAT, 128), F32), pltpu.HBM((FLAT, 128), F32), pltpu.HBM((2, 2, 3), F32)),
        in_specs=[vmem] * 3,
        out_specs=(hbm, hbm, hbm),
        scratch_shapes=[pltpu.SemaphoreType.DMA((9,))],
        name="store",
    )(*results)
    shape = (2, PLANES, 1, 1, CORE * CORE)
    return objects.reshape(shape), images.reshape(shape), factors.transpose(2, 0, 1)


def solution(mesh):
    placed = (
        P(None, None, "py", "px", None),
        P("py", "px", None, None, None),
        P("py", "px", None),
        P("py", "px"),
    )
    return jax.shard_map(
        body,
        mesh=mesh,
        in_specs=placed,
        out_specs=(P(None, None, "py", "px", None), P(None, None, "py", "px", None), P()),
        check_vma=False,
    )
```
